32 devices in a mesh: dp: 8 (over z, core), tensor: 4 (over y, x).
Axes of the slice: x: 2, y: 2, z: 4, core: 2. Of those that a mesh axis runs over, the one named last changes fastest.
Arguments:
- layer_input: bfloat16 [16384, 1024], P(('dp', 'tensor')), may hold values from -6 to 6
- segment_ids: int32 [32, 512], P('dp'), may hold values from 0 to 15, never falling along the last dimension, each value on 1 to 256 neighbouring positions
- w_qkv: bfloat16 [3, 1024, 1024], P(None, None, 'tensor'), may hold values from -0.1875 to 0.1875
- b_qv: bfloat16 [2, 1024], P(None, 'tensor'), may hold values from -3 to 3
- w_out: bfloat16 [1024, 1024], P('tensor'), may hold values from -0.5 to 0.5
- b_out: bfloat16 [1024], replicated, may hold values from -3 to 3
- ln1_gain: float32 [1024], replicated, may hold values from 0.5 to 1.5
- ln1_bias: float32 [1024], replicated, may hold values from -2 to 2
- w_up: bfloat16 [1024, 4096], P(None, 'tensor'), may hold values from -0.1875 to 0.1875
- b_up: bfloat16 [4096], P('tensor'), may hold values from -3 to 3
- w_down: bfloat16 [4096, 1024], P('tensor'), may hold values from -0.09375 to 0.09375
- b_down: bfloat16 [1024], replicated, may hold values from -2 to 2
- ln2_gain: float32 [1024], replicated, may hold values from 0.5 to 1.5
- ln2_bias: float32 [1024], replicated, may hold values from -2 to 2
- cotangent: bfloat16 [16384, 1024], P(('dp', 'tensor')), may hold values from -6 to 6
Outputs:
- output: bfloat16 [16384, 1024], P(('dp', 'tensor'))
- grad_input: float32 [16384, 1024], P(('dp', 'tensor'))
- grad_w_qkv: float32 [3, 1024, 1024], P(None, None, 'tensor')
- grad_b_qv: float32 [2, 1024], P(None, 'tensor')
- grad_w_out: float32 [1024, 1024], P('tensor')
- grad_b_out: float32 [1024], replicated
- grad_ln1_gain: float32 [1024], replicated
- grad_ln1_bias: float32 [1024], replicated
- grad_w_up: float32 [1024, 4096], P(None, 'tensor')
- grad_b_up: float32 [4096], P('tensor')
- grad_w_down: float32 [4096, 1024], P('tensor')
- grad_b_down: float32 [1024], replicated
- grad_ln2_gain: float32 [1024], replicated
- grad_ln2_bias: float32 [1024], replicated
The draws below stay inside these ranges and needn't reach their ends.
Inputs may be any that keep to these rules, and one draw needn't show every extreme that they name: `segment_ids`: within a sequence the ids never fall; a document has at most 256 tokens.
All inputs are finite; a program needn't handle non-finite values.
Results may differ from the reference program's by a relative error of at most 0.018.
Values may be sent and summed in bfloat16 or wider, within the bound.
No kernel may reach another device: no remote copies, remote signals or barrier semaphores. Data moves between devices by JAX's collectives and lax.ppermute only.
A program may use at most 128 MiB of HBM per device.

```python
import math
import jax
import jax.numpy as jnp
import numpy as np
from jax import lax

D = 1024
HEADS = 16
HEAD_DIM = 64
FF = 4096
SEQ = 512
SEQ_DEV = 4
NSEQ = 32
TOKENS = 16384


def block_levels(own_key, dims, split, least, top_value):
    factor_of, own = 1.0, jax.random.fold_in(own_key, 6)
    for axis_at, parts in split:
        heights = jnp.exp(jax.random.uniform(jax.random.fold_in(own, axis_at), (parts,), jnp.float32, least / len(split), top_value / len(split)))
        factor_of = factor_of * jnp.repeat(heights, dims[axis_at] // parts).reshape([-1 if axis == axis_at else 1 for axis in range(len(dims))])
    return factor_of


def length_profile(count, total, reach, lean):
    weights = [(1 << 20) // math.isqrt(grade ** lean) + 1 for grade in range(2, count + 1)]
    surplus, holding = total - reach - (count - 1), [1] * (count - 1)
    while surplus > 0:
        movable = [i for i in range(count - 1) if holding[i] < reach]
        pool, remaining = sum([weights[i] for i in movable]), surplus
        for i in movable:
            more = min(reach - holding[i], max(1, remaining * weights[i] // pool), surplus)
            holding[i] = holding[i] + more
            surplus = surplus - more
    return np.array([reach] + holding)


def ragged(rng, count, total, most, skew):
    if count == 2:
        one = jax.random.randint(rng, (), max(1, total - most), min(most, total - 1) + 1)
        return jnp.stack([one, total - one])
    lengths = jnp.asarray(length_profile(count, total, most, skew), jnp.int32)
    twos = (count - 1) // 2
    giver, sink = lengths[1:1 + 2 * twos:2], lengths[2:2 + 2 * twos:2]
    margin = jnp.minimum(giver - 1, most - sink)
    moved = jax.random.randint(jax.random.fold_in(rng, 1), (twos,), 0, 1 << 20) % (margin + 1)
    lengths = lengths.at[1:1 + 2 * twos:2].set(giver - moved).at[2:2 + 2 * twos:2].set(sink + moved)
    return lengths[jax.random.permutation(jax.random.fold_in(rng, 2), count)]


def bell_draw(rng, extent, spread, limit, cuts=(), held_as=jnp.bfloat16):
    entries = spread * jax.random.normal(rng, extent, jnp.float32)
    if cuts:
        entries = entries * block_levels(rng, extent, cuts, -0.22, 0.18)
    return jnp.clip(entries, -limit, limit).astype(held_as)


def setup_inputs(seed: int = 0) -> dict:
    key_of = jax.random.split(jax.random.key(seed), 16)
    layer_input = bell_draw(key_of[0], (TOKENS, D), 1.0, 6.0, ((0, 32),))
    segment_ids = jax.vmap(lambda own: jnp.searchsorted(jnp.cumsum(ragged(own, max(3, SEQ // 32), SEQ, SEQ // 2, 2)), jnp.arange(SEQ), side="right"))(jax.random.split(key_of[1], NSEQ)).reshape((NSEQ, SEQ)).astype(jnp.int32)
    w_qkv = bell_draw(key_of[2], (3, D, D), D ** -0.5, 0.1875, ((2, 4),))
    b_qv = bell_draw(key_of[3], (2, D), 0.5, 3.0, ((1, 4),))
    w_out = bell_draw(key_of[4], (D, D), (D // 8) ** -0.5, 0.5, ((0, 4),))
    b_out = bell_draw(key_of[5], (D,), 0.5, 3.0)
    ln1_gain = jnp.clip(1.0 + 0.1 * jax.random.normal(key_of[6], (D,), jnp.float32), 0.5, 1.5)
    ln1_bias = bell_draw(key_of[7], (D,), 0.3, 2.0, (), jnp.float32)
    w_up = bell_draw(key_of[8], (D, FF), D ** -0.5, 0.1875, ((1, 4),))
    b_up = bell_draw(key_of[9], (FF,), 0.5, 3.0, ((0, 4),))
    w_down = bell_draw(key_of[10], (FF, D), FF ** -0.5, 0.09375, ((0, 4),))
    b_down = bell_draw(key_of[11], (D,), 0.3, 2.0)
    ln2_gain = jnp.clip(1.0 + 0.1 * jax.random.normal(key_of[12], (D,), jnp.float32), 0.5, 1.5)
    ln2_bias = bell_draw(key_of[13], (D,), 0.3, 2.0, (), jnp.float32)
    cotangent = bell_draw(key_of[14], (TOKENS, D), 1.0, 6.0, ((0, 32),))
    return dict(layer_input=layer_input, segment_ids=segment_ids, w_qkv=w_qkv, b_qv=b_qv, w_out=w_out, b_out=b_out, ln1_gain=ln1_gain, ln1_bias=ln1_bias, w_up=w_up, b_up=b_up, w_down=w_down, b_down=b_down, ln2_gain=ln2_gain, ln2_bias=ln2_bias, cotangent=cotangent)


norm_epsilon = 1e-05
highest = lax.Precision.HIGHEST

@jax.custom_vjp
def low(v):
    return lax.optimization_barrier(v.astype(jnp.bfloat16)).astype(jnp.float32)

@jax.custom_vjp
def low_back(v):
    return v

def low_keep(v):
    return (low(v), None)

def low_pass(kept, grad):
    return (grad,)

def back_keep(v):
    return (v, None)

def back_low(kept, grad):
    return (low(grad),)
low.defvjp(low_keep, low_pass)
low_back.defvjp(back_keep, back_low)

def layer_norm(token_rows, norm_gain, norm_bias):
    row_mean = lax.optimization_barrier(jnp.mean(token_rows, -1, keepdims=True))
    centered = token_rows - row_mean
    variance = lax.optimization_barrier(jnp.mean(centered * centered, -1, keepdims=True))
    return centered * lax.rsqrt(variance + norm_epsilon) * norm_gain + norm_bias

def attend(seq_item):
    queries, keys_low, values, segment = seq_item
    raw = low_back(jnp.einsum('qhd,khd->hqk', queries, keys_low, precision=highest))
    same_doc = segment[:, None] == segment[None, :]
    logits = jnp.where(same_doc[None], raw * HEAD_DIM ** (-0.5), -1e+30)
    row_max = lax.optimization_barrier(jnp.max(logits, -1, keepdims=True))
    exponent = jnp.exp(logits - row_max)
    probability = exponent / lax.optimization_barrier(jnp.sum(exponent, -1, keepdims=True))
    context = jnp.einsum('hqk,khd->qhd', low(probability), values, precision=highest)
    return low(low_back(context)).reshape(queries.shape[0], -1)

def forward(params, token_rows, segments):
    w_qkv, b_qv, w_out, b_out, ln1_gain, ln1_bias, w_up, b_up, w_down, b_down, ln2_gain, ln2_bias = params
    queries = low(low_back(jnp.dot(token_rows, w_qkv[0], precision=highest) + b_qv[0]))
    keys_low = low(low_back(jnp.dot(token_rows, w_qkv[1], precision=highest)))
    values = low(low_back(jnp.dot(token_rows, w_qkv[2], precision=highest) + b_qv[1]))
    head_shape = (segments.shape[0], segments.shape[1], HEADS, HEAD_DIM)
    context = lax.map(jax.checkpoint(attend), (queries.reshape(head_shape), keys_low.reshape(head_shape), values.reshape(head_shape), segments))
    context = context.reshape(token_rows.shape)
    attention = low_back(jnp.dot(context, w_out, precision=highest) + b_out)
    normed_one = layer_norm(token_rows + attention, ln1_gain, ln1_bias)
    up_proj = low_back(jnp.dot(low(normed_one), w_up, precision=highest) + b_up)
    activation = low(jax.nn.gelu(up_proj, approximate=False))
    branch = low_back(jnp.dot(activation, w_down, precision=highest) + b_down)
    return layer_norm(normed_one + branch, ln2_gain, ln2_bias)

def reference(layer_input, segment_ids, w_qkv, b_qv, w_out, b_out, ln1_gain, ln1_bias, w_up, b_up, w_down, b_down, ln2_gain, ln2_bias, cotangent):
    params = tuple((p.astype(jnp.float32) for p in (w_qkv, b_qv, w_out, b_out, ln1_gain, ln1_bias, w_up, b_up, w_down, b_down, ln2_gain, ln2_bias)))
    groups = NSEQ // SEQ_DEV
    group_rows = layer_input.astype(jnp.float32).reshape(groups, SEQ_DEV * SEQ, D)
    group_segs = segment_ids.reshape(groups, SEQ_DEV, SEQ)
    group_cots = cotangent.astype(jnp.float32).reshape(groups, SEQ_DEV * SEQ, D)

    def group_step(totals, seq_item):
        token_rows, segments, incoming = seq_item
        result, pull = jax.vjp(lambda weights, inputs: forward(weights, inputs, segments), params, token_rows)
        d_params, d_rows = pull(incoming)
        totals = jax.tree.map(lambda summed, update: summed + update, totals, d_params)
        return (totals, (result.astype(jnp.bfloat16), d_rows))
    zeros = jax.tree.map(jnp.zeros_like, params)
    totals, (results, d_rows) = lax.scan(group_step, zeros, (group_rows, group_segs, group_cots))
    output = results.reshape(TOKENS, D)
    grad_input = d_rows.reshape(TOKENS, D)
    return (output, grad_input, totals[0], totals[1], totals[2], totals[3], totals[4], totals[5], totals[6], totals[7], totals[8], totals[9], totals[10], totals[11])
```

```python
import jax
import jax.numpy as jnp
from jax import lax
from jax.experimental import pallas as pl
from jax.experimental.pallas import tpu as pltpu
from jax.sharding import PartitionSpec as P

HEAD_DIM = 64


norm_epsilon = 1e-05
root_half = 0.7071067811865476
inverse_root_two_pi = 0.3989422804014327


def layer_norm(token_rows, norm_gain, norm_bias):
    row_mean = jnp.mean(token_rows, -1, keepdims=True)
    centered = token_rows - row_mean
    variance = jnp.mean(centered * centered, -1, keepdims=True)
    inv_std = lax.rsqrt(variance + norm_epsilon)
    scaled = centered * inv_std
    return (scaled * norm_gain + norm_bias, scaled, inv_std)


def norm_back(incoming, scaled, inv_std, norm_gain):
    weighted = incoming * norm_gain
    d_rows = inv_std * (
        weighted
        - jnp.mean(weighted, -1, keepdims=True)
        - scaled * jnp.mean(weighted * scaled, -1, keepdims=True)
    )
    return (d_rows, jnp.sum(incoming * scaled, 0), jnp.sum(incoming, 0))


def gelu_value(up_proj):
    return 0.5 * up_proj * (1.0 + lax.erf(up_proj * root_half))


def gelu_slope(up_proj):
    return (
        0.5 * (1.0 + lax.erf(up_proj * root_half))
        + up_proj * jnp.exp(-0.5 * up_proj * up_proj) * inverse_root_two_pi
    )


def split_heads(matrix, head_count):
    return matrix.reshape(matrix.shape[0], head_count, -1)


def project(token_rows, w_qkv, b_qv):
    queries = (
        jnp.dot(token_rows, w_qkv[0], preferred_element_type=jnp.float32)
        + b_qv[0].astype(jnp.float32)
    ).astype(jnp.bfloat16)
    keys_low = jnp.dot(token_rows, w_qkv[1], preferred_element_type=jnp.float32).astype(
        jnp.bfloat16
    )
    values = (
        jnp.dot(token_rows, w_qkv[2], preferred_element_type=jnp.float32)
        + b_qv[1].astype(jnp.float32)
    ).astype(jnp.bfloat16)
    return (queries, keys_low, values)


def scores(queries, keys_low, segment, head_count, score_scale):
    raw = jnp.einsum(
        "qhd,khd->hqk",
        split_heads(queries, head_count),
        split_heads(keys_low, head_count),
        preferred_element_type=jnp.float32,
    )
    same_doc = segment[:, None] == segment[None, :]
    return jnp.where(same_doc[None], raw * score_scale, -1e30)


def mix_values(prob_low, values, head_count):
    context = jnp.einsum(
        "hqk,khd->qhd",
        prob_low,
        split_heads(values, head_count),
        preferred_element_type=jnp.float32,
    )
    return context.reshape(context.shape[0], -1).astype(jnp.bfloat16)


def ffn_forward(normed_low, up_weight, up_bias, down_weight):
    up_proj = jnp.dot(normed_low, up_weight, preferred_element_type=jnp.float32) + up_bias.astype(
        jnp.float32
    )
    activation = gelu_value(up_proj).astype(jnp.bfloat16)
    return jnp.dot(activation, down_weight, preferred_element_type=jnp.float32)


def ffn_backward(normed_low, branch_low, up_weight, up_bias, down_weight):
    up_proj = jnp.dot(normed_low, up_weight, preferred_element_type=jnp.float32) + up_bias.astype(
        jnp.float32
    )
    activation = gelu_value(up_proj).astype(jnp.bfloat16)
    grad_down = jnp.einsum("tf,td->fd", activation, branch_low, preferred_element_type=jnp.float32)
    d_activation = jnp.einsum(
        "td,fd->tf", branch_low, down_weight, preferred_element_type=jnp.float32
    )
    d_up = (d_activation * gelu_slope(up_proj)).astype(jnp.bfloat16)
    grad_up = jnp.einsum("td,tf->df", normed_low, d_up, preferred_element_type=jnp.float32)
    grad_up_bias = jnp.sum(d_up.astype(jnp.float32), 0)
    return (grad_up, grad_up_bias, grad_down, d_up)


def general(
    layer_input,
    segment_ids,
    w_qkv,
    b_qv,
    w_out,
    b_out,
    ln1_gain,
    ln1_bias,
    w_up,
    b_up,
    w_down,
    b_down,
    ln2_gain,
    ln2_bias,
    cotangent,
):
    my_rows, model_width = layer_input.shape
    seq_len = segment_ids.shape[1]
    score_scale = HEAD_DIM ** (-0.5)
    whole_input = lax.all_gather(layer_input, "tensor", axis=0, tiled=True)
    seq_input = whole_input.reshape(segment_ids.shape[0], seq_len, model_width)
    attn_width = w_out.shape[0]
    head_count = attn_width // HEAD_DIM

    def forward_seq(running, seq_item):
        token_rows, segment = seq_item
        queries, keys_low, values = project(token_rows, w_qkv, b_qv)
        logits = scores(queries, keys_low, segment, head_count, score_scale)
        row_max = jnp.max(logits, -1, keepdims=True)
        exponent = jnp.exp(logits - row_max)
        expo_sum = jnp.sum(exponent, -1, keepdims=True)
        prob_low = (exponent / expo_sum).astype(jnp.bfloat16)
        return (running, (mix_values(prob_low, values, head_count), row_max + jnp.log(expo_sum)))

    _, (seq_context, seq_lse) = lax.scan(forward_seq, None, (seq_input, segment_ids))
    all_context = seq_context.reshape(-1, attn_width)
    attention = lax.psum_scatter(
        jnp.dot(all_context, w_out, preferred_element_type=jnp.float32),
        "tensor",
        scatter_dimension=0,
        tiled=True,
    ) + b_out.astype(jnp.float32)
    normed_one, scaled_one, inv_one = layer_norm(
        layer_input.astype(jnp.float32) + attention, ln1_gain, ln1_bias
    )
    normed_low = normed_one.astype(jnp.bfloat16)
    whole_normed = lax.all_gather(normed_low, "tensor", axis=0, tiled=True)
    branch = lax.psum_scatter(
        ffn_forward(whole_normed, w_up, b_up, w_down), "tensor", scatter_dimension=0, tiled=True
    )
    normed_two, scaled_two, inv_two = layer_norm(
        normed_one + branch + b_down.astype(jnp.float32), ln2_gain, ln2_bias
    )
    d_second, grad_ln2_gain, grad_ln2_bias = norm_back(
        cotangent.astype(jnp.float32), scaled_two, inv_two, ln2_gain
    )
    branch_low = d_second.astype(jnp.bfloat16)
    grad_b_down = jnp.sum(branch_low.astype(jnp.float32), 0)
    whole_branch = lax.all_gather(branch_low, "tensor", axis=0, tiled=True)
    grad_w_up, grad_b_up, grad_w_down, d_up = ffn_backward(
        whole_normed, whole_branch, w_up, b_up, w_down
    )
    d_normed = lax.psum_scatter(
        jnp.einsum("tf,df->td", d_up, w_up, preferred_element_type=jnp.float32),
        "tensor",
        scatter_dimension=0,
        tiled=True,
    )
    d_first, grad_ln1_gain, grad_ln1_bias = norm_back(
        d_second + d_normed, scaled_one, inv_one, ln1_gain
    )
    attention_low = d_first.astype(jnp.bfloat16)
    grad_b_out = jnp.sum(attention_low.astype(jnp.float32), 0)
    whole_grad = lax.all_gather(attention_low, "tensor", axis=0, tiled=True)
    seq_grad = whole_grad.reshape(seq_input.shape[0], seq_len, model_width)

    def backward_seq(running, seq_item):
        grad_qkv, grad_bias, grad_out = running
        token_rows, segment, seq_lse_one, grad_rows = seq_item
        queries, keys_low, values = project(token_rows, w_qkv, b_qv)
        logits = scores(queries, keys_low, segment, head_count, score_scale)
        probability = jnp.exp(logits - seq_lse_one)
        prob_low = probability.astype(jnp.bfloat16)
        context = mix_values(prob_low, values, head_count)
        grad_out = grad_out + jnp.einsum(
            "te,td->ed", context, grad_rows, preferred_element_type=jnp.float32
        )
        d_context = jnp.einsum(
            "td,ed->te", grad_rows, w_out, preferred_element_type=jnp.float32
        ).astype(jnp.bfloat16)
        d_heads = split_heads(d_context, head_count)
        d_prob = jnp.einsum(
            "qhd,khd->hqk",
            d_heads,
            split_heads(values, head_count),
            preferred_element_type=jnp.float32,
        )
        d_values = (
            jnp.einsum("hqk,qhd->khd", prob_low, d_heads, preferred_element_type=jnp.float32)
            .reshape(seq_len, -1)
            .astype(jnp.bfloat16)
        )
        inner_sum = jnp.sum(probability * d_prob, -1, keepdims=True)
        d_raw = (probability * (d_prob - inner_sum) * score_scale).astype(jnp.bfloat16)
        d_queries = (
            jnp.einsum(
                "hqk,khd->qhd",
                d_raw,
                split_heads(keys_low, head_count),
                preferred_element_type=jnp.float32,
            )
            .reshape(seq_len, -1)
            .astype(jnp.bfloat16)
        )
        d_keys = (
            jnp.einsum(
                "hqk,qhd->khd",
                d_raw,
                split_heads(queries, head_count),
                preferred_element_type=jnp.float32,
            )
            .reshape(seq_len, -1)
            .astype(jnp.bfloat16)
        )
        grad_qkv = grad_qkv + jnp.stack(
            [
                jnp.einsum("td,te->de", token_rows, gradient, preferred_element_type=jnp.float32)
                for gradient in (d_queries, d_keys, d_values)
            ]
        )
        grad_bias = grad_bias + jnp.stack(
            [jnp.sum(d_queries.astype(jnp.float32), 0), jnp.sum(d_values.astype(jnp.float32), 0)]
        )
        return ((grad_qkv, grad_bias, grad_out), (d_queries, d_keys, d_values))

    start_grads = (
        jnp.zeros((3, model_width, attn_width), jnp.float32),
        jnp.zeros((2, attn_width), jnp.float32),
        jnp.zeros((attn_width, model_width), jnp.float32),
    )
    (grad_w_qkv, grad_b_qv, grad_w_out), seq_d = lax.scan(
        backward_seq, start_grads, (seq_input, segment_ids, seq_lse, seq_grad)
    )
    all_d = [gradient.reshape(-1, attn_width) for gradient in seq_d]
    summed = jnp.zeros((my_rows * lax.axis_size("tensor"), model_width), jnp.float32)
    for which in range(3):
        piece = all_d[which]
        summed = summed + jnp.einsum(
            "te,de->td", piece, w_qkv[which], preferred_element_type=jnp.float32
        )
    grad_input = d_first + lax.psum_scatter(
        summed.astype(jnp.bfloat16), "tensor", scatter_dimension=0, tiled=True
    ).astype(jnp.float32)
    grad_w_qkv, grad_b_qv, grad_w_out, grad_w_up, grad_b_up, grad_w_down = (
        lax.psum(grad_w_qkv.astype(jnp.bfloat16), "dp").astype(jnp.float32),
        lax.psum(grad_b_qv.astype(jnp.bfloat16), "dp").astype(jnp.float32),
        lax.psum(grad_w_out.astype(jnp.bfloat16), "dp").astype(jnp.float32),
        lax.psum(grad_w_up.astype(jnp.bfloat16), "dp").astype(jnp.float32),
        lax.psum(grad_b_up.astype(jnp.bfloat16), "dp").astype(jnp.float32),
        lax.psum(grad_w_down.astype(jnp.bfloat16), "dp").astype(jnp.float32),
    )
    grad_b_out, grad_ln1_gain, grad_ln1_bias, grad_b_down, grad_ln2_gain, grad_ln2_bias = lax.psum(
        (grad_b_out, grad_ln1_gain, grad_ln1_bias, grad_b_down, grad_ln2_gain, grad_ln2_bias),
        ("dp", "tensor"),
    )
    return (
        normed_two.astype(jnp.bfloat16),
        grad_input,
        grad_w_qkv,
        grad_b_qv,
        grad_w_out,
        grad_b_out,
        grad_ln1_gain,
        grad_ln1_bias,
        grad_w_up,
        grad_b_up,
        grad_w_down,
        grad_b_down,
        grad_ln2_gain,
        grad_ln2_bias,
    )


F32 = jnp.float32
BF = jnp.bfloat16
LOG2E = 1.4426950408889634


def dotf(a, b, ca, cb):
    return lax.dot_general(a, b, (((ca,), (cb,)), ((), ())), preferred_element_type=F32)


class Order:
    def __init__(self):
        self.token = None

    def __call__(self, kernel, outs, args, name, limit, aliases=None, smem=0):
        count = len(args)
        specs = [pl.BlockSpec(memory_space=pltpu.SMEM)] * smem + [pl.BlockSpec()] * (count - smem)
        if self.token is not None:
            args = (*args, self.token)
            specs.append(pl.BlockSpec(memory_space=pl.ANY))

        def body(*refs):
            kernel(*refs[:count], *refs[len(args) :])

        result = pl.pallas_call(
            body,
            out_shape=tuple(jax.ShapeDtypeStruct(s, d) for s, d in outs),
            in_specs=specs,
            input_output_aliases=aliases or {},
            compiler_params=pltpu.CompilerParams(vmem_limit_bytes=limit << 20),
            name=name,
        )(*args)
        self.token = result[-1]
        return result

    def plain(self, fn, first, *rest):
        first, _ = lax.optimization_barrier((first, self.token))
        out = lax.optimization_barrier(fn(first, *rest))
        self.token = out[-1] if isinstance(out, (tuple, list)) else out
        return out

    def now(self, value):
        return lax.optimization_barrier((value, self.token))[0]


def pack_attn_kernel(core, w_qkv, w_out, b_qv, qkm, vom, qko, voo):
    width = w_qkv.shape[1]
    zero = jnp.zeros((16, 128), BF)
    first = lax.broadcasted_iota(jnp.int32, (16, 128), 0) == 0
    for qk, vo, half in ((qkm, vom, core[0]), (qko, voo, 1 - core[0])):
        part = pl.ds(pl.multiple_of(half * 128, 128), 128)
        qk[0:width, 0:128] = w_qkv[0, :, part]
        qk[0:width, 128:256] = w_qkv[1, :, part]
        vo[0:width, 0:128] = w_qkv[2, :, part]
        vo[0:width, 128:256] = w_out[part, :].astype(F32).T.astype(BF)
        qk[width : width + 16, 0:128] = jnp.where(first, b_qv[0:1, part].astype(F32), 0.0).astype(BF)
        vo[width : width + 16, 0:128] = jnp.where(first, b_qv[1:2, part].astype(F32), 0.0).astype(BF)
        qk[width : width + 16, 128:256] = zero
        vo[width : width + 16, 128:256] = zero


def pack_attn(order, core, w_qkv, w_out, b_qv):
    out = ((w_qkv.shape[1] + 16, 256), BF)
    return order(pack_attn_kernel, (out,) * 4, (core, w_qkv, w_out, b_qv), "pack_attn", 8, smem=1)


def pack_ffn_kernel(core, w_up, b_up, w_down, upm, dnm, upo, dno):
    width = w_up.shape[0]
    hid = w_up.shape[1] // 2
    first = lax.broadcasted_iota(jnp.int32, (16, hid), 0) == 0
    for up, dn, half in ((upm, dnm, core[0]), (upo, dno, 1 - core[0])):
        part = pl.ds(pl.multiple_of(half * hid, hid), hid)
        up[0:width, :] = w_up[:, part]
        up[width : width + 16, :] = jnp.where(first, b_up[0:1, part].astype(F32), 0.0).astype(BF)
        dn[...] = w_down[part, :]


def pack_ffn(order, core, w_up, b_up, w_down):
    width, hid = w_up.shape[0], w_up.shape[1] // 2
    outs = (((width + 16, hid), BF), ((hid, width), BF)) * 2
    return order(pack_ffn_kernel, outs, (core, w_up, b_up, w_down), "pack_ffn", 12, smem=1)


def attn_fwd_kernel(x_ref, bias_ref, qkm, vom, qko, voo, acc_ref, out_ref, pt_m, pt_o, qkv_m, qkv_o, ctx_m, ctx_o):
    width = x_ref.shape[1]
    x = x_ref[...]
    rows = x.shape[0]
    row = lax.broadcasted_iota(jnp.int32, (128, rows), 0)
    total = acc_ref[...]
    for qk, vo, pt, qkv, ctx_ref in ((qkm, vom, pt_m, qkv_m, ctx_m), (qko, voo, pt_o, qkv_o, ctx_o)):
        qkf = dotf(x, qk[0:width, :], 1, 0) + qk[width : width + 16, :][0:1, :].astype(F32)
        vf = dotf(x, vo[0:width, 0:128], 1, 0) + vo[width : width + 16, 0:128][0:1, :].astype(F32)
        k = qkf[:, 128:].astype(BF)
        qkv[0] = qkf[:, :128].astype(BF)
        qkv[1] = k
        qkv[2] = vf.astype(BF)
        q_t = qkf[:, :128].T.astype(BF)
        v_t = vf.T.astype(BF)
        outs = []
        for h in range(2):
            q_h = jnp.where((row // HEAD_DIM) == h, q_t, jnp.zeros_like(q_t))
            s = dotf(k, q_h, 1, 0) * (HEAD_DIM**-0.5 * LOG2E) + bias_ref[...]
            e = jnp.exp2(s - jnp.max(s, 0, keepdims=True))
            p = (e * (1.0 / jnp.sum(e, 0, keepdims=True))).astype(BF)
            pt[h] = p
            outs.append(dotf(v_t[h * HEAD_DIM : (h + 1) * HEAD_DIM, :], p, 1, 0))
        ctx = jnp.concatenate(outs, 0).T.astype(BF)
        ctx_ref[...] = ctx
        total = total + dotf(ctx, vo[0:width, 128:256], 1, 1)
    out_ref[...] = total


def attn_fwd(order, x, bias, qkm, vom, qko, voo, acc):
    rows, width = x.shape
    pt, qkv, ctx = ((2, rows, rows), BF), ((3, rows, 128), BF), ((rows, 128), BF)
    outs = (((rows, width), F32), pt, pt, qkv, qkv, ctx, ctx)
    return order(attn_fwd_kernel, outs, (x, bias, qkm, vom, qko, voo, acc), "attn_fwd", 14, {6: 0})


def part_rows(part, half, extra):
    whole = ((0, half), (half + extra, 2 * half + extra), (2 * half + extra, 2 * half + 2 * extra), (half, half + extra))
    own = ((0, half), (0, half), (half, half + extra), (half, half + extra))
    return whole[part], own[part]


def add_got(value, got, part, half, extra):
    whole, own = part_rows(part, half, extra)
    for kind, ref in got:
        if kind == "whole":
            value = value + ref[whole[0] : whole[1], :].astype(F32)
        elif (kind == "top") == (part == 0):
            value = value + ref[own[0] : own[1], :].astype(F32)
    return value


def put(outs, part, half, extra, value):
    whole, own = part_rows(part, half, extra)
    if len(outs) == 1:
        outs[0][whole[0] : whole[1], :] = value.astype(BF)
    else:
        outs[part in (1, 2)][own[0] : own[1], :] = value.astype(BF)


def gradient_shapes(width, columns, extra, split):
    if split:
        return (((width // 2 + extra, columns), BF),) * 2
    return (((width + 2 * extra, columns), BF),)


def outer(order, left_t, right, got, split, extra, name, odd=None):
    kinds = [kind for kind, _ in got]
    width = left_t.shape[0]
    half = width // 2

    def kernel(*refs):
        if odd is not None:
            flag, *refs = refs
        left_ref, right_ref, *refs = refs
        received = list(zip(kinds, refs))
        outs = refs[len(kinds) :]
        if odd is not None:
            swapped = flag[0] == 1
        values = []
        for part in (0, 1):
            value = dotf(left_ref[part * half : (part + 1) * half, :], right_ref[...], 1, 0)
            values.append(add_got(value, received, part, half, extra))
        if extra:
            first = lax.broadcasted_iota(jnp.int32, (extra, right_ref.shape[1]), 0) == 0
            row = jnp.where(first, jnp.sum(right_ref[...].astype(F32), 0, keepdims=True), 0.0)
            row = add_got(row, received, 2, half, extra)
            zero = jnp.zeros(row.shape, F32)
        if odd is None:
            for part in (0, 1):
                put(outs, part, half, extra, values[part])
            if extra:
                put(outs, 2, half, extra, row)
                put(outs, 3, half, extra, zero)
        else:
            outs[0][0:half, :] = jnp.where(swapped, values[1], values[0]).astype(BF)
            outs[1][0:half, :] = jnp.where(swapped, values[0], values[1]).astype(BF)
            if extra:
                outs[0][half:, :] = jnp.where(swapped, row, zero).astype(BF)
                outs[1][half:, :] = jnp.where(swapped, zero, row).astype(BF)

    outs = gradient_shapes(width, right.shape[1], extra, split)
    flags = () if odd is None else (odd,)
    return order(kernel, outs, (*flags, left_t, right, *(v for _, v in got)), name, 10, smem=len(flags))


def relay(order, row_part, bottom, col_part, top, extra):
    half = row_part.shape[0] // 2

    def kernel(row_ref, bot_ref, col_ref, top_ref, row_out, col_out):
        row_out[0:half, :] = row_ref[0:half, :]
        row_out[half:, :] = (row_ref[half:, :].astype(F32) + bot_ref[...].astype(F32)).astype(BF)
        col_out[half:, :] = col_ref[half:, :]
        col_out[0:half, :] = (col_ref[0:half, :].astype(F32) + top_ref[...].astype(F32)).astype(BF)

    out = (row_part.shape, BF)
    return order(kernel, (out, out), (row_part, bottom, col_part, top), "relay", 8, {0: 0, 2: 1})


def own_sum(order, odd, own, row_part, col_part):
    half = own.shape[0] // 2

    def kernel(flag, own_ref, row_ref, col_ref, keep, send):
        swapped = flag[0] == 1
        total = own_ref[...].astype(F32) + row_ref[...].astype(F32) + col_ref[...].astype(F32)
        keep[...] = jnp.where(swapped, total[half:], total[:half]).astype(BF)
        send[...] = jnp.where(swapped, total[:half], total[half:]).astype(BF)

    out = ((half, own.shape[1]), BF)
    return order(kernel, (out, out), (odd, own, row_part, col_part), "own_sum", 8, smem=1)


def attn_bwd(order, g, gt, xt, pt, qkv, ctx, qk, vo, acc, got, split):
    rows, width = g.shape
    half = width // 2
    kinds = [kind for kind, _ in got]

    def kernel(g_ref, gt_ref, xt_ref, pt_ref, qkv_ref, ctx_ref, qk, vo, acc_ref, *refs):
        received = list(zip(kinds, refs))
        out_ref, *outs = refs[len(kinds) :]
        row = lax.broadcasted_iota(jnp.int32, (128, rows), 0)
        lane = lax.broadcasted_iota(jnp.int32, (rows, 128), 1)
        first = lax.broadcasted_iota(jnp.int32, (16, 512), 0) == 0
        ctx = ctx_ref[...]
        d_o = dotf(g_ref[...], vo[0:width, 128:256], 1, 0).astype(BF)
        d_ot = d_o.astype(F32).T
        prod = d_ot * ctx.astype(F32).T * (HEAD_DIM**-0.5)
        d_ot = (d_ot * (HEAD_DIM**-0.5)).astype(BF)
        k_t = qkv_ref[1].astype(F32).T.astype(BF)
        dvs, dks, dqs = [], [], []
        for h in range(2):
            head = slice(h * HEAD_DIM, (h + 1) * HEAD_DIM)
            inner = jnp.sum(prod[head, :], 0, keepdims=True)
            p = pt_ref[h]
            dvs.append(dotf(p, d_o, 1, 0))
            d_h = jnp.where((row // HEAD_DIM) == h, d_ot, jnp.zeros_like(d_ot))
            ds = (p.astype(F32) * (dotf(qkv_ref[2], d_h, 1, 0) - inner)).astype(BF)
            dks.append(dotf(ds, qkv_ref[0], 1, 0))
            dqs.append(dotf(k_t[head, :], ds, 1, 0))
        dv = jnp.where(lane < HEAD_DIM, dvs[0], dvs[1]).astype(BF)
        dk = jnp.where(lane < HEAD_DIM, dks[0], dks[1]).astype(BF)
        dq = jnp.concatenate(dqs, 0).T.astype(BF)
        dqk = jnp.concatenate([dq, dk], 1)
        out_ref[...] = acc_ref[...] + dotf(dqk, qk[0:width, :], 1, 1) + dotf(dv, vo[0:width, 0:128], 1, 1)
        for part in (0, 1):
            piece = slice(part * half, (part + 1) * half)
            value = jnp.concatenate(
                [
                    dotf(xt_ref[piece, :], dqk, 1, 0),
                    dotf(xt_ref[piece, :], dv, 1, 0),
                    dotf(gt_ref[piece, :], ctx, 1, 0),
                ],
                1,
            )
            put(outs, part, half, 16, add_got(value, received, part, half, 16))
        sums = [jnp.sum(v.astype(F32), 0, keepdims=True) for v in (dqk, dv)]
        bias_row = jnp.where(first, jnp.concatenate([*sums, jnp.zeros((1, 128), F32)], 1), 0.0)
        put(outs, 2, half, 16, add_got(bias_row, received, 2, half, 16))
        put(outs, 3, half, 16, jnp.zeros((16, 512), F32))

    outs = (((rows, width), F32), *gradient_shapes(width, 512, 16, split))
    args = (g, gt, xt, pt, qkv, ctx, qk, vo, acc, *(v for _, v in got))
    return order(kernel, outs, args, "attn_bwd", 14, {8: 0})


def ffn_fwd_kernel(n_ref, upm, dnm, upo, dno, acc_ref, out_ref, act_m, slope_m, act_o, slope_o):
    rows, width = n_ref.shape
    step = rows // 2

    def body(i, carry):
        part = pl.ds(pl.multiple_of(i * step, step), step)
        n = n_ref[part, :]
        total = acc_ref[part, :]
        for up, dn, act_ref, slope_ref in ((upm, dnm, act_m, slope_m), (upo, dno, act_o, slope_o)):
            u = dotf(n, up[0:width, :], 1, 0) + up[width : width + 16, :][0:1, :].astype(F32)
            cdf = 0.5 + 0.5 * lax.erf(u * root_half)
            act = (u * cdf).astype(BF)
            act_ref[part, :] = act
            slope = cdf + u * (jnp.exp2(u * u * (-0.5 * LOG2E)) * inverse_root_two_pi)
            slope_ref[part, :] = slope.astype(BF)
            total = total + dotf(act, dn[...], 1, 0)
        out_ref[part, :] = total
        return carry

    lax.fori_loop(0, 2, body, 0)


def ffn_fwd(order, n, upm, dnm, upo, dno, acc):
    rows, width = n.shape
    mid = ((rows, upm.shape[1]), BF)
    return order(
        ffn_fwd_kernel, (((rows, width), F32), mid, mid, mid, mid), (n, upm, dnm, upo, dno, acc), "ffn_fwd", 12, {5: 0}
    )


def ffn_bwd_kernel(g_ref, upm, dnm, slope_m, upo, dno, slope_o, acc_ref, out_ref, d_m, d_o):
    width = g_ref.shape[1]
    total = acc_ref[...]
    for up, dn, slope, d_ref in ((upm, dnm, slope_m, d_m), (upo, dno, slope_o, d_o)):
        d_up = (dotf(g_ref[...], dn[...], 1, 1) * slope[...].astype(F32)).astype(BF)
        d_ref[...] = d_up
        total = total + dotf(d_up, up[0:width, :], 1, 1)
    out_ref[...] = total


def ffn_bwd(order, g, upm, dnm, slope_m, upo, dno, slope_o, acc):
    rows, width = g.shape
    mid = (slope_m.shape, BF)
    args = (g, upm, dnm, slope_m, upo, dno, slope_o, acc)
    return order(ffn_bwd_kernel, (((rows, width), F32), mid, mid), args, "ffn_bwd", 12, {7: 0})


def row_loop(rows, body, start):
    block = 128

    def wrapped(i, carry):
        return body(pl.ds(pl.multiple_of(i * block, block), block), carry)

    return lax.fori_loop(0, rows // block, wrapped, start)


def standard(v):
    centered = v - jnp.mean(v, -1, keepdims=True)
    inv = lax.rsqrt(jnp.mean(centered * centered, -1, keepdims=True) + norm_epsilon)
    return centered * inv, inv


def back_through(g, scaled, inv, gain):
    e = g * gain
    return inv * (e - jnp.mean(e, -1, keepdims=True) - scaled * jnp.mean(e * scaled, -1, keepdims=True))


def first_norm_kernel(x_ref, acc_ref, gain, bias, b_down, out_ref, low_ref, low_t):
    def body(part, carry):
        scaled, _ = standard(x_ref[part, :].astype(F32) + acc_ref[part, :])
        normed = scaled * gain[...] + bias[...]
        out_ref[part, :] = normed + b_down[...].astype(F32)
        low = normed.astype(BF)
        low_ref[part, :] = low
        low_t[:, part] = low.astype(F32).T.astype(BF)
        return carry

    row_loop(x_ref.shape[0], body, 0)


def first_norm(order, x, acc, gain, bias, b_down):
    rows, width = x.shape
    outs = (((rows, width), F32), ((rows, width), BF), ((width, rows), BF))
    return order(first_norm_kernel, outs, (x, acc, gain[None], bias[None], b_down[None]), "first_norm", 12)


def emit_back(part, carry, g, scaled, inv, gain, out_ref, low_ref, low_t):
    d_rows = back_through(g, scaled, inv, gain)
    out_ref[part, :] = d_rows
    low = d_rows.astype(BF)
    low_ref[part, :] = low
    low = low.astype(F32)
    low_t[:, part] = low.T.astype(BF)
    terms = (g * scaled, g, low)
    return tuple(c + jnp.sum(t, 0, keepdims=True) for c, t in zip(carry, terms))


def put_sums(sums_ref, carry):
    row = lax.broadcasted_iota(jnp.int32, sums_ref.shape, 0)
    sums_ref[...] = jnp.where(row == 0, carry[0], jnp.where(row == 1, carry[1], jnp.where(row == 2, carry[2], 0.0)))


def second_norm_kernel(sum_ref, cot_ref, gain, bias, d_ref, y_ref, low_ref, low_t, sums_ref):
    def body(part, carry):
        scaled, inv = standard(sum_ref[part, :])
        y_ref[part, :] = (scaled * gain[...] + bias[...]).astype(BF)
        g = cot_ref[part, :].astype(F32)
        return emit_back(part, carry, g, scaled, inv, gain[...], d_ref, low_ref, low_t)

    zero = jnp.zeros((1, sum_ref.shape[1]), F32)
    put_sums(sums_ref, row_loop(sum_ref.shape[0], body, (zero,) * 3))


def back_outs(rows, width):
    return (((rows, width), F32), ((rows, width), BF), ((rows, width), BF), ((width, rows), BF), ((8, width), F32))


def second_norm(order, total, cotangent, gain, bias):
    rows, width = total.shape
    return order(
        second_norm_kernel, back_outs(rows, width), (total, cotangent, gain[None], bias[None]), "second_norm", 12, {0: 0}
    )


def first_back_kernel(x_ref, acc_ref, gain, d_ref, out_ref, x_t, low_ref, low_t, sums_ref):
    def body(part, carry):
        x = x_ref[part, :].astype(F32)
        x_t[:, part] = x.T.astype(BF)
        scaled, inv = standard(x + acc_ref[part, :])
        return emit_back(part, carry, d_ref[part, :], scaled, inv, gain[...], out_ref, low_ref, low_t)

    zero = jnp.zeros((1, x_ref.shape[1]), F32)
    put_sums(sums_ref, row_loop(x_ref.shape[0], body, (zero,) * 3))


def first_back(order, x, acc, gain, d_normed):
    rows, width = x.shape
    outs = list(back_outs(rows, width))
    outs[1] = ((width, rows), BF)
    return order(first_back_kernel, tuple(outs), (x, acc, gain[None], d_normed), "first_back", 12, {3: 0})

CORE = [(d, d ^ 1) for d in range(8)]
ROW = [(t, t ^ 1) for t in range(4)]
COL = [(t, t ^ 2) for t in range(4)]
NEAR = [(d, d ^ 2) for d in range(8)]
FAR = [(d, d ^ 4) for d in range(8)]


def swap_core(v):
    return lax.ppermute(v, "dp", CORE)


def swap_row(v):
    return lax.ppermute(v, "tensor", ROW)


def swap_col(v):
    return lax.ppermute(v, "tensor", COL)


def swap_near(v):
    return lax.ppermute(v, "dp", NEAR)


def swap_far(v):
    return lax.ppermute(v, "dp", FAR)


def add_low(a, b):
    return (a.astype(F32) + b.astype(F32)).astype(BF)


class Piece:
    def __init__(self, order, odd, extra):
        self.order, self.odd, self.extra = order, odd, extra
        self.other, self.mine = [None] * 4, [None] * 4

    def diagonal(self, top, bottom):
        self.top, self.bottom = swap_row(top), swap_col(bottom)

    def direct(self, row_part, col_part):
        self.row_part, self.col_part = swap_row(row_part), swap_col(col_part)

    def along_z(self, keep, send):
        self.keep, self.got = keep, swap_near(send)

    def second(self):
        self.keep = self.order.plain(add_low, self.got, self.keep)
        self.got = swap_far(self.keep)

    def third(self):
        self.keep = self.order.plain(add_low, self.got, self.keep)
        self.got = swap_near(self.keep)
        self.keep_o = swap_core(self.keep)

    def last(self):
        self.got_o = swap_core(self.order.now(self.got))

    def halves(self, first_core, odd):
        sides = []
        for mine, other in ((self.keep, self.keep_o), (self.got, self.got_o)):
            sides.append((jnp.where(first_core, mine, other), jnp.where(first_core, other, mine)))
        kept, got = sides
        return [(jnp.where(odd, got[c], kept[c]), jnp.where(odd, kept[c], got[c])) for c in (0, 1)]


def fast(
    layer_input,
    segment_ids,
    w_qkv,
    b_qv,
    w_out,
    b_out,
    ln1_gain,
    ln1_bias,
    w_up,
    b_up,
    w_down,
    b_down,
    ln2_gain,
    ln2_bias,
    cotangent,
):
    rows, width = layer_input.shape
    hidden = w_up.shape[1] // 2
    core = lax.axis_index("dp") % 2
    first_core = core == 0
    odd_index = (lax.axis_index("dp") // 2) % 2
    is_odd = odd_index == 1
    odd = odd_index.astype(jnp.int32)[None]
    core = core.astype(jnp.int32)[None]
    segment = lax.dynamic_index_in_dim(segment_ids, lax.axis_index("tensor"), keepdims=False)
    order = Order()

    qk_m, qk_o, vo_m, vo_o = [None] * 4, [None] * 4, [None] * 4, [None] * 4
    up_m, up_o, dn_m, dn_o = [None] * 4, [None] * 4, [None] * 4, [None] * 4
    qk_m[0], vo_m[0], qk_o[0], vo_o[0] = pack_attn(order, core, w_qkv, w_out, b_qv)
    qk_m[1], qk_m[2] = swap_row(qk_m[0]), swap_col(qk_m[0])
    vo_m[1], vo_m[2] = swap_row(vo_m[0]), swap_col(vo_m[0])
    up_m[0], dn_m[0], up_o[0], dn_o[0] = pack_ffn(order, core, w_up, b_up[None], w_down)

    bias = jnp.where(segment[:, None] == segment[None, :], 0.0, -1e30).astype(F32)
    attention = jnp.broadcast_to(b_out.astype(F32), (rows, width))
    saved = [None] * 4

    def attend(r, acc):
        acc, *saved[r] = attn_fwd(order, layer_input, bias, qk_m[r], vo_m[r], qk_o[r], vo_o[r], acc)
        return acc

    attention = attend(0, attention)
    now = order.now
    up_m[1], up_m[2] = swap_row(now(up_m[0])), swap_col(now(up_m[0]))
    qk_m[3], vo_m[3] = swap_row(now(qk_m[2])), swap_col(now(vo_m[1]))
    for r in (1, 2):
        qk_o[r], vo_o[r] = swap_core(now(qk_m[r])), swap_core(now(vo_m[r]))
    attention = attend(1, attention)
    dn_m[1], dn_m[2] = swap_row(now(dn_m[0])), swap_col(now(dn_m[0]))
    attention = attend(2, attention)
    qk_o[3], vo_o[3] = swap_core(now(qk_m[3])), swap_core(now(vo_m[3]))
    attention = attend(3, attention)
    branch, normed_low, normed_t = first_norm(order, layer_input, attention, ln1_gain, ln1_bias, b_down)
    acts, slopes = [None] * 8, [None] * 8

    def expand(r, acc):
        acc, acts[2 * r], slopes[2 * r], acts[2 * r + 1], slopes[2 * r + 1] = ffn_fwd(
            order, normed_low, up_m[r], dn_m[r], up_o[r], dn_o[r], acc
        )
        return acc

    up_m[3] = swap_row(now(up_m[2]))
    up_o[1], up_o[2] = swap_core(now(up_m[1])), swap_core(now(up_m[2]))
    branch = expand(0, branch)
    dn_m[3] = swap_col(now(dn_m[1]))
    dn_o[1], dn_o[2] = swap_core(now(dn_m[1])), swap_core(now(dn_m[2]))
    branch = expand(1, branch)
    branch = expand(2, branch)
    up_o[3], dn_o[3] = swap_core(now(up_m[3])), swap_core(now(dn_m[3]))
    branch = expand(3, branch)
    d_normed, output, branch_low, branch_t, sums_two = second_norm(order, branch, cotangent, ln2_gain, ln2_bias)

    down, up, attn = Piece(order, odd, 0), Piece(order, odd, 16), Piece(order, odd, 16)
    d_up = [None] * 8

    def back(r, acc):
        acc, d_up[2 * r], d_up[2 * r + 1] = ffn_bwd(
            order, branch_low, up_m[r], dn_m[r], slopes[2 * r], up_o[r], dn_o[r], slopes[2 * r + 1], acc
        )
        return acc

    def down_other(r):
        down.other[r] = swap_core(outer(order, branch_t, acts[2 * r + 1], [], False, 0, "grad_down")[0])

    def down_mine(r, got=(), split=False, z=None):
        return outer(
            order, branch_t, acts[2 * r], [("whole", down.other[r]), *got], split, 0, "grad_down", z
        )

    def up_other(r):
        up.other[r] = swap_core(outer(order, normed_t, d_up[2 * r + 1], [], False, 16, "grad_up")[0])

    def up_mine(r, got=(), split=False, z=None):
        return outer(order, normed_t, d_up[2 * r], [("whole", up.other[r]), *got], split, 16, "grad_up", z)

    down_other(3)
    d_normed = back(3, d_normed)
    up_other(3)
    down.diagonal(*down_mine(3, split=True))
    down_other(1)
    up.diagonal(*up_mine(3, split=True))
    down_other(2)
    d_normed = back(1, d_normed)
    up_other(1)
    d_normed = back(2, d_normed)
    up_other(2)
    down_row = down_mine(1, [("bottom", down.bottom)])[0]
    down_col = down_mine(2, [("top", down.top)])[0]
    down.direct(down_row, down_col)
    d_normed = back(0, d_normed)
    down_other(0)
    up_other(0)
    grad_input, input_t, attention_low, grad_t, sums_one = first_back(
        order, layer_input, attention, ln1_gain, d_normed
    )

    def attend_back(r, other, acc, split=False):
        got = [] if other else [("whole", attn.other[r])]
        acc, *parts = attn_bwd(
            order,
            attention_low,
            grad_t,
            input_t,
            saved[r][0 + other],
            saved[r][2 + other],
            saved[r][4 + other],
            qk_o[r] if other else qk_m[r],
            vo_o[r] if other else vo_m[r],
            acc,
            got,
            split,
        )
        if other:
            attn.other[r] = swap_core(parts[0])
        else:
            attn.mine[r] = parts
        return acc

    small = jnp.concatenate([sums_one, sums_two], 0)
    grad_input = attend_back(3, True, grad_input)
    small = order.plain(jnp.add, swap_core(small), small)
    up_row = up_mine(1, [("bottom", up.bottom)])[0]
    up_col = up_mine(2, [("top", up.top)])[0]
    up.direct(up_row, up_col)
    grad_input = attend_back(1, True, grad_input)
    small_row = swap_row(small)
    grad_input = attend_back(3, False, grad_input, True)
    attn.diagonal(*attn.mine[3])
    small = order.plain(jnp.add, small_row, small)
    grad_input = attend_back(2, True, grad_input)
    small_col = swap_col(small)
    grad_input = attend_back(1, False, grad_input)
    small = order.plain(jnp.add, small_col, small)
    small_near = swap_near(small)
    down.along_z(*down_mine(0, [("whole", down.row_part), ("whole", down.col_part)], True, odd))
    grad_input = attend_back(0, True, grad_input)
    small = order.plain(jnp.add, small_near, small)
    small_far = swap_far(small)
    grad_input = attend_back(2, False, grad_input)
    down.second()
    grad_input = attend_back(0, False, grad_input)
    small = order.plain(jnp.add, small_far, small)
    up.along_z(*up_mine(0, [("whole", up.row_part), ("whole", up.col_part)], True, odd))
    attn.direct(*relay(order, attn.mine[1][0], attn.bottom, attn.mine[2][0], attn.top, 16))
    down.third()
    up.second()
    down.last()
    up.third()
    attn.along_z(*own_sum(order, odd, attn.mine[0][0], attn.row_part, attn.col_part))
    up.last()
    attn.second()
    attn.third()
    attn.last()

    half = width // 2

    def matrix(piece, columns=slice(None)):
        halves = piece.halves(first_core, is_odd)
        return jnp.concatenate(
            [jnp.concatenate([top[:half, columns], bot[:half, columns]], 0) for top, bot in halves], 1
        ).astype(F32)

    def bias_of(piece, columns=slice(None)):
        return jnp.concatenate([bot[half, columns] for _, bot in piece.halves(first_core, is_odd)]).astype(F32)

    grad_w_down = matrix(down).T
    grad_w_up = matrix(up)
    grad_b_up = bias_of(up)
    grad_w_qkv = jnp.stack([matrix(attn, slice(128 * i, 128 * i + 128)) for i in range(3)])
    grad_b_qv = jnp.stack([bias_of(attn, slice(0, 128)), bias_of(attn, slice(256, 384))])
    grad_w_out = matrix(attn, slice(384, 512)).T
    return (
        output,
        grad_input,
        grad_w_qkv,
        grad_b_qv,
        grad_w_out,
        small[2],
        small[0],
        small[1],
        grad_w_up,
        grad_b_up,
        grad_w_down,
        small[10],
        small[8],
        small[9],
    )


def local(*arrays):
    my_rows = arrays[0].shape[0]
    seq_len = arrays[1].shape[1]
    grid = (lax.axis_size("dp"), lax.axis_size("tensor"))
    if grid == (8, 4) and my_rows == seq_len and arrays[4].shape[0] == 4 * HEAD_DIM:
        return fast(*arrays)
    return general(*arrays)


def solution(mesh):
    return jax.shard_map(
        local,
        mesh=mesh,
        in_specs=(
            P(("dp", "tensor"), None),
            P("dp", None),
            P(None, None, "tensor"),
            P(None, "tensor"),
            P("tensor", None),
            P(),
            P(),
            P(),
            P(None, "tensor"),
            P("tensor"),
            P("tensor", None),
            P(),
            P(),
            P(),
            P(("dp", "tensor"), None),
        ),
        out_specs=(
            P(("dp", "tensor"), None),
            P(("dp", "tensor"), None),
            P(None, None, "tensor"),
            P(None, "tensor"),
            P("tensor", None),
            P(),
            P(),
            P(),
            P(None, "tensor"),
            P("tensor"),
            P("tensor", None),
            P(),
            P(),
            P(),
        ),
        check_vma=False,
    )
```

```python
import jax
import jax.numpy as jnp
from jax import lax
from jax.experimental import pallas as pl
from jax.experimental.pallas import tpu as pltpu
from jax.sharding import PartitionSpec as P

HEAD_DIM = 64


norm_epsilon = 1e-05
root_half = 0.7071067811865476
inverse_root_two_pi = 0.3989422804014327


def layer_norm(token_rows, norm_gain, norm_bias):
    row_mean = jnp.mean(token_rows, -1, keepdims=True)
    centered = token_rows - row_mean
    variance = jnp.mean(centered * centered, -1, keepdims=True)
    inv_std = lax.rsqrt(variance + norm_epsilon)
    scaled = centered * inv_std
    return (scaled * norm_gain + norm_bias, scaled, inv_std)


def norm_back(incoming, scaled, inv_std, norm_gain):
    weighted = incoming * norm_gain
    d_rows = inv_std * (
        weighted
        - jnp.mean(weighted, -1, keepdims=True)
        - scaled * jnp.mean(weighted * scaled, -1, keepdims=True)
    )
    return (d_rows, jnp.sum(incoming * scaled, 0), jnp.sum(incoming, 0))


def gelu_value(up_proj):
    return 0.5 * up_proj * (1.0 + lax.erf(up_proj * root_half))


def gelu_slope(up_proj):
    return (
        0.5 * (1.0 + lax.erf(up_proj * root_half))
        + up_proj * jnp.exp(-0.5 * up_proj * up_proj) * inverse_root_two_pi
    )


def split_heads(matrix, head_count):
    return matrix.reshape(matrix.shape[0], head_count, -1)


def project(token_rows, w_qkv, b_qv):
    queries = (
        jnp.dot(token_rows, w_qkv[0], preferred_element_type=jnp.float32)
        + b_qv[0].astype(jnp.float32)
    ).astype(jnp.bfloat16)
    keys_low = jnp.dot(token_rows, w_qkv[1], preferred_element_type=jnp.float32).astype(
        jnp.bfloat16
    )
    values = (
        jnp.dot(token_rows, w_qkv[2], preferred_element_type=jnp.float32)
        + b_qv[1].astype(jnp.float32)
    ).astype(jnp.bfloat16)
    return (queries, keys_low, values)


def scores(queries, keys_low, segment, head_count, score_scale):
    raw = jnp.einsum(
        "qhd,khd->hqk",
        split_heads(queries, head_count),
        split_heads(keys_low, head_count),
        preferred_element_type=jnp.float32,
    )
    same_doc = segment[:, None] == segment[None, :]
    return jnp.where(same_doc[None], raw * score_scale, -1e30)


def mix_values(prob_low, values, head_count):
    context = jnp.einsum(
        "hqk,khd->qhd",
        prob_low,
        split_heads(values, head_count),
        preferred_element_type=jnp.float32,
    )
    return context.reshape(context.shape[0], -1).astype(jnp.bfloat16)


def ffn_forward(normed_low, up_weight, up_bias, down_weight):
    up_proj = jnp.dot(normed_low, up_weight, preferred_element_type=jnp.float32) + up_bias.astype(
        jnp.float32
    )
    activation = gelu_value(up_proj).astype(jnp.bfloat16)
    return jnp.dot(activation, down_weight, preferred_element_type=jnp.float32)


def ffn_backward(normed_low, branch_low, up_weight, up_bias, down_weight):
    up_proj = jnp.dot(normed_low, up_weight, preferred_element_type=jnp.float32) + up_bias.astype(
        jnp.float32
    )
    activation = gelu_value(up_proj).astype(jnp.bfloat16)
    grad_down = jnp.einsum("tf,td->fd", activation, branch_low, preferred_element_type=jnp.float32)
    d_activation = jnp.einsum(
        "td,fd->tf", branch_low, down_weight, preferred_element_type=jnp.float32
    )
    d_up = (d_activation * gelu_slope(up_proj)).astype(jnp.bfloat16)
    grad_up = jnp.einsum("td,tf->df", normed_low, d_up, preferred_element_type=jnp.float32)
    grad_up_bias = jnp.sum(d_up.astype(jnp.float32), 0)
    return (grad_up, grad_up_bias, grad_down, d_up)


def general(
    layer_input,
    segment_ids,
    w_qkv,
    b_qv,
    w_out,
    b_out,
    ln1_gain,
    ln1_bias,
    w_up,
    b_up,
    w_down,
    b_down,
    ln2_gain,
    ln2_bias,
    cotangent,
):
    my_rows, model_width = layer_input.shape
    seq_len = segment_ids.shape[1]
    score_scale = HEAD_DIM ** (-0.5)
    whole_input = lax.all_gather(layer_input, "tensor", axis=0, tiled=True)
    seq_input = whole_input.reshape(segment_ids.shape[0], seq_len, model_width)
    attn_width = w_out.shape[0]
    head_count = attn_width // HEAD_DIM

    def forward_seq(running, seq_item):
        token_rows, segment = seq_item
        queries, keys_low, values = project(token_rows, w_qkv, b_qv)
        logits = scores(queries, keys_low, segment, head_count, score_scale)
        row_max = jnp.max(logits, -1, keepdims=True)
        exponent = jnp.exp(logits - row_max)
        expo_sum = jnp.sum(exponent, -1, keepdims=True)
        prob_low = (exponent / expo_sum).astype(jnp.bfloat16)
        return (running, (mix_values(prob_low, values, head_count), row_max + jnp.log(expo_sum)))

    _, (seq_context, seq_lse) = lax.scan(forward_seq, None, (seq_input, segment_ids))
    all_context = seq_context.reshape(-1, attn_width)
    attention = lax.psum_scatter(
        jnp.dot(all_context, w_out, preferred_element_type=jnp.float32),
        "tensor",
        scatter_dimension=0,
        tiled=True,
    ) + b_out.astype(jnp.float32)
    normed_one, scaled_one, inv_one = layer_norm(
        layer_input.astype(jnp.float32) + attention, ln1_gain, ln1_bias
    )
    normed_low = normed_one.astype(jnp.bfloat16)
    whole_normed = lax.all_gather(normed_low, "tensor", axis=0, tiled=True)
    branch = lax.psum_scatter(
        ffn_forward(whole_normed, w_up, b_up, w_down), "tensor", scatter_dimension=0, tiled=True
    )
    normed_two, scaled_two, inv_two = layer_norm(
        normed_one + branch + b_down.astype(jnp.float32), ln2_gain, ln2_bias
    )
    d_second, grad_ln2_gain, grad_ln2_bias = norm_back(
        cotangent.astype(jnp.float32), scaled_two, inv_two, ln2_gain
    )
    branch_low = d_second.astype(jnp.bfloat16)
    grad_b_down = jnp.sum(branch_low.astype(jnp.float32), 0)
    whole_branch = lax.all_gather(branch_low, "tensor", axis=0, tiled=True)
    grad_w_up, grad_b_up, grad_w_down, d_up = ffn_backward(
        whole_normed, whole_branch, w_up, b_up, w_down
    )
    d_normed = lax.psum_scatter(
        jnp.einsum("tf,df->td", d_up, w_up, preferred_element_type=jnp.float32),
        "tensor",
        scatter_dimension=0,
        tiled=True,
    )
    d_first, grad_ln1_gain, grad_ln1_bias = norm_back(
        d_second + d_normed, scaled_one, inv_one, ln1_gain
    )
    attention_low = d_first.astype(jnp.bfloat16)
    grad_b_out = jnp.sum(attention_low.astype(jnp.float32), 0)
    whole_grad = lax.all_gather(attention_low, "tensor", axis=0, tiled=True)
    seq_grad = whole_grad.reshape(seq_input.shape[0], seq_len, model_width)

    def backward_seq(running, seq_item):
        grad_qkv, grad_bias, grad_out = running
        token_rows, segment, seq_lse_one, grad_rows = seq_item
        queries, keys_low, values = project(token_rows, w_qkv, b_qv)
        logits = scores(queries, keys_low, segment, head_count, score_scale)
        probability = jnp.exp(logits - seq_lse_one)
        prob_low = probability.astype(jnp.bfloat16)
        context = mix_values(prob_low, values, head_count)
        grad_out = grad_out + jnp.einsum(
            "te,td->ed", context, grad_rows, preferred_element_type=jnp.float32
        )
        d_context = jnp.einsum(
            "td,ed->te", grad_rows, w_out, preferred_element_type=jnp.float32
        ).astype(jnp.bfloat16)
        d_heads = split_heads(d_context, head_count)
        d_prob = jnp.einsum(
            "qhd,khd->hqk",
            d_heads,
            split_heads(values, head_count),
            preferred_element_type=jnp.float32,
        )
        d_values = (
            jnp.einsum("hqk,qhd->khd", prob_low, d_heads, preferred_element_type=jnp.float32)
            .reshape(seq_len, -1)
            .astype(jnp.bfloat16)
        )
        inner_sum = jnp.sum(probability * d_prob, -1, keepdims=True)
        d_raw = (probability * (d_prob - inner_sum) * score_scale).astype(jnp.bfloat16)
        d_queries = (
            jnp.einsum(
                "hqk,khd->qhd",
                d_raw,
                split_heads(keys_low, head_count),
                preferred_element_type=jnp.float32,
            )
            .reshape(seq_len, -1)
            .astype(jnp.bfloat16)
        )
        d_keys = (
            jnp.einsum(
                "hqk,qhd->khd",
                d_raw,
                split_heads(queries, head_count),
                preferred_element_type=jnp.float32,
            )
            .reshape(seq_len, -1)
            .astype(jnp.bfloat16)
        )
        grad_qkv = grad_qkv + jnp.stack(
            [
                jnp.einsum("td,te->de", token_rows, gradient, preferred_element_type=jnp.float32)
                for gradient in (d_queries, d_keys, d_values)
            ]
        )
        grad_bias = grad_bias + jnp.stack(
            [jnp.sum(d_queries.astype(jnp.float32), 0), jnp.sum(d_values.astype(jnp.float32), 0)]
        )
        return ((grad_qkv, grad_bias, grad_out), (d_queries, d_keys, d_values))

    start_grads = (
        jnp.zeros((3, model_width, attn_width), jnp.float32),
        jnp.zeros((2, attn_width), jnp.float32),
        jnp.zeros((attn_width, model_width), jnp.float32),
    )
    (grad_w_qkv, grad_b_qv, grad_w_out), seq_d = lax.scan(
        backward_seq, start_grads, (seq_input, segment_ids, seq_lse, seq_grad)
    )
    all_d = [gradient.reshape(-1, attn_width) for gradient in seq_d]
    summed = jnp.zeros((my_rows * lax.axis_size("tensor"), model_width), jnp.float32)
    for which in range(3):
        piece = all_d[which]
        summed = summed + jnp.einsum(
            "te,de->td", piece, w_qkv[which], preferred_element_type=jnp.float32
        )
    grad_input = d_first + lax.psum_scatter(
        summed.astype(jnp.bfloat16), "tensor", scatter_dimension=0, tiled=True
    ).astype(jnp.float32)
    grad_w_qkv, grad_b_qv, grad_w_out, grad_w_up, grad_b_up, grad_w_down = (
        lax.psum(grad_w_qkv.astype(jnp.bfloat16), "dp").astype(jnp.float32),
        lax.psum(grad_b_qv.astype(jnp.bfloat16), "dp").astype(jnp.float32),
        lax.psum(grad_w_out.astype(jnp.bfloat16), "dp").astype(jnp.float32),
        lax.psum(grad_w_up.astype(jnp.bfloat16), "dp").astype(jnp.float32),
        lax.psum(grad_b_up.astype(jnp.bfloat16), "dp").astype(jnp.float32),
        lax.psum(grad_w_down.astype(jnp.bfloat16), "dp").astype(jnp.float32),
    )
    grad_b_out, grad_ln1_gain, grad_ln1_bias, grad_b_down, grad_ln2_gain, grad_ln2_bias = lax.psum(
        (grad_b_out, grad_ln1_gain, grad_ln1_bias, grad_b_down, grad_ln2_gain, grad_ln2_bias),
        ("dp", "tensor"),
    )
    return (
        normed_two.astype(jnp.bfloat16),
        grad_input,
        grad_w_qkv,
        grad_b_qv,
        grad_w_out,
        grad_b_out,
        grad_ln1_gain,
        grad_ln1_bias,
        grad_w_up,
        grad_b_up,
        grad_w_down,
        grad_b_down,
        grad_ln2_gain,
        grad_ln2_bias,
    )


F32 = jnp.float32
BF = jnp.bfloat16
LOG2E = 1.4426950408889634


def dotf(a, b, ca, cb):
    return lax.dot_general(a, b, (((ca,), (cb,)), ((), ())), preferred_element_type=F32)


class Order:
    def __init__(self):
        self.token, self.waited = None, []

    def wait(self, *values):
        self.waited.extend(values)

    def __call__(self, kernel, outs, args, name, limit, aliases=None, smem=0):
        count = len(args)
        specs = [pl.BlockSpec(memory_space=pltpu.SMEM)] * smem + [pl.BlockSpec()] * (count - smem)
        unread = ([] if self.token is None else [self.token]) + self.waited
        self.waited = []
        args = (*args, *unread)
        specs += [pl.BlockSpec(memory_space=pl.ANY)] * len(unread)

        def body(*refs):
            kernel(*refs[:count], *refs[len(args) :])

        result = pl.pallas_call(
            body,
            out_shape=tuple(jax.ShapeDtypeStruct(s, d) for s, d in outs),
            in_specs=specs,
            input_output_aliases=aliases or {},
            compiler_params=pltpu.CompilerParams(vmem_limit_bytes=limit << 20),
            cost_estimate=pl.CostEstimate(flops=1, bytes_accessed=1, transcendentals=0),
            name=name,
        )(*args)
        self.token = result[-1]
        return result

    def plain(self, fn, first, *rest):
        first, *_ = lax.optimization_barrier((first, self.token, *self.waited))
        self.waited = []
        out = lax.optimization_barrier(fn(first, *rest))
        self.token = out[-1] if isinstance(out, (tuple, list)) else out
        return out

    def now(self, value):
        return lax.optimization_barrier((value, self.token))[0]


def pack_attn_kernel(core, w_qkv, w_out, b_qv, qk, vo):
    width = w_qkv.shape[1]
    zero = jnp.zeros((16, 128), BF)
    first = lax.broadcasted_iota(jnp.int32, (16, 128), 0) == 0
    part = pl.ds(pl.multiple_of(core[0] * 128, 128), 128)
    qk[0:width, 0:128] = w_qkv[0, :, part]
    qk[0:width, 128:256] = w_qkv[1, :, part]
    vo[0:width, 0:128] = w_qkv[2, :, part]
    vo[0:width, 128:256] = w_out[part, :].astype(F32).T.astype(BF)
    qk[width : width + 16, 0:128] = jnp.where(first, b_qv[0:1, part].astype(F32), 0.0).astype(BF)
    vo[width : width + 16, 0:128] = jnp.where(first, b_qv[1:2, part].astype(F32), 0.0).astype(BF)
    qk[width : width + 16, 128:256] = zero
    vo[width : width + 16, 128:256] = zero


def pack_attn(order, core, w_qkv, w_out, b_qv):
    out = ((w_qkv.shape[1] + 16, 256), BF)
    return order(pack_attn_kernel, (out,) * 2, (core, w_qkv, w_out, b_qv), "pack_attn", 8, smem=1)


def pack_ffn_kernel(core, w_up, b_up, w_down, up, dn):
    width = w_up.shape[0]
    hid = w_up.shape[1] // 2
    first = lax.broadcasted_iota(jnp.int32, (16, hid), 0) == 0
    part = pl.ds(pl.multiple_of(core[0] * hid, hid), hid)
    up[0:width, :] = w_up[:, part]
    up[width : width + 16, :] = jnp.where(first, b_up[0:1, part].astype(F32), 0.0).astype(BF)
    dn[...] = w_down[part, :]


def pack_ffn(order, core, w_up, b_up, w_down):
    width, hid = w_up.shape[0], w_up.shape[1] // 2
    outs = (((width + 16, hid), BF), ((hid, width), BF))
    return order(pack_ffn_kernel, outs, (core, w_up, b_up, w_down), "pack_ffn", 12, smem=1)


def flip(order, matrix):
    width = matrix[0].shape[1]

    def kernel(*refs):
        start = 0
        for ref in refs[:-1]:
            rows = ref.shape[0]
            refs[-1][:, start : start + rows] = ref[...].astype(F32).T.astype(BF)
            start += rows

    rows = sum(m.shape[0] for m in matrix)
    return order(kernel, (((width, rows), BF),), tuple(matrix), "flip", 8)[0]


def take(refs, part):
    if len(refs) == 1:
        return refs[0][part, :]
    half = refs[0].shape[0]
    return refs[part.start // half][part.start % half : (part.stop - 1) % half + 1, :]


def whole(refs):
    return refs[0][...] if len(refs) == 1 else jnp.concatenate([r[...] for r in refs], 0)


def split_refs(refs, counts):
    out = []
    for count in counts:
        out.append(refs[:count])
        refs = refs[count:]
    return out


def attn_fwd(order, seqs, qk, vo, last=False):
    rows = sum(m.shape[0] for m in seqs[0][0])
    width = qk.shape[0] - 16
    counts, args, outs, aliases = [], [qk, vo], [], {}
    pt, qkv, ctx = ((2, rows, rows), BF), ((3, rows, 128), BF), ((rows, 128), BF)
    for x, mask, acc, low in seqs:
        counts += [len(x), 1, acc is not None]
        args += [*x, mask]
        if acc is not None:
            if not low:
                aliases[len(args)] = len(outs)
            args.append(acc)
        total = (((rows // 2, width), BF),) * 2 if low else (((rows, width), F32),)
        outs += [*total, pt, qkv, ctx]

    def kernel(qk, vo, *refs):
        ins = split_refs(refs[: sum(counts)], counts)
        results = refs[sum(counts) :]
        row = lax.broadcasted_iota(jnp.int32, (128, rows), 0)
        for index, (_, _, _, low) in enumerate(seqs):
            x_refs, (mask,), acc = ins[3 * index : 3 * index + 3]
            total_refs, results = results[: 1 + low], results[1 + low :]
            (pt, qkv, ctx_ref), results = results[:3], results[3:]
            x = whole(x_refs)
            qkf = dotf(x, qk[0:width, :], 1, 0) + qk[width : width + 16, :][0:1, :].astype(F32)
            vf = dotf(x, vo[0:width, 0:128], 1, 0) + vo[width : width + 16, 0:128][0:1, :].astype(F32)
            k = qkf[:, 128:].astype(BF)
            qkv[0] = qkf[:, :128].astype(BF)
            qkv[1] = k
            qkv[2] = vf.astype(BF)
            q_t = qkf[:, :128].T.astype(BF)
            v_t = vf.T.astype(BF)
            parts = []
            for h in range(2):
                q_h = jnp.where((row // HEAD_DIM) == h, q_t, jnp.zeros_like(q_t))
                s = dotf(k, q_h, 1, 0) * (HEAD_DIM**-0.5 * LOG2E) + mask[...]
                e = jnp.exp2(s - jnp.max(s, 0, keepdims=True))
                p = (e * (1.0 / jnp.sum(e, 0, keepdims=True))).astype(BF)
                pt[h] = p
                parts.append(dotf(v_t[h * HEAD_DIM : (h + 1) * HEAD_DIM, :], p, 1, 0))
            ctx = jnp.concatenate(parts, 0).T.astype(BF)
            ctx_ref[...] = ctx
            total = dotf(ctx, vo[0:width, 128:256], 1, 1)
            if acc:
                total = total + acc[0][...]
            if low:
                total_refs[0][...] = total[: rows // 2].astype(BF)
                total_refs[1][...] = total[rows // 2 :].astype(BF)
            else:
                total_refs[0][...] = total

    result = list(order(kernel, tuple(outs), tuple(args), "attn_fwd", 8, aliases))
    out = []
    for _, _, _, low in seqs:
        out.append((result[: 1 + low], result[1 + low : 4 + low]))
        result = result[4 + low :]
    return out


def part_rows(part, half, extra):
    whole = ((0, half), (half + extra, 2 * half + extra), (2 * half + extra, 2 * half + 2 * extra), (half, half + extra))
    own = ((0, half), (0, half), (half, half + extra), (half, half + extra))
    return whole[part], own[part]


def add_got(value, got, part, half, extra):
    whole, own = part_rows(part, half, extra)
    for kind, ref in got:
        if kind == "whole":
            value = value + ref[whole[0] : whole[1], :].astype(F32)
        elif (kind == "top") == (part == 0):
            value = value + ref[own[0] : own[1], :].astype(F32)
    return value


def put(outs, part, half, extra, value):
    whole, own = part_rows(part, half, extra)
    if len(outs) == 1:
        outs[0][whole[0] : whole[1], :] = value.astype(BF)
    else:
        outs[part in (1, 2)][own[0] : own[1], :] = value.astype(BF)


def gradient_shapes(width, columns, extra, split):
    if split:
        return (((width // 2 + extra, columns), BF),) * 2
    return (((width + 2 * extra, columns), BF),)


def outer(order, left_t, right, got, split, extra, name, odd=None):
    kinds = [kind for kind, _ in got]
    width = left_t[0].shape[0]
    half = width // 2

    def kernel(*refs):
        if odd is not None:
            flag, *refs = refs
        left_refs, right_refs, refs = refs[:2], refs[2:4], refs[4:]
        received = list(zip(kinds, refs))
        outs = refs[len(kinds) :]
        if odd is not None:
            swapped = flag[0] == 1
        values = []
        for part in (0, 1):
            piece = slice(part * half, (part + 1) * half)
            value = dotf(left_refs[0][piece, :], right_refs[0][...], 1, 0)
            value = value + dotf(left_refs[1][piece, :], right_refs[1][...], 1, 0)
            values.append(add_got(value, received, part, half, extra))
        if extra:
            first = lax.broadcasted_iota(jnp.int32, (extra, values[0].shape[1]), 0) == 0
            row = sum(jnp.sum(r[...].astype(F32), 0, keepdims=True) for r in right_refs)
            row = add_got(jnp.where(first, row, 0.0), received, 2, half, extra)
            zero = jnp.zeros(row.shape, F32)
        if odd is None:
            for part in (0, 1):
                put(outs, part, half, extra, values[part])
            if extra:
                put(outs, 2, half, extra, row)
                put(outs, 3, half, extra, zero)
        else:
            outs[0][0:half, :] = jnp.where(swapped, values[1], values[0]).astype(BF)
            outs[1][0:half, :] = jnp.where(swapped, values[0], values[1]).astype(BF)
            if extra:
                outs[0][half:, :] = jnp.where(swapped, row, zero).astype(BF)
                outs[1][half:, :] = jnp.where(swapped, zero, row).astype(BF)

    outs = gradient_shapes(width, right[0].shape[1], extra, split)
    flags = () if odd is None else (odd,)
    args = (*flags, *left_t, *right, *(v for _, v in got))
    return order(kernel, outs, args, name, 8, smem=len(flags))


def own_sum(order, odd, parts):
    half = parts[0][0].shape[0] // 2
    columns = sum(own.shape[1] for own, _, _ in parts)

    def kernel(flag, *refs):
        keep, send = refs[-2:]
        swapped = flag[0] == 1
        start = 0
        for i in range(0, len(refs) - 2, 3):
            total = sum(ref[...].astype(F32) for ref in refs[i : i + 3])
            stop = start + total.shape[1]
            keep[:, start:stop] = jnp.where(swapped, total[half:], total[:half]).astype(BF)
            send[:, start:stop] = jnp.where(swapped, total[:half], total[half:]).astype(BF)
            start = stop

    out = ((half, columns), BF)
    return order(kernel, (out, out), (odd, *(v for p in parts for v in p)), "own_sum", 10, smem=1)


def final_halves(core, odd, refs):
    keep, keep_o, got, got_o = refs
    second, swapped = core[0] == 1, odd[0] == 1

    def value(ref):
        return ref[...].astype(F32)

    out = []
    for a, b, c, d in ((keep, keep_o, got, got_o), (keep_o, keep, got_o, got)):
        kept = jnp.where(second, value(b), value(a))
        received = jnp.where(second, value(d), value(c))
        out.append((jnp.where(swapped, received, kept), jnp.where(swapped, kept, received)))
    return out


def finish_down(order, core, odd, refs):
    half, columns = refs[0].shape

    def kernel(core, odd, *refs):
        for i, pair in enumerate(final_halves(core, odd, refs[:4])):
            for j, value in enumerate(pair):
                refs[4][i * columns : (i + 1) * columns, j * half : (j + 1) * half] = value.T

    return order(kernel, (((2 * columns, 2 * half), F32),), (core, odd, *refs), "finish_down", 12, smem=2)[0]


def finish_up(order, core, odd, refs):
    half, columns = refs[0].shape
    half -= 16

    def kernel(core, odd, *refs):
        for i, pair in enumerate(final_halves(core, odd, refs[:4])):
            place = slice(i * columns, (i + 1) * columns)
            for j, value in enumerate(pair):
                refs[5][j * half : (j + 1) * half, place] = value[:half]
            refs[4][0:1, place] = pair[1][half : half + 1]

    outs = (((1, 2 * columns), F32), ((2 * half, 2 * columns), F32))
    return order(kernel, outs, (core, odd, *refs), "finish_up", 12, smem=2)


def finish_attn(order, core, odd, refs):
    half = refs[0].shape[0] - 16

    def kernel(core, odd, *refs):
        w_qkv, b_qv, w_out = refs[4:]
        for i, pair in enumerate(final_halves(core, odd, refs[:4])):
            place = slice(i * 128, (i + 1) * 128)
            for j, value in enumerate(pair):
                rows = slice(j * half, (j + 1) * half)
                for k in range(3):
                    w_qkv[k, rows, place] = value[:half, k * 128 : (k + 1) * 128]
                w_out[place, rows] = value[:half, 384:512].T
            b_qv[0:1, place] = pair[1][half : half + 1, 0:128]
            b_qv[1:2, place] = pair[1][half : half + 1, 256:384]

    outs = (((3, 2 * half, 256), F32), ((2, 256), F32), ((256, 2 * half), F32))
    return order(kernel, outs, (core, odd, *refs), "finish_attn", 12, smem=2)


def attn_bwd(order, seqs, qk, vo, low=False):
    width = qk.shape[0] - 16
    half = width // 2
    rows = seqs[0][1].shape[1]
    counts, args, outs, aliases = [], [qk, vo], [], {}
    for index, (g, gt, xt, pt, qkv, ctx, acc) in enumerate(seqs):
        counts += [len(g), 1, 1, 1, 1, 1, acc is not None]
        args += [*g, gt, xt, pt, qkv, ctx]
        down = low and index == 1
        if acc is not None:
            if not down:
                aliases[len(args)] = len(outs)
            args.append(acc)
        outs.append(((rows, width), BF if down else F32))

    def kernel(qk, vo, *refs):
        ins = split_refs(refs[: sum(counts)], counts)
        totals, outs = refs[sum(counts) : sum(counts) + 2], refs[sum(counts) + 2 :]
        row = lax.broadcasted_iota(jnp.int32, (128, rows), 0)
        lane = lax.broadcasted_iota(jnp.int32, (rows, 128), 1)
        first = lax.broadcasted_iota(jnp.int32, (16, 256), 0) == 0
        dqks, dvs_all, ctxs = [], [], []
        for index in (0, 1):
            g, _, _, (pt_ref,), (qkv_ref,), (ctx_ref,), acc = ins[7 * index : 7 * index + 7]
            ctx = ctx_ref[...]
            d_o = dotf(whole(g), vo[0:width, 128:256], 1, 0).astype(BF)
            d_ot = d_o.astype(F32).T
            prod = d_ot * ctx.astype(F32).T * (HEAD_DIM**-0.5)
            d_ot = (d_ot * (HEAD_DIM**-0.5)).astype(BF)
            k_t = qkv_ref[1].astype(F32).T.astype(BF)
            dvs, dks, dqs = [], [], []
            for h in range(2):
                head = slice(h * HEAD_DIM, (h + 1) * HEAD_DIM)
                inner = jnp.sum(prod[head, :], 0, keepdims=True)
                p = pt_ref[h]
                dvs.append(dotf(p, d_o, 1, 0))
                d_h = jnp.where((row // HEAD_DIM) == h, d_ot, jnp.zeros_like(d_ot))
                ds = (p.astype(F32) * (dotf(qkv_ref[2], d_h, 1, 0) - inner)).astype(BF)
                dks.append(dotf(ds, qkv_ref[0], 1, 0))
                dqs.append(dotf(k_t[head, :], ds, 1, 0))
            dv = jnp.where(lane < HEAD_DIM, dvs[0], dvs[1]).astype(BF)
            dk = jnp.where(lane < HEAD_DIM, dks[0], dks[1]).astype(BF)
            dq = jnp.concatenate(dqs, 0).T.astype(BF)
            dqk = jnp.concatenate([dq, dk], 1)
            total = dotf(dqk, qk[0:width, :], 1, 1) + dotf(dv, vo[0:width, 0:128], 1, 1)
            if acc:
                total = total + acc[0][...]
            totals[index][...] = total.astype(totals[index].dtype)
            dqks.append(dqk)
            dvs_all.append(dv)
            ctxs.append(ctx)

        def both(place, rights, piece):
            return sum(dotf(ins[7 * i + place][0][piece, :], rights[i], 1, 0) for i in (0, 1))

        def column_sums(values):
            return sum(jnp.sum(v.astype(F32), 0, keepdims=True) for v in values)

        sums = [column_sums(dqks), jnp.concatenate([column_sums(dvs_all), jnp.zeros((1, 128), F32)], 1)]
        for index in (0, 1):
            out = outs[index : index + 1]
            for part in (0, 1):
                piece = slice(part * half, (part + 1) * half)
                if index == 0:
                    value = both(2, dqks, piece)
                else:
                    value = jnp.concatenate([both(2, dvs_all, piece), both(1, ctxs, piece)], 1)
                put(out, part, half, 16, value)
            put(out, 2, half, 16, jnp.where(first, sums[index], 0.0))
            put(out, 3, half, 16, jnp.zeros((16, 256), F32))

    outs += [*gradient_shapes(width, 256, 16, False) * 2]
    return order(kernel, tuple(outs), tuple(args), "attn_bwd", 8, aliases)


def ffn_fwd(order, seqs, up, dn, low=False):
    width = dn.shape[1]
    counts, args, outs, aliases = [], [up, dn], [], {}
    rows = sum(m.shape[0] for m in seqs[0][0])
    mid = ((rows, dn.shape[0]), BF)
    for n, acc in seqs:
        counts += [len(n), acc is not None]
        args += n
        if acc is not None:
            if not low:
                aliases[len(args)] = len(outs)
            args.append(acc)
        outs += [*((((rows // 2, width), BF),) * 2 if low else (((rows, width), F32),)), mid, mid]

    def kernel(up, dn, *refs):
        ins = split_refs(refs[: sum(counts)], counts)
        results = refs[sum(counts) :]
        for index in range(len(seqs)):
            n_refs, acc = ins[2 * index : 2 * index + 2]
            total_refs, results = results[: 1 + low], results[1 + low :]
            (act_ref, slope_ref), results = results[:2], results[2:]
            for i in (0, 1):
                part = slice(i * (rows // 2), (i + 1) * (rows // 2))
                u = dotf(take(n_refs, part), up[0:width, :], 1, 0) + up[width : width + 16, :][0:1, :].astype(F32)
                cdf = 0.5 + 0.5 * lax.erf(u * root_half)
                act = (u * cdf).astype(BF)
                act_ref[part, :] = act
                slope = cdf + u * (jnp.exp2(u * u * (-0.5 * LOG2E)) * inverse_root_two_pi)
                slope_ref[part, :] = slope.astype(BF)
                total = dotf(act, dn[...], 1, 0)
                if acc:
                    total = total + acc[0][part, :]
                if low:
                    total_refs[i][...] = total.astype(BF)
                else:
                    total_refs[0][part, :] = total

    result = list(order(kernel, tuple(outs), tuple(args), "ffn_fwd", 8, aliases))
    out = []
    for _ in seqs:
        out.append((result[: 1 + low], result[1 + low : 3 + low]))
        result = result[3 + low :]
    return out


def ffn_bwd(order, seqs, up, dn, low=False):
    width = dn.shape[1]
    counts, args, outs, aliases = [], [up, dn], [], {}
    rows = seqs[0][1].shape[0]
    for g, slope, acc in seqs:
        counts += [len(g), 1, acc is not None]
        args += [*g, slope]
        if acc is not None:
            if not low:
                aliases[len(args)] = len(outs)
            args.append(acc)
        outs += [*((((rows // 2, width), BF),) * 2 if low else (((rows, width), F32),)), (slope.shape, BF)]

    def kernel(up, dn, *refs):
        ins = split_refs(refs[: sum(counts)], counts)
        results = refs[sum(counts) :]
        for index in range(len(seqs)):
            g, (slope,), acc = ins[3 * index : 3 * index + 3]
            total_refs, results = results[: 1 + low], results[1 + low :]
            d_ref, *results = results
            d_up = (dotf(whole(g), dn[...], 1, 1) * slope[...].astype(F32)).astype(BF)
            d_ref[...] = d_up
            total = dotf(d_up, up[0:width, :], 1, 1)
            if acc:
                total = total + acc[0][...]
            if low:
                total_refs[0][...] = total[: rows // 2].astype(BF)
                total_refs[1][...] = total[rows // 2 :].astype(BF)
            else:
                total_refs[0][...] = total

    result = list(order(kernel, tuple(outs), tuple(args), "ffn_bwd", 8, aliases))
    out = []
    for _ in seqs:
        out.append((result[: 1 + low], result[1 + low]))
        result = result[2 + low :]
    return out


def standard(v):
    centered = v - jnp.mean(v, -1, keepdims=True)
    inv = lax.rsqrt(jnp.mean(centered * centered, -1, keepdims=True) + norm_epsilon)
    return centered * inv, inv


def back_through(g, scaled, inv, gain):
    e = g * gain
    return inv * (e - jnp.mean(e, -1, keepdims=True) - scaled * jnp.mean(e * scaled, -1, keepdims=True))


def half_of(refs, i):
    per = refs[0].shape[0] // 128
    return refs[i // per][(i % per) * 128 : (i % per + 1) * 128, :]


def first_norm(order, x, acc, got, b_out, gain, bias, b_down):
    rows, width = x.shape

    def kernel(x_ref, acc_ref, got_a, got_b, b_out, gain, bias, b_down, sum_ref, out_ref, low_a, low_b, low_t):
        for i in range(rows // 128):
            part = slice(i * 128, (i + 1) * 128)
            total = x_ref[part, :].astype(F32) + b_out[...].astype(F32)
            total = total + acc_ref[part, :] + half_of((got_a, got_b), i).astype(F32)
            sum_ref[part, :] = total
            scaled, _ = standard(total)
            normed = scaled * gain[...] + bias[...]
            out_ref[part, :] = normed + b_down[...].astype(F32)
            low = normed.astype(BF)
            place = (i * 128) % (rows // 2)
            (low_a, low_b)[i * 256 // rows][place : place + 128, :] = low
            low_t[:, part] = low.astype(F32).T.astype(BF)

    half = ((rows // 2, width), BF)
    outs = (((rows, width), F32), ((rows, width), F32), half, half, ((width, rows), BF))
    args = (x, acc, *got, b_out[None], gain[None], bias[None], b_down[None])
    return order(kernel, outs, args, "first_norm", 14, {1: 0})


def emit_back(i, carry, g, scaled, inv, gain, out_ref, low_halves, low_t):
    part = slice(i * 128, (i + 1) * 128)
    d_rows = back_through(g, scaled, inv, gain)
    out_ref[part, :] = d_rows
    low = d_rows.astype(BF)
    half = low_halves[0].shape[0]
    place = (i * 128) % half
    low_halves[i * 128 // half][place : place + 128, :] = low
    low = low.astype(F32)
    low_t[:, part] = low.T.astype(BF)
    terms = (g * scaled, g, low)
    return tuple(c + jnp.sum(t, 0, keepdims=True) for c, t in zip(carry, terms))


def put_sums(sums_ref, carry):
    row = lax.broadcasted_iota(jnp.int32, sums_ref.shape, 0)
    sums_ref[...] = jnp.where(row == 0, carry[0], jnp.where(row == 1, carry[1], jnp.where(row == 2, carry[2], 0.0)))


def back_outs(rows, width):
    half = ((rows // 2, width), BF)
    return (((rows, width), F32), half, half, ((width, rows), BF), ((8, width), F32))


def second_norm(order, total, got, cotangent, gain, bias):
    rows, width = total.shape

    def kernel(sum_ref, got_a, got_b, cot_ref, gain, bias, d_ref, low_a, low_b, low_t, sums_ref, y_ref):
        carry = (jnp.zeros((1, width), F32),) * 3
        for i in range(rows // 128):
            part = slice(i * 128, (i + 1) * 128)
            scaled, inv = standard(sum_ref[part, :] + half_of((got_a, got_b), i).astype(F32))
            y_ref[part, :] = (scaled * gain[...] + bias[...]).astype(BF)
            g = cot_ref[part, :].astype(F32)
            carry = emit_back(i, carry, g, scaled, inv, gain[...], d_ref, (low_a, low_b), low_t)
        put_sums(sums_ref, carry)

    outs = (*back_outs(rows, width), ((rows, width), BF))
    return order(kernel, outs, (total, *got, cotangent, gain[None], bias[None]), "second_norm", 14, {0: 0})


def first_back(order, first, gain, d_normed, got):
    rows, width = first.shape

    def kernel(sum_ref, gain, d_ref, got_a, got_b, out_ref, low_a, low_b, low_t, sums_ref):
        carry = (jnp.zeros((1, width), F32),) * 3
        for i in range(rows // 128):
            part = slice(i * 128, (i + 1) * 128)
            scaled, inv = standard(sum_ref[part, :])
            g = d_ref[part, :] + half_of((got_a, got_b), i).astype(F32)
            carry = emit_back(i, carry, g, scaled, inv, gain[...], out_ref, (low_a, low_b), low_t)
        put_sums(sums_ref, carry)

    return order(kernel, back_outs(rows, width), (first, gain[None], d_normed, *got), "first_back", 14, {2: 0})

CORE = [(d, d ^ 1) for d in range(8)]
ROW = [(t, t ^ 1) for t in range(4)]
COL = [(t, t ^ 2) for t in range(4)]
NEAR = [(d, d ^ 2) for d in range(8)]
FAR = [(d, d ^ 4) for d in range(8)]


def swap_core(v):
    return lax.ppermute(v, "dp", CORE)


def swap_row(v):
    return lax.ppermute(v, "tensor", ROW)


def swap_col(v):
    return lax.ppermute(v, "tensor", COL)


def swap_near(v):
    return lax.ppermute(v, "dp", NEAR)


def swap_far(v):
    return lax.ppermute(v, "dp", FAR)


def add_low(a, b):
    return (a.astype(F32) + b.astype(F32)).astype(BF)


class Piece:
    def __init__(self, order, odd):
        self.order, self.odd = order, odd
        self.mine = [None] * 4

    def diagonal(self, top, bottom):
        self.top, self.bottom = swap_row(top), swap_col(bottom)

    def direct(self, row_part, col_part):
        self.row_part, self.col_part = swap_row(row_part), swap_col(col_part)

    def along_z(self, keep, send):
        self.keep, self.got = keep, swap_near(send)

    def second(self):
        self.keep = self.order.plain(add_low, self.got, self.keep)
        self.got = swap_far(self.keep)

    def third(self):
        self.keep = self.order.plain(add_low, self.got, self.keep)
        self.got = swap_near(self.keep)

    def kept(self):
        self.keep_o = swap_core(self.order.now(self.keep))

    def last(self):
        self.got_o = swap_core(self.order.now(self.got))

    def all(self):
        return self.keep, self.keep_o, self.got, self.got_o


def fast(
    layer_input,
    segment_ids,
    w_qkv,
    b_qv,
    w_out,
    b_out,
    ln1_gain,
    ln1_bias,
    w_up,
    b_up,
    w_down,
    b_down,
    ln2_gain,
    ln2_bias,
    cotangent,
):
    rows, width = layer_input.shape
    hidden = w_up.shape[1] // 2
    core = lax.axis_index("dp") % 2
    odd_index = (lax.axis_index("dp") // 2) % 2
    odd = odd_index.astype(jnp.int32)[None]
    core = core.astype(jnp.int32)[None]
    order = Order()
    now, wait = order.now, order.wait

    segment = lax.dynamic_index_in_dim(segment_ids, lax.axis_index("tensor"), keepdims=False)
    inputs = ((layer_input,), (swap_core(layer_input),))
    qk, vo, up_w, dn_w = [None] * 4, [None] * 4, [None] * 4, [None] * 4
    qk[0], vo[0] = pack_attn(order, core, w_qkv, w_out, b_qv)
    qk[1], qk[2] = swap_row(qk[0]), swap_col(qk[0])
    vo[1], vo[2] = swap_row(vo[0]), swap_col(vo[0])
    up_w[0], dn_w[0] = pack_ffn(order, core, w_up, b_up[None], w_down)

    masks = [
        jnp.where(ids[:, None] == ids[None, :], 0.0, -1e30).astype(F32) for ids in (segment, swap_core(segment))
    ]
    total = [None, None]
    saved = [[None, None] for _ in range(4)]

    def attend(r, which, low=False):
        found = attn_fwd(order, [(inputs[s], masks[s], total[s], low) for s in which], qk[r], vo[r])
        for s, (total[s], saved[r][s]) in zip(which, found):
            total[s] = total[s] if low else total[s][0]

    attend(0, (0, 1))
    up_w[1], up_w[2] = swap_row(now(up_w[0])), swap_col(now(up_w[0]))
    qk[3], vo[3] = swap_row(now(qk[2])), swap_col(now(vo[1]))
    attend(1, (0, 1))
    attend(2, (0, 1))
    attend(3, (1,), True)
    got = [swap_core(v) for v in total[1]]
    attend(3, (0,))
    wait(up_w[1], up_w[2])
    first, branch, *low, normed_t = first_norm(
        order, layer_input, total[0], got, b_out, ln1_gain, ln1_bias, b_down
    )
    dn_w[1], dn_w[2] = swap_row(now(dn_w[0])), swap_col(now(dn_w[0]))
    normed = (tuple(low), tuple(swap_core(v) for v in low))
    total = [branch, None]
    acts = [[None, None] for _ in range(4)]
    slopes = [[None, None] for _ in range(4)]

    def expand(r, which, low=False):
        found = ffn_fwd(order, [(normed[s], total[s]) for s in which], up_w[r], dn_w[r], low)
        for s, (total[s], (acts[r][s], slopes[r][s])) in zip(which, found):
            total[s] = total[s] if low else total[s][0]

    expand(0, (0,))
    expand(0, (1,))
    wait(dn_w[1], dn_w[2])
    normed_t = (normed_t, flip(order, normed[1]))
    up_w[3], dn_w[3] = swap_row(now(up_w[2])), swap_col(now(dn_w[1]))
    expand(1, (0, 1))
    expand(2, (0, 1))
    expand(3, (1,), True)
    got = [swap_core(v) for v in total[1]]
    expand(3, (0,))
    d_second, *low, branch_t, sums_two, output = second_norm(order, total[0], got, cotangent, ln2_gain, ln2_bias)
    branch_low = (tuple(low), tuple(swap_core(v) for v in low))

    down, up = Piece(order, odd), Piece(order, odd)
    attn, attn_qk, attn_vo = Piece(order, odd), Piece(order, odd), Piece(order, odd)
    total = [d_second, None]
    d_up = [[None, None] for _ in range(4)]

    def back(r, which, low=False):
        found = ffn_bwd(order, [(branch_low[s], slopes[r][s], total[s]) for s in which], up_w[r], dn_w[r], low)
        for s, (total[s], d_up[r][s]) in zip(which, found):
            total[s] = total[s] if low else total[s][0]

    def grad_down(r, got=(), split=False, z=None):
        return outer(order, branch_t, acts[r], got, split, 0, "grad_down", z)

    def grad_up(r, got=(), split=False, z=None):
        return outer(order, normed_t, d_up[r], got, split, 16, "grad_up", z)

    back(3, (0,))
    branch_t = (branch_t, flip(order, branch_low[1]))
    down.diagonal(*grad_down(3, split=True))
    back(3, (1,))
    up.diagonal(*grad_up(3, split=True))
    back(1, (0, 1))
    back(2, (0, 1))
    down_row = grad_down(1, [("bottom", down.bottom)])[0]
    down_col = grad_down(2, [("top", down.top)])[0]
    down.direct(down_row, down_col)
    back(0, (1,), True)
    got = [swap_core(v) for v in total[1]]
    back(0, (0,))
    d_first, *low, attention_t, sums_one = first_back(order, first, ln1_gain, total[0], got)
    attention_low = (tuple(low), tuple(swap_core(v) for v in low))
    inputs_t = [flip(order, inputs[s]) for s in (0, 1)]
    attention_t = (attention_t, flip(order, attention_low[1]))
    total = [d_first, None]

    def attend_back(r, low=False):
        seqs = [
            (attention_low[s], attention_t[s], inputs_t[s], *saved[r][s], total[s]) for s in (0, 1)
        ]
        total[0], total[1], attn_qk.mine[r], attn_vo.mine[r] = attn_bwd(order, seqs, qk[r], vo[r], low)

    down.along_z(*grad_down(0, [("whole", down.row_part), ("whole", down.col_part)], True, odd))
    up_row = grad_up(1, [("bottom", up.bottom)])[0]
    up_col = grad_up(2, [("top", up.top)])[0]
    up.direct(up_row, up_col)
    down.second()
    attend_back(3)
    qk_diag, vo_diag = swap_row(attn_qk.mine[3]), swap_col(attn_vo.mine[3])
    attend_back(1)
    attend_back(2)
    down.third()
    attend_back(0, True)
    qk_col = swap_col(order.plain(add_low, qk_diag, attn_qk.mine[2]))
    vo_row = swap_row(order.plain(add_low, vo_diag, attn_vo.mine[1]))
    wait(down.got)
    up.along_z(*grad_up(0, [("whole", up.row_part), ("whole", up.col_part)], True, odd))
    qk_row, vo_col = swap_row(now(attn_qk.mine[1])), swap_col(now(attn_vo.mine[2]))
    up.second()
    attn.along_z(
        *own_sum(order, odd, [(attn_qk.mine[0], qk_row, qk_col), (attn_vo.mine[0], vo_row, vo_col)])
    )
    small = jnp.concatenate([sums_one, sums_two], 0)
    small = order.plain(jnp.add, swap_core(now(small)), small)
    small = order.plain(jnp.add, swap_row(small), small)
    small = order.plain(jnp.add, swap_col(small), small)
    small_near = swap_near(small)
    up.third()
    small = order.plain(jnp.add, small_near, small)
    attn.second()
    small_far = swap_far(small)
    down.kept()
    down.last()
    got = swap_core(now(total[1]))
    grad_w_down = finish_down(order, core, odd, down.all())
    grad_input = order.plain(lambda a, b: a.astype(F32) + b, got, total[0])
    small = order.plain(jnp.add, small_far, small)
    wait(up.got)
    attn.third()
    attn.kept()
    up.kept()
    up.last()
    grad_b_up, grad_w_up = finish_up(order, core, odd, up.all())
    attn.last()
    grad_w_qkv, grad_b_qv, grad_w_out = finish_attn(order, core, odd, attn.all())
    return (
        output,
        grad_input,
        grad_w_qkv,
        grad_b_qv,
        grad_w_out,
        small[2],
        small[0],
        small[1],
        grad_w_up,
        grad_b_up[0],
        grad_w_down,
        small[10],
        small[8],
        small[9],
    )


def local(*arrays):
    my_rows = arrays[0].shape[0]
    seq_len = arrays[1].shape[1]
    grid = (lax.axis_size("dp"), lax.axis_size("tensor"))
    if grid == (8, 4) and my_rows == seq_len and arrays[4].shape[0] == 4 * HEAD_DIM:
        return fast(*arrays)
    return general(*arrays)


def solution(mesh):
    return jax.shard_map(
        local,
        mesh=mesh,
        in_specs=(
            P(("dp", "tensor"), None),
            P("dp", None),
            P(None, None, "tensor"),
            P(None, "tensor"),
            P("tensor", None),
            P(),
            P(),
            P(),
            P(None, "tensor"),
            P("tensor"),
            P("tensor", None),
            P(),
            P(),
            P(),
            P(("dp", "tensor"), None),
        ),
        out_specs=(
            P(("dp", "tensor"), None),
            P(("dp", "tensor"), None),
            P(None, None, "tensor"),
            P(None, "tensor"),
            P("tensor", None),
            P(),
            P(),
            P(),
            P(None, "tensor"),
            P("tensor"),
            P("tensor", None),
            P(),
            P(),
            P(),
        ),
        check_vma=False,
    )
```

```python
import jax
import jax.numpy as jnp
from jax import lax
from jax.experimental import pallas as pl
from jax.experimental.pallas import tpu as pltpu
from jax.sharding import PartitionSpec as P

HEAD_DIM = 64


norm_epsilon = 1e-05
root_half = 0.7071067811865476
inverse_root_two_pi = 0.3989422804014327


def layer_norm(token_rows, norm_gain, norm_bias):
    row_mean = jnp.mean(token_rows, -1, keepdims=True)
    centered = token_rows - row_mean
    variance = jnp.mean(centered * centered, -1, keepdims=True)
    inv_std = lax.rsqrt(variance + norm_epsilon)
    scaled = centered * inv_std
    return (scaled * norm_gain + norm_bias, scaled, inv_std)


def norm_back(incoming, scaled, inv_std, norm_gain):
    weighted = incoming * norm_gain
    d_rows = inv_std * (
        weighted
        - jnp.mean(weighted, -1, keepdims=True)
        - scaled * jnp.mean(weighted * scaled, -1, keepdims=True)
    )
    return (d_rows, jnp.sum(incoming * scaled, 0), jnp.sum(incoming, 0))


def gelu_value(up_proj):
    return 0.5 * up_proj * (1.0 + lax.erf(up_proj * root_half))


def gelu_slope(up_proj):
    return (
        0.5 * (1.0 + lax.erf(up_proj * root_half))
        + up_proj * jnp.exp(-0.5 * up_proj * up_proj) * inverse_root_two_pi
    )


def split_heads(matrix, head_count):
    return matrix.reshape(matrix.shape[0], head_count, -1)


def project(token_rows, w_qkv, b_qv):
    queries = (
        jnp.dot(token_rows, w_qkv[0], preferred_element_type=jnp.float32)
        + b_qv[0].astype(jnp.float32)
    ).astype(jnp.bfloat16)
    keys_low = jnp.dot(token_rows, w_qkv[1], preferred_element_type=jnp.float32).astype(
        jnp.bfloat16
    )
    values = (
        jnp.dot(token_rows, w_qkv[2], preferred_element_type=jnp.float32)
        + b_qv[1].astype(jnp.float32)
    ).astype(jnp.bfloat16)
    return (queries, keys_low, values)


def scores(queries, keys_low, segment, head_count, score_scale):
    raw = jnp.einsum(
        "qhd,khd->hqk",
        split_heads(queries, head_count),
        split_heads(keys_low, head_count),
        preferred_element_type=jnp.float32,
    )
    same_doc = segment[:, None] == segment[None, :]
    return jnp.where(same_doc[None], raw * score_scale, -1e30)


def mix_values(prob_low, values, head_count):
    context = jnp.einsum(
        "hqk,khd->qhd",
        prob_low,
        split_heads(values, head_count),
        preferred_element_type=jnp.float32,
    )
    return context.reshape(context.shape[0], -1).astype(jnp.bfloat16)


def ffn_forward(normed_low, up_weight, up_bias, down_weight):
    up_proj = jnp.dot(normed_low, up_weight, preferred_element_type=jnp.float32) + up_bias.astype(
        jnp.float32
    )
    activation = gelu_value(up_proj).astype(jnp.bfloat16)
    return jnp.dot(activation, down_weight, preferred_element_type=jnp.float32)


def ffn_backward(normed_low, branch_low, up_weight, up_bias, down_weight):
    up_proj = jnp.dot(normed_low, up_weight, preferred_element_type=jnp.float32) + up_bias.astype(
        jnp.float32
    )
    activation = gelu_value(up_proj).astype(jnp.bfloat16)
    grad_down = jnp.einsum("tf,td->fd", activation, branch_low, preferred_element_type=jnp.float32)
    d_activation = jnp.einsum(
        "td,fd->tf", branch_low, down_weight, preferred_element_type=jnp.float32
    )
    d_up = (d_activation * gelu_slope(up_proj)).astype(jnp.bfloat16)
    grad_up = jnp.einsum("td,tf->df", normed_low, d_up, preferred_element_type=jnp.float32)
    grad_up_bias = jnp.sum(d_up.astype(jnp.float32), 0)
    return (grad_up, grad_up_bias, grad_down, d_up)


def general(
    layer_input,
    segment_ids,
    w_qkv,
    b_qv,
    w_out,
    b_out,
    ln1_gain,
    ln1_bias,
    w_up,
    b_up,
    w_down,
    b_down,
    ln2_gain,
    ln2_bias,
    cotangent,
):
    my_rows, model_width = layer_input.shape
    seq_len = segment_ids.shape[1]
    score_scale = HEAD_DIM ** (-0.5)
    whole_input = lax.all_gather(layer_input, "tensor", axis=0, tiled=True)
    seq_input = whole_input.reshape(segment_ids.shape[0], seq_len, model_width)
    attn_width = w_out.shape[0]
    head_count = attn_width // HEAD_DIM

    def forward_seq(running, seq_item):
        token_rows, segment = seq_item
        queries, keys_low, values = project(token_rows, w_qkv, b_qv)
        logits = scores(queries, keys_low, segment, head_count, score_scale)
        row_max = jnp.max(logits, -1, keepdims=True)
        exponent = jnp.exp(logits - row_max)
        expo_sum = jnp.sum(exponent, -1, keepdims=True)
        prob_low = (exponent / expo_sum).astype(jnp.bfloat16)
        return (running, (mix_values(prob_low, values, head_count), row_max + jnp.log(expo_sum)))

    _, (seq_context, seq_lse) = lax.scan(forward_seq, None, (seq_input, segment_ids))
    all_context = seq_context.reshape(-1, attn_width)
    attention = lax.psum_scatter(
        jnp.dot(all_context, w_out, preferred_element_type=jnp.float32),
        "tensor",
        scatter_dimension=0,
        tiled=True,
    ) + b_out.astype(jnp.float32)
    normed_one, scaled_one, inv_one = layer_norm(
        layer_input.astype(jnp.float32) + attention, ln1_gain, ln1_bias
    )
    normed_low = normed_one.astype(jnp.bfloat16)
    whole_normed = lax.all_gather(normed_low, "tensor", axis=0, tiled=True)
    branch = lax.psum_scatter(
        ffn_forward(whole_normed, w_up, b_up, w_down), "tensor", scatter_dimension=0, tiled=True
    )
    normed_two, scaled_two, inv_two = layer_norm(
        normed_one + branch + b_down.astype(jnp.float32), ln2_gain, ln2_bias
    )
    d_second, grad_ln2_gain, grad_ln2_bias = norm_back(
        cotangent.astype(jnp.float32), scaled_two, inv_two, ln2_gain
    )
    branch_low = d_second.astype(jnp.bfloat16)
    grad_b_down = jnp.sum(branch_low.astype(jnp.float32), 0)
    whole_branch = lax.all_gather(branch_low, "tensor", axis=0, tiled=True)
    grad_w_up, grad_b_up, grad_w_down, d_up = ffn_backward(
        whole_normed, whole_branch, w_up, b_up, w_down
    )
    d_normed = lax.psum_scatter(
        jnp.einsum("tf,df->td", d_up, w_up, preferred_element_type=jnp.float32),
        "tensor",
        scatter_dimension=0,
        tiled=True,
    )
    d_first, grad_ln1_gain, grad_ln1_bias = norm_back(
        d_second + d_normed, scaled_one, inv_one, ln1_gain
    )
    attention_low = d_first.astype(jnp.bfloat16)
    grad_b_out = jnp.sum(attention_low.astype(jnp.float32), 0)
    whole_grad = lax.all_gather(attention_low, "tensor", axis=0, tiled=True)
    seq_grad = whole_grad.reshape(seq_input.shape[0], seq_len, model_width)

    def backward_seq(running, seq_item):
        grad_qkv, grad_bias, grad_out = running
        token_rows, segment, seq_lse_one, grad_rows = seq_item
        queries, keys_low, values = project(token_rows, w_qkv, b_qv)
        logits = scores(queries, keys_low, segment, head_count, score_scale)
        probability = jnp.exp(logits - seq_lse_one)
        prob_low = probability.astype(jnp.bfloat16)
        context = mix_values(prob_low, values, head_count)
        grad_out = grad_out + jnp.einsum(
            "te,td->ed", context, grad_rows, preferred_element_type=jnp.float32
        )
        d_context = jnp.einsum(
            "td,ed->te", grad_rows, w_out, preferred_element_type=jnp.float32
        ).astype(jnp.bfloat16)
        d_heads = split_heads(d_context, head_count)
        d_prob = jnp.einsum(
            "qhd,khd->hqk",
            d_heads,
            split_heads(values, head_count),
            preferred_element_type=jnp.float32,
        )
        d_values = (
            jnp.einsum("hqk,qhd->khd", prob_low, d_heads, preferred_element_type=jnp.float32)
            .reshape(seq_len, -1)
            .astype(jnp.bfloat16)
        )
        inner_sum = jnp.sum(probability * d_prob, -1, keepdims=True)
        d_raw = (probability * (d_prob - inner_sum) * score_scale).astype(jnp.bfloat16)
        d_queries = (
            jnp.einsum(
                "hqk,khd->qhd",
                d_raw,
                split_heads(keys_low, head_count),
                preferred_element_type=jnp.float32,
            )
            .reshape(seq_len, -1)
            .astype(jnp.bfloat16)
        )
        d_keys = (
            jnp.einsum(
                "hqk,qhd->khd",
                d_raw,
                split_heads(queries, head_count),
                preferred_element_type=jnp.float32,
            )
            .reshape(seq_len, -1)
            .astype(jnp.bfloat16)
        )
        grad_qkv = grad_qkv + jnp.stack(
            [
                jnp.einsum("td,te->de", token_rows, gradient, preferred_element_type=jnp.float32)
                for gradient in (d_queries, d_keys, d_values)
            ]
        )
        grad_bias = grad_bias + jnp.stack(
            [jnp.sum(d_queries.astype(jnp.float32), 0), jnp.sum(d_values.astype(jnp.float32), 0)]
        )
        return ((grad_qkv, grad_bias, grad_out), (d_queries, d_keys, d_values))

    start_grads = (
        jnp.zeros((3, model_width, attn_width), jnp.float32),
        jnp.zeros((2, attn_width), jnp.float32),
        jnp.zeros((attn_width, model_width), jnp.float32),
    )
    (grad_w_qkv, grad_b_qv, grad_w_out), seq_d = lax.scan(
        backward_seq, start_grads, (seq_input, segment_ids, seq_lse, seq_grad)
    )
    all_d = [gradient.reshape(-1, attn_width) for gradient in seq_d]
    summed = jnp.zeros((my_rows * lax.axis_size("tensor"), model_width), jnp.float32)
    for which in range(3):
        piece = all_d[which]
        summed = summed + jnp.einsum(
            "te,de->td", piece, w_qkv[which], preferred_element_type=jnp.float32
        )
    grad_input = d_first + lax.psum_scatter(
        summed.astype(jnp.bfloat16), "tensor", scatter_dimension=0, tiled=True
    ).astype(jnp.float32)
    grad_w_qkv, grad_b_qv, grad_w_out, grad_w_up, grad_b_up, grad_w_down = (
        lax.psum(grad_w_qkv.astype(jnp.bfloat16), "dp").astype(jnp.float32),
        lax.psum(grad_b_qv.astype(jnp.bfloat16), "dp").astype(jnp.float32),
        lax.psum(grad_w_out.astype(jnp.bfloat16), "dp").astype(jnp.float32),
        lax.psum(grad_w_up.astype(jnp.bfloat16), "dp").astype(jnp.float32),
        lax.psum(grad_b_up.astype(jnp.bfloat16), "dp").astype(jnp.float32),
        lax.psum(grad_w_down.astype(jnp.bfloat16), "dp").astype(jnp.float32),
    )
    grad_b_out, grad_ln1_gain, grad_ln1_bias, grad_b_down, grad_ln2_gain, grad_ln2_bias = lax.psum(
        (grad_b_out, grad_ln1_gain, grad_ln1_bias, grad_b_down, grad_ln2_gain, grad_ln2_bias),
        ("dp", "tensor"),
    )
    return (
        normed_two.astype(jnp.bfloat16),
        grad_input,
        grad_w_qkv,
        grad_b_qv,
        grad_w_out,
        grad_b_out,
        grad_ln1_gain,
        grad_ln1_bias,
        grad_w_up,
        grad_b_up,
        grad_w_down,
        grad_b_down,
        grad_ln2_gain,
        grad_ln2_bias,
    )


F32 = jnp.float32
BF = jnp.bfloat16
LOG2E = 1.4426950408889634


def dotf(a, b, ca, cb):
    return lax.dot_general(a, b, (((ca,), (cb,)), ((), ())), preferred_element_type=F32)


class Order:
    def __init__(self):
        self.token, self.waited = None, []

    def wait(self, *values):
        self.waited.extend(values)

    def __call__(self, kernel, outs, args, name, limit, aliases=None, smem=0):
        count = len(args)
        specs = [pl.BlockSpec(memory_space=pltpu.SMEM)] * smem + [pl.BlockSpec()] * (count - smem)
        unread = ([] if self.token is None else [self.token]) + self.waited
        specs += [pl.BlockSpec(memory_space=pltpu.HBM)] * len(unread)
        self.waited = []
        args = (*args, *unread)

        def body(*refs):
            kernel(*refs[:count], *refs[len(args) : -1])
            refs[-1][...] = jnp.zeros((8, 128), F32)

        *result, self.token = pl.pallas_call(
            body,
            out_shape=tuple(jax.ShapeDtypeStruct(s, d) for s, d in (*outs, ((8, 128), F32))),
            in_specs=specs,
            input_output_aliases=aliases or {},
            compiler_params=pltpu.CompilerParams(vmem_limit_bytes=limit << 20),
            cost_estimate=pl.CostEstimate(flops=1, bytes_accessed=1, transcendentals=0),
            name=name,
        )(*args)
        return result

    def add(self, a, b):
        def kernel(a_ref, b_ref, out):
            out[...] = (a_ref[...].astype(F32) + b_ref[...].astype(F32)).astype(out.dtype)

        return self(kernel, ((b.shape, b.dtype),), (a, b), "add", 8)[0]

    def now(self, value):
        return lax.optimization_barrier((value, self.token))[0]


def pack_attn_kernel(core, w_qkv, w_out, b_qv, qk, vo):
    width = w_qkv.shape[1]
    zero = jnp.zeros((16, 128), BF)
    first = lax.broadcasted_iota(jnp.int32, (16, 128), 0) == 0
    part = pl.ds(pl.multiple_of(core[0] * 128, 128), 128)
    qk[0:width, 0:128] = w_qkv[0, :, part]
    qk[0:width, 128:256] = w_qkv[1, :, part]
    vo[0:width, 0:128] = w_qkv[2, :, part]
    vo[0:width, 128:256] = w_out[part, :].astype(F32).T.astype(BF)
    qk[width : width + 16, 0:128] = jnp.where(first, b_qv[0:1, part].astype(F32), 0.0).astype(BF)
    vo[width : width + 16, 0:128] = jnp.where(first, b_qv[1:2, part].astype(F32), 0.0).astype(BF)
    qk[width : width + 16, 128:256] = zero
    vo[width : width + 16, 128:256] = zero


def pack_attn(order, core, w_qkv, w_out, b_qv):
    out = ((w_qkv.shape[1] + 16, 256), BF)
    return order(pack_attn_kernel, (out,) * 2, (core, w_qkv, w_out, b_qv), "pack_attn", 8, smem=1)


def pack_ffn_kernel(core, w_up, b_up, w_down, up, dn):
    width = w_up.shape[0]
    hid = w_up.shape[1] // 2
    first = lax.broadcasted_iota(jnp.int32, (16, hid), 0) == 0
    part = pl.ds(pl.multiple_of(core[0] * hid, hid), hid)
    up[0:width, :] = w_up[:, part]
    up[width : width + 16, :] = jnp.where(first, b_up[0:1, part].astype(F32), 0.0).astype(BF)
    dn[...] = w_down[part, :]


def pack_ffn(order, core, w_up, b_up, w_down):
    width, hid = w_up.shape[0], w_up.shape[1] // 2
    outs = (((width + 16, hid), BF), ((hid, width), BF))
    return order(pack_ffn_kernel, outs, (core, w_up, b_up, w_down), "pack_ffn", 12, smem=1)


def flip(order, matrix):
    width = matrix[0].shape[1]

    def kernel(*refs):
        start = 0
        for ref in refs[:-1]:
            rows = ref.shape[0]
            refs[-1][:, start : start + rows] = ref[...].astype(F32).T.astype(BF)
            start += rows

    rows = sum(m.shape[0] for m in matrix)
    return order(kernel, (((width, rows), BF),), tuple(matrix), "flip", 8)[0]


def take(refs, part):
    if len(refs) == 1:
        return refs[0][part, :]
    half = refs[0].shape[0]
    return refs[part.start // half][part.start % half : (part.stop - 1) % half + 1, :]


def whole(refs):
    return refs[0][...] if len(refs) == 1 else jnp.concatenate([r[...] for r in refs], 0)


def split_refs(refs, counts):
    out = []
    for count in counts:
        out.append(refs[:count])
        refs = refs[count:]
    return out


def attn_fwd(order, seqs, qk, vo):
    rows = sum(m.shape[0] for m in seqs[0][0])
    width = qk.shape[0] - 16
    counts, args, outs, aliases = [], [qk, vo], [], {}
    pt, qkv, ctx = ((2, rows, rows), BF), ((3, rows, 128), BF), ((rows, 128), BF)
    for x, mask, acc, low in seqs:
        counts += [len(x), 1, acc is not None]
        args += [*x, mask]
        if acc is not None:
            if not low:
                aliases[len(args)] = len(outs)
            args.append(acc)
        outs += [((rows, width), BF if low else F32), pt, qkv, ctx]

    def kernel(qk, vo, *refs):
        ins = split_refs(refs[: sum(counts)], counts)
        results = refs[sum(counts) :]
        row = lax.broadcasted_iota(jnp.int32, (128, rows), 0)
        for index, (_, _, _, low) in enumerate(seqs):
            x_refs, (mask,), acc = ins[3 * index : 3 * index + 3]
            (total_ref, pt, qkv, ctx_ref), results = results[:4], results[4:]
            x = whole(x_refs)
            qkf = dotf(x, qk[0:width, :], 1, 0) + qk[width : width + 16, :][0:1, :].astype(F32)
            vf = dotf(x, vo[0:width, 0:128], 1, 0) + vo[width : width + 16, 0:128][0:1, :].astype(F32)
            k = qkf[:, 128:].astype(BF)
            qkv[0] = qkf[:, :128].astype(BF)
            qkv[1] = k
            qkv[2] = vf.astype(BF)
            q_t = qkf[:, :128].T.astype(BF)
            v_t = vf.T.astype(BF)
            parts = []
            for h in range(2):
                q_h = jnp.where((row // HEAD_DIM) == h, q_t, jnp.zeros_like(q_t))
                s = dotf(k, q_h, 1, 0) * (HEAD_DIM**-0.5 * LOG2E) + mask[...]
                e = jnp.exp2(s - jnp.max(s, 0, keepdims=True))
                p = (e * (1.0 / jnp.sum(e, 0, keepdims=True))).astype(BF)
                pt[h] = p
                parts.append(dotf(v_t[h * HEAD_DIM : (h + 1) * HEAD_DIM, :], p, 1, 0))
            ctx = jnp.concatenate(parts, 0).T.astype(BF)
            ctx_ref[...] = ctx
            total = dotf(ctx, vo[0:width, 128:256], 1, 1)
            if acc:
                total = total + acc[0][...]
            total_ref[...] = total.astype(total_ref.dtype)

    result = list(order(kernel, tuple(outs), tuple(args), "attn_fwd", 8, aliases))
    out = []
    for _ in seqs:
        out.append((result[0], result[1:4]))
        result = result[4:]
    return out


def part_rows(part, half, extra):
    whole = ((0, half), (half + extra, 2 * half + extra), (2 * half + extra, 2 * half + 2 * extra), (half, half + extra))
    own = ((0, half), (0, half), (half, half + extra), (half, half + extra))
    return whole[part], own[part]


def add_got(value, got, part, half, extra):
    whole, own = part_rows(part, half, extra)
    for kind, ref in got:
        if kind == "whole":
            value = value + ref[whole[0] : whole[1], :].astype(F32)
        elif (kind == "top") == (part == 0):
            value = value + ref[own[0] : own[1], :].astype(F32)
    return value


def put(outs, part, half, extra, value):
    whole, own = part_rows(part, half, extra)
    if len(outs) == 1:
        outs[0][whole[0] : whole[1], :] = value.astype(BF)
    else:
        outs[part in (1, 2)][own[0] : own[1], :] = value.astype(BF)


def gradient_shapes(width, columns, extra, split):
    if split:
        return (((width // 2 + extra, columns), BF),) * 2
    return (((width + 2 * extra, columns), BF),)


def outer(order, left_t, right, got, split, name, bias, odd=None):
    kinds = [kind for kind, _ in got]
    width = left_t[0].shape[0]
    half, extra = width // 2, 16

    def kernel(*refs):
        if odd is not None:
            flag, *refs = refs
        left_refs, right_refs, refs = refs[:2], refs[2:4], refs[4:]
        received = list(zip(kinds, refs))
        outs = refs[len(kinds) :]
        if odd is not None:
            swapped = flag[0] == 1
        values = []
        for part in (0, 1):
            piece = slice(part * half, (part + 1) * half)
            value = dotf(left_refs[0][piece, :], right_refs[0][...], 1, 0)
            value = value + dotf(left_refs[1][piece, :], right_refs[1][...], 1, 0)
            values.append(add_got(value, received, part, half, extra))
        zero = jnp.zeros((extra, values[0].shape[1]), F32)
        row = zero
        if bias:
            first = lax.broadcasted_iota(jnp.int32, zero.shape, 0) == 0
            row = sum(jnp.sum(r[...].astype(F32), 0, keepdims=True) for r in right_refs)
            row = add_got(jnp.where(first, row, 0.0), received, 2, half, extra)
        if odd is None:
            for part in (0, 1):
                put(outs, part, half, extra, values[part])
            put(outs, 2, half, extra, row)
            put(outs, 3, half, extra, zero)
        else:
            outs[0][0:half, :] = jnp.where(swapped, values[1], values[0]).astype(BF)
            outs[1][0:half, :] = jnp.where(swapped, values[0], values[1]).astype(BF)
            outs[0][half:, :] = jnp.where(swapped, row, zero).astype(BF)
            outs[1][half:, :] = jnp.where(swapped, zero, row).astype(BF)

    outs = gradient_shapes(width, right[0].shape[1], extra, split)
    flags = () if odd is None else (odd,)
    args = (*flags, *left_t, *right, *(v for _, v in got))
    return order(kernel, outs, args, name, 8, smem=len(flags))


def relay(order, row_qk, row_vo, vo_diag, col_qk, col_vo, qk_diag):
    def kernel(row_qk, row_vo, vo_diag, col_qk, col_vo, qk_diag, row, col):
        row[:, 0:256] = row_qk[...]
        row[:, 256:512] = (row_vo[...].astype(F32) + vo_diag[...].astype(F32)).astype(BF)
        col[:, 0:256] = (col_qk[...].astype(F32) + qk_diag[...].astype(F32)).astype(BF)
        col[:, 256:512] = col_vo[...]

    out = ((row_qk.shape[0], 512), BF)
    return order(kernel, (out, out), (row_qk, row_vo, vo_diag, col_qk, col_vo, qk_diag), "relay", 10)


def own_sum(order, odd, own_qk, own_vo, row, col):
    half = row.shape[0] // 2

    def kernel(flag, own_qk, own_vo, row, col, keep, send):
        swapped = flag[0] == 1
        for own, place in ((own_qk, slice(0, 256)), (own_vo, slice(256, 512))):
            total = own[...].astype(F32) + row[:, place].astype(F32) + col[:, place].astype(F32)
            keep[:, place] = jnp.where(swapped, total[half:], total[:half]).astype(BF)
            send[:, place] = jnp.where(swapped, total[:half], total[half:]).astype(BF)

    out = ((half, 512), BF)
    return order(kernel, (out, out), (odd, own_qk, own_vo, row, col), "own_sum", 12, smem=1)


def final_halves(core, odd, refs):
    keep, keep_o, got, got_o = refs
    second, swapped = core[0] == 1, odd[0] == 1

    def value(ref):
        return ref[...].astype(F32)

    out = []
    for a, b, c, d in ((keep, keep_o, got, got_o), (keep_o, keep, got_o, got)):
        kept = jnp.where(second, value(b), value(a))
        received = jnp.where(second, value(d), value(c))
        out.append((jnp.where(swapped, received, kept), jnp.where(swapped, kept, received)))
    return out


def finish_down(order, core, odd, refs):
    half, columns = refs[0].shape
    half -= 16

    def kernel(core, odd, *refs):
        for i, pair in enumerate(final_halves(core, odd, refs[:4])):
            for j, value in enumerate(pair):
                refs[4][i * columns : (i + 1) * columns, j * half : (j + 1) * half] = value[:half].T

    return order(kernel, (((2 * columns, 2 * half), F32),), (core, odd, *refs), "finish_down", 12, smem=2)[0]


def finish_up(order, core, odd, refs):
    half, columns = refs[0].shape
    half -= 16

    def kernel(core, odd, *refs):
        for i, pair in enumerate(final_halves(core, odd, refs[:4])):
            place = slice(i * columns, (i + 1) * columns)
            for j, value in enumerate(pair):
                refs[5][j * half : (j + 1) * half, place] = value[:half]
            refs[4][0:1, place] = pair[1][half : half + 1]

    outs = (((1, 2 * columns), F32), ((2 * half, 2 * columns), F32))
    return order(kernel, outs, (core, odd, *refs), "finish_up", 12, smem=2)


def finish_attn(order, core, odd, refs):
    half = refs[0].shape[0] - 16

    def kernel(core, odd, *refs):
        w_qkv, b_qv, w_out = refs[4:]
        for i, pair in enumerate(final_halves(core, odd, refs[:4])):
            place = slice(i * 128, (i + 1) * 128)
            for j, value in enumerate(pair):
                rows = slice(j * half, (j + 1) * half)
                for k in range(3):
                    w_qkv[k, rows, place] = value[:half, k * 128 : (k + 1) * 128]
                w_out[place, rows] = value[:half, 384:512].T
            b_qv[0:1, place] = pair[1][half : half + 1, 0:128]
            b_qv[1:2, place] = pair[1][half : half + 1, 256:384]

    outs = (((3, 2 * half, 256), F32), ((2, 256), F32), ((256, 2 * half), F32))
    return order(kernel, outs, (core, odd, *refs), "finish_attn", 12, smem=2)


def attn_bwd(order, seqs, qk, vo, low=False):
    width = qk.shape[0] - 16
    half = width // 2
    rows = seqs[0][1].shape[1]
    counts, args, outs, aliases = [], [qk, vo], [], {}
    for index, (g, gt, xt, pt, qkv, ctx, acc) in enumerate(seqs):
        counts += [len(g), 1, 1, 1, 1, 1, acc is not None]
        args += [*g, gt, xt, pt, qkv, ctx]
        down = low and index == 1
        if acc is not None:
            if not down:
                aliases[len(args)] = len(outs)
            args.append(acc)
        outs.append(((rows, width), BF if down else F32))

    def kernel(qk, vo, *refs):
        ins = split_refs(refs[: sum(counts)], counts)
        totals, outs = refs[sum(counts) : sum(counts) + 2], refs[sum(counts) + 2 :]
        row = lax.broadcasted_iota(jnp.int32, (128, rows), 0)
        lane = lax.broadcasted_iota(jnp.int32, (rows, 128), 1)
        first = lax.broadcasted_iota(jnp.int32, (16, 256), 0) == 0
        dqks, dvs_all, ctxs = [], [], []
        for index in (0, 1):
            g, _, _, (pt_ref,), (qkv_ref,), (ctx_ref,), acc = ins[7 * index : 7 * index + 7]
            ctx = ctx_ref[...]
            d_o = dotf(whole(g), vo[0:width, 128:256], 1, 0).astype(BF)
            d_ot = d_o.astype(F32).T
            prod = d_ot * ctx.astype(F32).T * (HEAD_DIM**-0.5)
            d_ot = (d_ot * (HEAD_DIM**-0.5)).astype(BF)
            k_t = qkv_ref[1].astype(F32).T.astype(BF)
            dvs, dks, dqs = [], [], []
            for h in range(2):
                head = slice(h * HEAD_DIM, (h + 1) * HEAD_DIM)
                inner = jnp.sum(prod[head, :], 0, keepdims=True)
                p = pt_ref[h]
                dvs.append(dotf(p, d_o, 1, 0))
                d_h = jnp.where((row // HEAD_DIM) == h, d_ot, jnp.zeros_like(d_ot))
                ds = (p.astype(F32) * (dotf(qkv_ref[2], d_h, 1, 0) - inner)).astype(BF)
                dks.append(dotf(ds, qkv_ref[0], 1, 0))
                dqs.append(dotf(k_t[head, :], ds, 1, 0))
            dv = jnp.where(lane < HEAD_DIM, dvs[0], dvs[1]).astype(BF)
            dk = jnp.where(lane < HEAD_DIM, dks[0], dks[1]).astype(BF)
            dq = jnp.concatenate(dqs, 0).T.astype(BF)
            dqk = jnp.concatenate([dq, dk], 1)
            total = dotf(dqk, qk[0:width, :], 1, 1) + dotf(dv, vo[0:width, 0:128], 1, 1)
            if acc:
                total = total + acc[0][...]
            totals[index][...] = total.astype(totals[index].dtype)
            dqks.append(dqk)
            dvs_all.append(dv)
            ctxs.append(ctx)

        def both(place, rights, piece):
            return sum(dotf(ins[7 * i + place][0][piece, :], rights[i], 1, 0) for i in (0, 1))

        def column_sums(values):
            return sum(jnp.sum(v.astype(F32), 0, keepdims=True) for v in values)

        sums = [column_sums(dqks), jnp.concatenate([column_sums(dvs_all), jnp.zeros((1, 128), F32)], 1)]
        for index in (0, 1):
            out = outs[index : index + 1]
            for part in (0, 1):
                piece = slice(part * half, (part + 1) * half)
                if index == 0:
                    value = both(2, dqks, piece)
                else:
                    value = jnp.concatenate([both(2, dvs_all, piece), both(1, ctxs, piece)], 1)
                put(out, part, half, 16, value)
            put(out, 2, half, 16, jnp.where(first, sums[index], 0.0))
            put(out, 3, half, 16, jnp.zeros((16, 256), F32))

    outs += [*gradient_shapes(width, 256, 16, False) * 2]
    return order(kernel, tuple(outs), tuple(args), "attn_bwd", 8, aliases)


def ffn_fwd(order, seqs, up, dn, low=False):
    width = dn.shape[1]
    counts, args, outs, aliases = [], [up, dn], [], {}
    rows = sum(m.shape[0] for m in seqs[0][0])
    mid = ((rows, dn.shape[0]), BF)
    for n, acc in seqs:
        counts += [len(n), acc is not None]
        args += n
        if acc is not None:
            if not low:
                aliases[len(args)] = len(outs)
            args.append(acc)
        outs += [*((((rows // 2, width), BF),) * 2 if low else (((rows, width), F32),)), mid, mid]

    def kernel(up, dn, *refs):
        ins = split_refs(refs[: sum(counts)], counts)
        results = refs[sum(counts) :]
        for index in range(len(seqs)):
            n_refs, acc = ins[2 * index : 2 * index + 2]
            total_refs, results = results[: 1 + low], results[1 + low :]
            (act_ref, slope_ref), results = results[:2], results[2:]
            for i in (0, 1):
                part = slice(i * (rows // 2), (i + 1) * (rows // 2))
                u = dotf(take(n_refs, part), up[0:width, :], 1, 0) + up[width : width + 16, :][0:1, :].astype(F32)
                cdf = 0.5 + 0.5 * lax.erf(u * root_half)
                act = (u * cdf).astype(BF)
                act_ref[part, :] = act
                slope = cdf + u * (jnp.exp2(u * u * (-0.5 * LOG2E)) * inverse_root_two_pi)
                slope_ref[part, :] = slope.astype(BF)
                total = dotf(act, dn[...], 1, 0)
                if acc:
                    total = total + acc[0][part, :]
                if low:
                    total_refs[i][...] = total.astype(BF)
                else:
                    total_refs[0][part, :] = total

    result = list(order(kernel, tuple(outs), tuple(args), "ffn_fwd", 8, aliases))
    out = []
    for _ in seqs:
        out.append((result[: 1 + low], result[1 + low : 3 + low]))
        result = result[3 + low :]
    return out


def ffn_bwd(order, seqs, up, dn, low=False):
    width = dn.shape[1]
    counts, args, outs, aliases = [], [up, dn], [], {}
    rows = seqs[0][1].shape[0]
    for g, slope, acc in seqs:
        counts += [len(g), 1, acc is not None]
        args += [*g, slope]
        if acc is not None:
            if not low:
                aliases[len(args)] = len(outs)
            args.append(acc)
        outs += [*((((rows // 2, width), BF),) * 2 if low else (((rows, width), F32),)), (slope.shape, BF)]

    def kernel(up, dn, *refs):
        ins = split_refs(refs[: sum(counts)], counts)
        results = refs[sum(counts) :]
        for index in range(len(seqs)):
            g, (slope,), acc = ins[3 * index : 3 * index + 3]
            total_refs, results = results[: 1 + low], results[1 + low :]
            d_ref, *results = results
            d_up = (dotf(whole(g), dn[...], 1, 1) * slope[...].astype(F32)).astype(BF)
            d_ref[...] = d_up
            total = dotf(d_up, up[0:width, :], 1, 1)
            if acc:
                total = total + acc[0][...]
            if low:
                total_refs[0][...] = total[: rows // 2].astype(BF)
                total_refs[1][...] = total[rows // 2 :].astype(BF)
            else:
                total_refs[0][...] = total

    result = list(order(kernel, tuple(outs), tuple(args), "ffn_bwd", 8, aliases))
    out = []
    for _ in seqs:
        out.append((result[: 1 + low], result[1 + low]))
        result = result[2 + low :]
    return out


def standard(v):
    centered = v - jnp.mean(v, -1, keepdims=True)
    inv = lax.rsqrt(jnp.mean(centered * centered, -1, keepdims=True) + norm_epsilon)
    return centered * inv, inv


def back_through(g, scaled, inv, gain):
    e = g * gain
    return inv * (e - jnp.mean(e, -1, keepdims=True) - scaled * jnp.mean(e * scaled, -1, keepdims=True))


def half_of(refs, i):
    per = refs[0].shape[0] // 128
    return refs[i // per][(i % per) * 128 : (i % per + 1) * 128, :]


def first_norm(order, x, acc, got, b_out, gain, bias, b_down):
    rows, width = x.shape

    def kernel(x_ref, acc_ref, got_ref, b_out, gain, bias, b_down, sum_ref, out_ref, low_a, low_b, low_t):
        for i in range(rows // 128):
            part = slice(i * 128, (i + 1) * 128)
            total = x_ref[part, :].astype(F32) + b_out[...].astype(F32)
            total = total + acc_ref[part, :] + got_ref[part, :].astype(F32)
            sum_ref[part, :] = total
            scaled, _ = standard(total)
            normed = scaled * gain[...] + bias[...]
            out_ref[part, :] = normed + b_down[...].astype(F32)
            low = normed.astype(BF)
            place = (i * 128) % (rows // 2)
            (low_a, low_b)[i * 256 // rows][place : place + 128, :] = low
            low_t[:, part] = low.astype(F32).T.astype(BF)

    half = ((rows // 2, width), BF)
    outs = (((rows, width), F32), ((rows, width), F32), half, half, ((width, rows), BF))
    args = (x, acc, got, b_out[None], gain[None], bias[None], b_down[None])
    return order(kernel, outs, args, "first_norm", 14, {1: 0})


def emit_back(i, carry, g, scaled, inv, gain, out_ref, low_halves, low_t):
    part = slice(i * 128, (i + 1) * 128)
    d_rows = back_through(g, scaled, inv, gain)
    out_ref[part, :] = d_rows
    low = d_rows.astype(BF)
    half = low_halves[0].shape[0]
    place = (i * 128) % half
    low_halves[i * 128 // half][place : place + 128, :] = low
    low = low.astype(F32)
    low_t[:, part] = low.T.astype(BF)
    terms = (g * scaled, g, low)
    return tuple(c + jnp.sum(t, 0, keepdims=True) for c, t in zip(carry, terms))


def put_sums(sums_ref, carry):
    row = lax.broadcasted_iota(jnp.int32, sums_ref.shape, 0)
    sums_ref[...] = jnp.where(row == 0, carry[0], jnp.where(row == 1, carry[1], jnp.where(row == 2, carry[2], 0.0)))


def back_outs(rows, width):
    half = ((rows // 2, width), BF)
    return (((rows, width), F32), half, half, ((width, rows), BF), ((8, width), F32))


def second_norm(order, total, got, cotangent, gain, bias):
    rows, width = total.shape

    def kernel(sum_ref, got_a, got_b, cot_ref, gain, bias, d_ref, low_a, low_b, low_t, sums_ref, y_ref):
        carry = (jnp.zeros((1, width), F32),) * 3
        for i in range(rows // 128):
            part = slice(i * 128, (i + 1) * 128)
            scaled, inv = standard(sum_ref[part, :] + half_of((got_a, got_b), i).astype(F32))
            y_ref[part, :] = (scaled * gain[...] + bias[...]).astype(BF)
            g = cot_ref[part, :].astype(F32)
            carry = emit_back(i, carry, g, scaled, inv, gain[...], d_ref, (low_a, low_b), low_t)
        put_sums(sums_ref, carry)

    outs = (*back_outs(rows, width), ((rows, width), BF))
    return order(kernel, outs, (total, *got, cotangent, gain[None], bias[None]), "second_norm", 14, {0: 0})


def first_back(order, first, gain, d_normed, got):
    rows, width = first.shape

    def kernel(sum_ref, gain, d_ref, got_a, got_b, out_ref, low_a, low_b, low_t, sums_ref):
        carry = (jnp.zeros((1, width), F32),) * 3
        for i in range(rows // 128):
            part = slice(i * 128, (i + 1) * 128)
            scaled, inv = standard(sum_ref[part, :])
            g = d_ref[part, :] + half_of((got_a, got_b), i).astype(F32)
            carry = emit_back(i, carry, g, scaled, inv, gain[...], out_ref, (low_a, low_b), low_t)
        put_sums(sums_ref, carry)

    return order(kernel, back_outs(rows, width), (first, gain[None], d_normed, *got), "first_back", 14, {2: 0})

CORE = [(d, d ^ 1) for d in range(8)]
ROW = [(t, t ^ 1) for t in range(4)]
COL = [(t, t ^ 2) for t in range(4)]
NEAR = [(d, d ^ 2) for d in range(8)]
FAR = [(d, d ^ 4) for d in range(8)]


def swap_core(v):
    return lax.ppermute(v, "dp", CORE)


def swap_row(v):
    return lax.ppermute(v, "tensor", ROW)


def swap_col(v):
    return lax.ppermute(v, "tensor", COL)


def swap_near(v):
    return lax.ppermute(v, "dp", NEAR)


def swap_far(v):
    return lax.ppermute(v, "dp", FAR)


class Piece:
    def __init__(self, order, odd):
        self.order, self.odd = order, odd
        self.mine = [None] * 4

    def diagonal(self, top, bottom):
        self.top, self.bottom = swap_row(top), swap_col(bottom)

    def direct(self, row_part, col_part):
        self.row_part, self.col_part = swap_row(row_part), swap_col(col_part)

    def along_z(self, keep, send):
        self.keep, self.got = keep, swap_near(send)

    def second(self):
        self.keep = self.order.add(self.got, self.keep)
        self.got = swap_far(self.keep)

    def third(self):
        self.keep = self.order.add(self.got, self.keep)

    def fourth(self):
        self.got = swap_near(self.order.now(self.keep))

    def kept(self):
        self.keep_o = swap_core(self.order.now(self.keep))

    def last(self):
        self.got_o = swap_core(self.order.now(self.got))

    def all(self):
        return self.keep, self.keep_o, self.got, self.got_o


def fast(
    layer_input,
    segment_ids,
    w_qkv,
    b_qv,
    w_out,
    b_out,
    ln1_gain,
    ln1_bias,
    w_up,
    b_up,
    w_down,
    b_down,
    ln2_gain,
    ln2_bias,
    cotangent,
):
    rows, width = layer_input.shape
    hidden = w_up.shape[1] // 2
    core = lax.axis_index("dp") % 2
    odd_index = (lax.axis_index("dp") // 2) % 2
    odd = odd_index.astype(jnp.int32)[None]
    core = core.astype(jnp.int32)[None]
    order = Order()
    now, wait = order.now, order.wait

    segment = lax.dynamic_index_in_dim(segment_ids, lax.axis_index("tensor"), keepdims=False)
    inputs = ((layer_input,), (swap_core(layer_input),))
    qk, vo, up_w, dn_w = [None] * 4, [None] * 4, [None] * 4, [None] * 4
    qk[0], vo[0] = pack_attn(order, core, w_qkv, w_out, b_qv)
    qk[1], qk[2] = swap_row(qk[0]), swap_col(qk[0])
    vo[1], vo[2] = swap_row(vo[0]), swap_col(vo[0])
    up_w[0], dn_w[0] = pack_ffn(order, core, w_up, b_up[None], w_down)

    masks = [
        jnp.where(ids[:, None] == ids[None, :], 0.0, -1e30).astype(F32) for ids in (segment, swap_core(segment))
    ]
    total = [None, None]
    saved = [[None, None] for _ in range(4)]

    def attend(r, which, low=False):
        found = attn_fwd(order, [(inputs[s], masks[s], total[s], low) for s in which], qk[r], vo[r])
        for s, (total[s], saved[r][s]) in zip(which, found):
            continue

    attend(0, (0, 1))
    qk[3], vo[3] = swap_row(now(qk[2])), swap_col(now(vo[1]))
    attend(1, (0, 1))
    up_w[1], up_w[2] = swap_row(now(up_w[0])), swap_col(now(up_w[0]))
    attend(2, (0, 1))
    attend(3, (1,), True)
    got = swap_core(total[1])
    attend(3, (0,))
    wait(up_w[1], up_w[2])
    first, branch, *low, normed_t = first_norm(
        order, layer_input, total[0], got, b_out, ln1_gain, ln1_bias, b_down
    )
    dn_w[1], dn_w[2] = swap_row(now(dn_w[0])), swap_col(now(dn_w[0]))
    normed = (tuple(low), tuple(swap_core(v) for v in low))
    total = [branch, None]
    acts = [[None, None] for _ in range(4)]
    slopes = [[None, None] for _ in range(4)]

    def expand(r, which, low=False):
        found = ffn_fwd(order, [(normed[s], total[s]) for s in which], up_w[r], dn_w[r], low)
        for s, (total[s], (acts[r][s], slopes[r][s])) in zip(which, found):
            total[s] = total[s] if low else total[s][0]

    expand(0, (0,))
    expand(0, (1,))
    wait(dn_w[1], dn_w[2])
    normed_t = (normed_t, flip(order, normed[1]))
    up_w[3], dn_w[3] = swap_row(now(up_w[2])), swap_col(now(dn_w[1]))
    expand(1, (0, 1))
    expand(2, (0, 1))
    expand(3, (1,), True)
    got = [swap_core(v) for v in total[1]]
    expand(3, (0,))
    d_second, *low, branch_t, sums_two, output = second_norm(order, total[0], got, cotangent, ln2_gain, ln2_bias)
    branch_low = (tuple(low), tuple(swap_core(v) for v in low))

    down, up = Piece(order, odd), Piece(order, odd)
    attn, attn_qk, attn_vo = Piece(order, odd), Piece(order, odd), Piece(order, odd)
    total = [d_second, None]
    d_up = [[None, None] for _ in range(4)]

    def back(r, which, low=False):
        found = ffn_bwd(order, [(branch_low[s], slopes[r][s], total[s]) for s in which], up_w[r], dn_w[r], low)
        for s, (total[s], d_up[r][s]) in zip(which, found):
            total[s] = total[s] if low else total[s][0]

    def grad_down(r, got=(), split=False, z=None):
        return outer(order, branch_t, acts[r], got, split, "grad_down", False, z)

    def grad_up(r, got=(), split=False, z=None):
        return outer(order, normed_t, d_up[r], got, split, "grad_up", True, z)

    back(3, (0,))
    branch_t = (branch_t, flip(order, branch_low[1]))
    down.diagonal(*grad_down(3, split=True))
    back(3, (1,))
    up.diagonal(*grad_up(3, split=True))
    back(1, (0, 1))
    back(2, (0, 1))
    down_row = grad_down(1, [("bottom", down.bottom)])[0]
    down_col = grad_down(2, [("top", down.top)])[0]
    down.direct(down_row, down_col)
    back(0, (1,), True)
    got = [swap_core(v) for v in total[1]]
    back(0, (0,))
    d_first, *low, attention_t, sums_one = first_back(order, first, ln1_gain, total[0], got)
    attention_low = (tuple(low), tuple(swap_core(v) for v in low))
    inputs_t = [flip(order, inputs[s]) for s in (0, 1)]
    attention_t = (attention_t, flip(order, attention_low[1]))
    total = [d_first, None]

    def attend_back(r, low=False):
        seqs = [
            (attention_low[s], attention_t[s], inputs_t[s], *saved[r][s], total[s]) for s in (0, 1)
        ]
        total[0], total[1], attn_qk.mine[r], attn_vo.mine[r] = attn_bwd(order, seqs, qk[r], vo[r], low)

    down.along_z(*grad_down(0, [("whole", down.row_part), ("whole", down.col_part)], True, odd))
    up_rows = [swap_row(v) for v in grad_up(1, [("bottom", up.bottom)], True)]
    up_cols = [swap_col(v) for v in grad_up(2, [("top", up.top)], True)]
    down.second()
    attend_back(3)
    qk_diag, vo_diag = swap_row(attn_qk.mine[3]), swap_col(attn_vo.mine[3])
    attend_back(1)
    arrived = [(kind, v) for part in (up_rows, up_cols) for kind, v in zip(("top", "bottom"), part)]
    up.along_z(*grad_up(0, arrived, True, odd))
    attend_back(2)
    down.third()
    up.second()
    row, col = relay(order, attn_qk.mine[1], attn_vo.mine[1], vo_diag, attn_qk.mine[2], attn_vo.mine[2], qk_diag)
    row, col = swap_row(row), swap_col(col)
    down.fourth()
    attend_back(0, True)
    wait(down.got)
    attn.along_z(*own_sum(order, odd, attn_qk.mine[0], attn_vo.mine[0], row, col))
    up.third()
    small = jnp.concatenate([sums_one, sums_two], 0)
    small = order.add(swap_core(now(small)), small)
    small = order.add(swap_row(small), small)
    small = order.add(swap_col(small), small)
    small_near = swap_near(small)
    attn.second()
    up.fourth()
    down.kept()
    down.last()
    got = swap_core(now(total[1]))
    grad_w_down = finish_down(order, core, odd, down.all())
    small = order.add(small_near, small)
    small_far = swap_far(small)
    grad_input = order.add(got, total[0])
    wait(up.got)
    attn.third()
    attn.fourth()
    small = order.add(small_far, small)
    attn.kept()
    up.kept()
    up.last()
    grad_b_up, grad_w_up = finish_up(order, core, odd, up.all())
    attn.last()
    grad_w_qkv, grad_b_qv, grad_w_out = finish_attn(order, core, odd, attn.all())
    return (
        output,
        grad_input,
        grad_w_qkv,
        grad_b_qv,
        grad_w_out,
        small[2],
        small[0],
        small[1],
        grad_w_up,
        grad_b_up[0],
        grad_w_down,
        small[10],
        small[8],
        small[9],
    )


def local(*arrays):
    my_rows = arrays[0].shape[0]
    seq_len = arrays[1].shape[1]
    grid = (lax.axis_size("dp"), lax.axis_size("tensor"))
    if grid == (8, 4) and my_rows == seq_len and arrays[4].shape[0] == 4 * HEAD_DIM:
        return fast(*arrays)
    return general(*arrays)


def solution(mesh):
    return jax.shard_map(
        local,
        mesh=mesh,
        in_specs=(
            P(("dp", "tensor"), None),
            P("dp", None),
            P(None, None, "tensor"),
            P(None, "tensor"),
            P("tensor", None),
            P(),
            P(),
            P(),
            P(None, "tensor"),
            P("tensor"),
            P("tensor", None),
            P(),
            P(),
            P(),
            P(("dp", "tensor"), None),
        ),
        out_specs=(
            P(("dp", "tensor"), None),
            P(("dp", "tensor"), None),
            P(None, None, "tensor"),
            P(None, "tensor"),
            P("tensor", None),
            P(),
            P(),
            P(),
            P(None, "tensor"),
            P("tensor"),
            P("tensor", None),
            P(),
            P(),
            P(),
        ),
        check_vma=False,
    )
```

```python
import jax
import jax.numpy as jnp
from jax import lax
from jax.experimental import pallas as pl
from jax.experimental.pallas import tpu as pltpu
from jax.sharding import PartitionSpec as P

HEAD_DIM = 64


norm_epsilon = 1e-05
root_half = 0.7071067811865476
inverse_root_two_pi = 0.3989422804014327


def layer_norm(token_rows, norm_gain, norm_bias):
    row_mean = jnp.mean(token_rows, -1, keepdims=True)
    centered = token_rows - row_mean
    variance = jnp.mean(centered * centered, -1, keepdims=True)
    inv_std = lax.rsqrt(variance + norm_epsilon)
    scaled = centered * inv_std
    return (scaled * norm_gain + norm_bias, scaled, inv_std)


def norm_back(incoming, scaled, inv_std, norm_gain):
    weighted = incoming * norm_gain
    d_rows = inv_std * (
        weighted
        - jnp.mean(weighted, -1, keepdims=True)
        - scaled * jnp.mean(weighted * scaled, -1, keepdims=True)
    )
    return (d_rows, jnp.sum(incoming * scaled, 0), jnp.sum(incoming, 0))


def gelu_value(up_proj):
    return 0.5 * up_proj * (1.0 + lax.erf(up_proj * root_half))


def gelu_slope(up_proj):
    return (
        0.5 * (1.0 + lax.erf(up_proj * root_half))
        + up_proj * jnp.exp(-0.5 * up_proj * up_proj) * inverse_root_two_pi
    )


def split_heads(matrix, head_count):
    return matrix.reshape(matrix.shape[0], head_count, -1)


def project(token_rows, w_qkv, b_qv):
    queries = (
        jnp.dot(token_rows, w_qkv[0], preferred_element_type=jnp.float32)
        + b_qv[0].astype(jnp.float32)
    ).astype(jnp.bfloat16)
    keys_low = jnp.dot(token_rows, w_qkv[1], preferred_element_type=jnp.float32).astype(
        jnp.bfloat16
    )
    values = (
        jnp.dot(token_rows, w_qkv[2], preferred_element_type=jnp.float32)
        + b_qv[1].astype(jnp.float32)
    ).astype(jnp.bfloat16)
    return (queries, keys_low, values)


def scores(queries, keys_low, segment, head_count, score_scale):
    raw = jnp.einsum(
        "qhd,khd->hqk",
        split_heads(queries, head_count),
        split_heads(keys_low, head_count),
        preferred_element_type=jnp.float32,
    )
    same_doc = segment[:, None] == segment[None, :]
    return jnp.where(same_doc[None], raw * score_scale, -1e30)


def mix_values(prob_low, values, head_count):
    context = jnp.einsum(
        "hqk,khd->qhd",
        prob_low,
        split_heads(values, head_count),
        preferred_element_type=jnp.float32,
    )
    return context.reshape(context.shape[0], -1).astype(jnp.bfloat16)


def ffn_forward(normed_low, up_weight, up_bias, down_weight):
    up_proj = jnp.dot(normed_low, up_weight, preferred_element_type=jnp.float32) + up_bias.astype(
        jnp.float32
    )
    activation = gelu_value(up_proj).astype(jnp.bfloat16)
    return jnp.dot(activation, down_weight, preferred_element_type=jnp.float32)


def ffn_backward(normed_low, branch_low, up_weight, up_bias, down_weight):
    up_proj = jnp.dot(normed_low, up_weight, preferred_element_type=jnp.float32) + up_bias.astype(
        jnp.float32
    )
    activation = gelu_value(up_proj).astype(jnp.bfloat16)
    grad_down = jnp.einsum("tf,td->fd", activation, branch_low, preferred_element_type=jnp.float32)
    d_activation = jnp.einsum(
        "td,fd->tf", branch_low, down_weight, preferred_element_type=jnp.float32
    )
    d_up = (d_activation * gelu_slope(up_proj)).astype(jnp.bfloat16)
    grad_up = jnp.einsum("td,tf->df", normed_low, d_up, preferred_element_type=jnp.float32)
    grad_up_bias = jnp.sum(d_up.astype(jnp.float32), 0)
    return (grad_up, grad_up_bias, grad_down, d_up)


def general(
    layer_input,
    segment_ids,
    w_qkv,
    b_qv,
    w_out,
    b_out,
    ln1_gain,
    ln1_bias,
    w_up,
    b_up,
    w_down,
    b_down,
    ln2_gain,
    ln2_bias,
    cotangent,
):
    my_rows, model_width = layer_input.shape
    seq_len = segment_ids.shape[1]
    score_scale = HEAD_DIM ** (-0.5)
    whole_input = lax.all_gather(layer_input, "tensor", axis=0, tiled=True)
    seq_input = whole_input.reshape(segment_ids.shape[0], seq_len, model_width)
    attn_width = w_out.shape[0]
    head_count = attn_width // HEAD_DIM

    def forward_seq(running, seq_item):
        token_rows, segment = seq_item
        queries, keys_low, values = project(token_rows, w_qkv, b_qv)
        logits = scores(queries, keys_low, segment, head_count, score_scale)
        row_max = jnp.max(logits, -1, keepdims=True)
        exponent = jnp.exp(logits - row_max)
        expo_sum = jnp.sum(exponent, -1, keepdims=True)
        prob_low = (exponent / expo_sum).astype(jnp.bfloat16)
        return (running, (mix_values(prob_low, values, head_count), row_max + jnp.log(expo_sum)))

    _, (seq_context, seq_lse) = lax.scan(forward_seq, None, (seq_input, segment_ids))
    all_context = seq_context.reshape(-1, attn_width)
    attention = lax.psum_scatter(
        jnp.dot(all_context, w_out, preferred_element_type=jnp.float32),
        "tensor",
        scatter_dimension=0,
        tiled=True,
    ) + b_out.astype(jnp.float32)
    normed_one, scaled_one, inv_one = layer_norm(
        layer_input.astype(jnp.float32) + attention, ln1_gain, ln1_bias
    )
    normed_low = normed_one.astype(jnp.bfloat16)
    whole_normed = lax.all_gather(normed_low, "tensor", axis=0, tiled=True)
    branch = lax.psum_scatter(
        ffn_forward(whole_normed, w_up, b_up, w_down), "tensor", scatter_dimension=0, tiled=True
    )
    normed_two, scaled_two, inv_two = layer_norm(
        normed_one + branch + b_down.astype(jnp.float32), ln2_gain, ln2_bias
    )
    d_second, grad_ln2_gain, grad_ln2_bias = norm_back(
        cotangent.astype(jnp.float32), scaled_two, inv_two, ln2_gain
    )
    branch_low = d_second.astype(jnp.bfloat16)
    grad_b_down = jnp.sum(branch_low.astype(jnp.float32), 0)
    whole_branch = lax.all_gather(branch_low, "tensor", axis=0, tiled=True)
    grad_w_up, grad_b_up, grad_w_down, d_up = ffn_backward(
        whole_normed, whole_branch, w_up, b_up, w_down
    )
    d_normed = lax.psum_scatter(
        jnp.einsum("tf,df->td", d_up, w_up, preferred_element_type=jnp.float32),
        "tensor",
        scatter_dimension=0,
        tiled=True,
    )
    d_first, grad_ln1_gain, grad_ln1_bias = norm_back(
        d_second + d_normed, scaled_one, inv_one, ln1_gain
    )
    attention_low = d_first.astype(jnp.bfloat16)
    grad_b_out = jnp.sum(attention_low.astype(jnp.float32), 0)
    whole_grad = lax.all_gather(attention_low, "tensor", axis=0, tiled=True)
    seq_grad = whole_grad.reshape(seq_input.shape[0], seq_len, model_width)

    def backward_seq(running, seq_item):
        grad_qkv, grad_bias, grad_out = running
        token_rows, segment, seq_lse_one, grad_rows = seq_item
        queries, keys_low, values = project(token_rows, w_qkv, b_qv)
        logits = scores(queries, keys_low, segment, head_count, score_scale)
        probability = jnp.exp(logits - seq_lse_one)
        prob_low = probability.astype(jnp.bfloat16)
        context = mix_values(prob_low, values, head_count)
        grad_out = grad_out + jnp.einsum(
            "te,td->ed", context, grad_rows, preferred_element_type=jnp.float32
        )
        d_context = jnp.einsum(
            "td,ed->te", grad_rows, w_out, preferred_element_type=jnp.float32
        ).astype(jnp.bfloat16)
        d_heads = split_heads(d_context, head_count)
        d_prob = jnp.einsum(
            "qhd,khd->hqk",
            d_heads,
            split_heads(values, head_count),
            preferred_element_type=jnp.float32,
        )
        d_values = (
            jnp.einsum("hqk,qhd->khd", prob_low, d_heads, preferred_element_type=jnp.float32)
            .reshape(seq_len, -1)
            .astype(jnp.bfloat16)
        )
        inner_sum = jnp.sum(probability * d_prob, -1, keepdims=True)
        d_raw = (probability * (d_prob - inner_sum) * score_scale).astype(jnp.bfloat16)
        d_queries = (
            jnp.einsum(
                "hqk,khd->qhd",
                d_raw,
                split_heads(keys_low, head_count),
                preferred_element_type=jnp.float32,
            )
            .reshape(seq_len, -1)
            .astype(jnp.bfloat16)
        )
        d_keys = (
            jnp.einsum(
                "hqk,qhd->khd",
                d_raw,
                split_heads(queries, head_count),
                preferred_element_type=jnp.float32,
            )
            .reshape(seq_len, -1)
            .astype(jnp.bfloat16)
        )
        grad_qkv = grad_qkv + jnp.stack(
            [
                jnp.einsum("td,te->de", token_rows, gradient, preferred_element_type=jnp.float32)
                for gradient in (d_queries, d_keys, d_values)
            ]
        )
        grad_bias = grad_bias + jnp.stack(
            [jnp.sum(d_queries.astype(jnp.float32), 0), jnp.sum(d_values.astype(jnp.float32), 0)]
        )
        return ((grad_qkv, grad_bias, grad_out), (d_queries, d_keys, d_values))

    start_grads = (
        jnp.zeros((3, model_width, attn_width), jnp.float32),
        jnp.zeros((2, attn_width), jnp.float32),
        jnp.zeros((attn_width, model_width), jnp.float32),
    )
    (grad_w_qkv, grad_b_qv, grad_w_out), seq_d = lax.scan(
        backward_seq, start_grads, (seq_input, segment_ids, seq_lse, seq_grad)
    )
    all_d = [gradient.reshape(-1, attn_width) for gradient in seq_d]
    summed = jnp.zeros((my_rows * lax.axis_size("tensor"), model_width), jnp.float32)
    for which in range(3):
        piece = all_d[which]
        summed = summed + jnp.einsum(
            "te,de->td", piece, w_qkv[which], preferred_element_type=jnp.float32
        )
    grad_input = d_first + lax.psum_scatter(
        summed.astype(jnp.bfloat16), "tensor", scatter_dimension=0, tiled=True
    ).astype(jnp.float32)
    grad_w_qkv, grad_b_qv, grad_w_out, grad_w_up, grad_b_up, grad_w_down = (
        lax.psum(grad_w_qkv.astype(jnp.bfloat16), "dp").astype(jnp.float32),
        lax.psum(grad_b_qv.astype(jnp.bfloat16), "dp").astype(jnp.float32),
        lax.psum(grad_w_out.astype(jnp.bfloat16), "dp").astype(jnp.float32),
        lax.psum(grad_w_up.astype(jnp.bfloat16), "dp").astype(jnp.float32),
        lax.psum(grad_b_up.astype(jnp.bfloat16), "dp").astype(jnp.float32),
        lax.psum(grad_w_down.astype(jnp.bfloat16), "dp").astype(jnp.float32),
    )
    grad_b_out, grad_ln1_gain, grad_ln1_bias, grad_b_down, grad_ln2_gain, grad_ln2_bias = lax.psum(
        (grad_b_out, grad_ln1_gain, grad_ln1_bias, grad_b_down, grad_ln2_gain, grad_ln2_bias),
        ("dp", "tensor"),
    )
    return (
        normed_two.astype(jnp.bfloat16),
        grad_input,
        grad_w_qkv,
        grad_b_qv,
        grad_w_out,
        grad_b_out,
        grad_ln1_gain,
        grad_ln1_bias,
        grad_w_up,
        grad_b_up,
        grad_w_down,
        grad_b_down,
        grad_ln2_gain,
        grad_ln2_bias,
    )


F32 = jnp.float32
BF = jnp.bfloat16
LOG2E = 1.4426950408889634


def dotf(a, b, ca, cb):
    return lax.dot_general(a, b, (((ca,), (cb,)), ((), ())), preferred_element_type=F32)


class Order:
    def __init__(self):
        self.token, self.waited = None, []

    def wait(self, *values):
        self.waited.extend(values)

    def __call__(self, kernel, outs, args, name, limit, aliases=None, smem=0):
        count = len(args)
        specs = [pl.BlockSpec(memory_space=pltpu.SMEM)] * smem + [pl.BlockSpec()] * (count - smem)
        unread = ([] if self.token is None else [self.token]) + self.waited
        specs += [pl.BlockSpec(memory_space=pltpu.HBM)] * len(unread)
        self.waited = []
        args = (*args, *unread)

        def body(*refs):
            kernel(*refs[:count], *refs[len(args) : -1])
            refs[-1][...] = jnp.zeros((8, 128), F32)

        *result, self.token = pl.pallas_call(
            body,
            out_shape=tuple(jax.ShapeDtypeStruct(s, d) for s, d in (*outs, ((8, 128), F32))),
            in_specs=specs,
            input_output_aliases=aliases or {},
            compiler_params=pltpu.CompilerParams(vmem_limit_bytes=limit << 20),
            cost_estimate=pl.CostEstimate(flops=1, bytes_accessed=1, transcendentals=0),
            name=name,
        )(*args)
        return result

    def add(self, a, b):
        def kernel(a_ref, b_ref, out):
            out[...] = (a_ref[...].astype(F32) + b_ref[...].astype(F32)).astype(out.dtype)

        return self(kernel, ((b.shape, b.dtype),), (a, b), "add", 8)[0]

    def now(self, value):
        return lax.optimization_barrier((value, self.token))[0]


def pack_attn_kernel(core, w_qkv, w_out, b_qv, qk, vo):
    width = w_qkv.shape[1]
    zero = jnp.zeros((16, 128), BF)
    first = lax.broadcasted_iota(jnp.int32, (16, 128), 0) == 0
    part = pl.ds(pl.multiple_of(core[0] * 128, 128), 128)
    qk[0:width, 0:128] = w_qkv[0, :, part]
    qk[0:width, 128:256] = w_qkv[1, :, part]
    vo[0:width, 0:128] = w_qkv[2, :, part]
    vo[0:width, 128:256] = w_out[part, :].astype(F32).T.astype(BF)
    qk[width : width + 16, 0:128] = jnp.where(first, b_qv[0:1, part].astype(F32), 0.0).astype(BF)
    vo[width : width + 16, 0:128] = jnp.where(first, b_qv[1:2, part].astype(F32), 0.0).astype(BF)
    qk[width : width + 16, 128:256] = zero
    vo[width : width + 16, 128:256] = zero


def pack_attn(order, core, w_qkv, w_out, b_qv):
    out = ((w_qkv.shape[1] + 16, 256), BF)
    return order(pack_attn_kernel, (out,) * 2, (core, w_qkv, w_out, b_qv), "pack_attn", 8, smem=1)


def pack_ffn_kernel(core, w_up, b_up, w_down, up, dn):
    width = w_up.shape[0]
    hid = w_up.shape[1] // 2
    first = lax.broadcasted_iota(jnp.int32, (16, hid), 0) == 0
    part = pl.ds(pl.multiple_of(core[0] * hid, hid), hid)
    up[0:width, :] = w_up[:, part]
    up[width : width + 16, :] = jnp.where(first, b_up[0:1, part].astype(F32), 0.0).astype(BF)
    dn[...] = w_down[part, :]


def pack_ffn(order, core, w_up, b_up, w_down):
    width, hid = w_up.shape[0], w_up.shape[1] // 2
    outs = (((width + 16, hid), BF), ((hid, width), BF))
    return order(pack_ffn_kernel, outs, (core, w_up, b_up, w_down), "pack_ffn", 12, smem=1)


def flip(order, matrix):
    width = matrix[0].shape[1]

    def kernel(*refs):
        start = 0
        for ref in refs[:-1]:
            rows = ref.shape[0]
            refs[-1][:, start : start + rows] = ref[...].astype(F32).T.astype(BF)
            start += rows

    rows = sum(m.shape[0] for m in matrix)
    return order(kernel, (((width, rows), BF),), tuple(matrix), "flip", 8)[0]


def take(refs, part):
    if len(refs) == 1:
        return refs[0][part, :]
    half = refs[0].shape[0]
    return refs[part.start // half][part.start % half : (part.stop - 1) % half + 1, :]


def whole(refs):
    return refs[0][...] if len(refs) == 1 else jnp.concatenate([r[...] for r in refs], 0)


def split_refs(refs, counts):
    out = []
    for count in counts:
        out.append(refs[:count])
        refs = refs[count:]
    return out


def attn_fwd(order, seqs, qk, vo):
    rows = sum(m.shape[0] for m in seqs[0][0])
    width = qk.shape[0] - 16
    counts, args, outs, aliases = [], [qk, vo], [], {}
    pt, qkv, ctx = ((2, rows, rows), BF), ((3, rows, 128), BF), ((rows, 128), BF)
    for x, mask, acc, low in seqs:
        counts += [len(x), 1, acc is not None]
        args += [*x, mask]
        if acc is not None:
            if not low:
                aliases[len(args)] = len(outs)
            args.append(acc)
        outs += [((rows, width), BF if low else F32), pt, qkv, ctx]

    def kernel(qk, vo, *refs):
        ins = split_refs(refs[: sum(counts)], counts)
        results = refs[sum(counts) :]
        row = lax.broadcasted_iota(jnp.int32, (128, rows), 0)
        for index, (_, _, _, low) in enumerate(seqs):
            x_refs, (mask,), acc = ins[3 * index : 3 * index + 3]
            (total_ref, pt, qkv, ctx_ref), results = results[:4], results[4:]
            x = whole(x_refs)
            qkf = dotf(x, qk[0:width, :], 1, 0) + qk[width : width + 16, :][0:1, :].astype(F32)
            vf = dotf(x, vo[0:width, 0:128], 1, 0) + vo[width : width + 16, 0:128][0:1, :].astype(F32)
            k = qkf[:, 128:].astype(BF)
            qkv[0] = qkf[:, :128].astype(BF)
            qkv[1] = k
            qkv[2] = vf.astype(BF)
            q_t = qkf[:, :128].T.astype(BF)
            v_t = vf.T.astype(BF)
            parts = []
            for h in range(2):
                q_h = jnp.where((row // HEAD_DIM) == h, q_t, jnp.zeros_like(q_t))
                s = dotf(k, q_h, 1, 0) * (HEAD_DIM**-0.5 * LOG2E) + mask[...]
                e = jnp.exp2(s - jnp.max(s, 0, keepdims=True))
                p = (e * (1.0 / jnp.sum(e, 0, keepdims=True))).astype(BF)
                pt[h] = p
                parts.append(dotf(v_t[h * HEAD_DIM : (h + 1) * HEAD_DIM, :], p, 1, 0))
            ctx = jnp.concatenate(parts, 0).T.astype(BF)
            ctx_ref[...] = ctx
            total = dotf(ctx, vo[0:width, 128:256], 1, 1)
            if acc:
                total = total + acc[0][...]
            total_ref[...] = total.astype(total_ref.dtype)

    result = list(order(kernel, tuple(outs), tuple(args), "attn_fwd", 8, aliases))
    out = []
    for _ in seqs:
        out.append((result[0], result[1:4]))
        result = result[4:]
    return out


def part_rows(part, half, extra):
    whole = ((0, half), (half + extra, 2 * half + extra), (2 * half + extra, 2 * half + 2 * extra), (half, half + extra))
    own = ((0, half), (0, half), (half, half + extra), (half, half + extra))
    return whole[part], own[part]


def add_got(value, got, part, half, extra):
    whole, own = part_rows(part, half, extra)
    for kind, ref in got:
        if kind == "whole":
            value = value + ref[whole[0] : whole[1], :].astype(F32)
        elif (kind == "top") == (part == 0):
            value = value + ref[own[0] : own[1], :].astype(F32)
    return value


def put(outs, part, half, extra, value):
    whole, own = part_rows(part, half, extra)
    if len(outs) == 1:
        outs[0][whole[0] : whole[1], :] = value.astype(BF)
    else:
        outs[part in (1, 2)][own[0] : own[1], :] = value.astype(BF)


def gradient_shapes(width, columns, extra, split):
    if split:
        return (((width // 2 + extra, columns), BF),) * 2
    return (((width + 2 * extra, columns), BF),)


def outer(order, left_t, right, got, split, name, bias, odd=None):
    kinds = [kind for kind, _ in got]
    width = left_t[0].shape[0]
    half, extra = width // 2, 16

    def kernel(*refs):
        if odd is not None:
            flag, *refs = refs
        left_refs, right_refs, refs = refs[:2], refs[2:4], refs[4:]
        received = list(zip(kinds, refs))
        outs = refs[len(kinds) :]
        if odd is not None:
            swapped = flag[0] == 1
        values = []
        for part in (0, 1):
            piece = slice(part * half, (part + 1) * half)
            value = dotf(left_refs[0][piece, :], right_refs[0][...], 1, 0)
            value = value + dotf(left_refs[1][piece, :], right_refs[1][...], 1, 0)
            values.append(add_got(value, received, part, half, extra))
        zero = jnp.zeros((extra, values[0].shape[1]), F32)
        row = zero
        if bias:
            first = lax.broadcasted_iota(jnp.int32, zero.shape, 0) == 0
            row = sum(jnp.sum(r[...].astype(F32), 0, keepdims=True) for r in right_refs)
            row = add_got(jnp.where(first, row, 0.0), received, 2, half, extra)
        if odd is None:
            for part in (0, 1):
                put(outs, part, half, extra, values[part])
            put(outs, 2, half, extra, row)
            put(outs, 3, half, extra, zero)
        else:
            outs[0][0:half, :] = jnp.where(swapped, values[1], values[0]).astype(BF)
            outs[1][0:half, :] = jnp.where(swapped, values[0], values[1]).astype(BF)
            outs[0][half:, :] = jnp.where(swapped, row, zero).astype(BF)
            outs[1][half:, :] = jnp.where(swapped, zero, row).astype(BF)

    outs = gradient_shapes(width, right[0].shape[1], extra, split)
    flags = () if odd is None else (odd,)
    args = (*flags, *left_t, *right, *(v for _, v in got))
    return order(kernel, outs, args, name, 8, smem=len(flags))


def pass_on(order, row_part, bottom, col_part, top):
    half = row_part.shape[0] // 2

    def kernel(row_ref, bottom_ref, col_ref, top_ref, row, col):
        row[0:half, :] = row_ref[0:half, :]
        row[half:, :] = (row_ref[half:, :].astype(F32) + bottom_ref[...].astype(F32)).astype(BF)
        col[half:, :] = col_ref[half:, :]
        col[0:half, :] = (col_ref[0:half, :].astype(F32) + top_ref[...].astype(F32)).astype(BF)

    out = (row_part.shape, BF)
    return order(kernel, (out, out), (row_part, bottom, col_part, top), "pass_on", 10)


def add_pair(order, a, b, c, d):
    def kernel(a, b, c, d, first, second):
        first[...] = (a[...].astype(F32) + b[...].astype(F32)).astype(BF)
        second[...] = (c[...].astype(F32) + d[...].astype(F32)).astype(BF)

    return order(kernel, ((a.shape, BF), (c.shape, BF)), (a, b, c, d), "add_pair", 8)


def sum_halves(order, odd, own, row, col):
    half = own.shape[0] // 2

    def kernel(flag, own, row, col, keep, send):
        swapped = flag[0] == 1
        total = own[...].astype(F32) + row[...].astype(F32) + col[...].astype(F32)
        keep[...] = jnp.where(swapped, total[half:], total[:half]).astype(BF)
        send[...] = jnp.where(swapped, total[:half], total[half:]).astype(BF)

    out = ((half, own.shape[1]), BF)
    return order(kernel, (out, out), (odd, own, row, col), "sum_halves", 10, smem=1)


def relay(order, row_qk, row_vo, vo_diag, col_qk, col_vo, qk_diag):
    def kernel(row_qk, row_vo, vo_diag, col_qk, col_vo, qk_diag, row, col):
        row[:, 0:256] = row_qk[...]
        row[:, 256:512] = (row_vo[...].astype(F32) + vo_diag[...].astype(F32)).astype(BF)
        col[:, 0:256] = (col_qk[...].astype(F32) + qk_diag[...].astype(F32)).astype(BF)
        col[:, 256:512] = col_vo[...]

    out = ((row_qk.shape[0], 512), BF)
    return order(kernel, (out, out), (row_qk, row_vo, vo_diag, col_qk, col_vo, qk_diag), "relay", 10)


def own_sum(order, odd, own_qk, own_vo, row, col):
    half = row.shape[0] // 2

    def kernel(flag, own_qk, own_vo, row, col, keep, send):
        swapped = flag[0] == 1
        for own, place in ((own_qk, slice(0, 256)), (own_vo, slice(256, 512))):
            total = own[...].astype(F32) + row[:, place].astype(F32) + col[:, place].astype(F32)
            keep[:, place] = jnp.where(swapped, total[half:], total[:half]).astype(BF)
            send[:, place] = jnp.where(swapped, total[:half], total[half:]).astype(BF)

    out = ((half, 512), BF)
    return order(kernel, (out, out), (odd, own_qk, own_vo, row, col), "own_sum", 12, smem=1)


def final_halves(core, odd, refs):
    keep, keep_o, got, got_o = refs
    second, swapped = core[0] == 1, odd[0] == 1

    def value(ref):
        return ref[...].astype(F32)

    out = []
    for a, b, c, d in ((keep, keep_o, got, got_o), (keep_o, keep, got_o, got)):
        kept = jnp.where(second, value(b), value(a))
        received = jnp.where(second, value(d), value(c))
        out.append((jnp.where(swapped, received, kept), jnp.where(swapped, kept, received)))
    return out


def finish_down(order, core, odd, refs):
    half, columns = refs[0].shape
    half -= 16

    def kernel(core, odd, *refs):
        for i, pair in enumerate(final_halves(core, odd, refs[:4])):
            for j, value in enumerate(pair):
                refs[4][i * columns : (i + 1) * columns, j * half : (j + 1) * half] = value[:half].T

    return order(kernel, (((2 * columns, 2 * half), F32),), (core, odd, *refs), "finish_down", 12, smem=2)[0]


def finish_up(order, core, odd, refs):
    half, columns = refs[0].shape
    half -= 16

    def kernel(core, odd, *refs):
        for i, pair in enumerate(final_halves(core, odd, refs[:4])):
            place = slice(i * columns, (i + 1) * columns)
            for j, value in enumerate(pair):
                refs[5][j * half : (j + 1) * half, place] = value[:half]
            refs[4][0:1, place] = pair[1][half : half + 1]

    outs = (((1, 2 * columns), F32), ((2 * half, 2 * columns), F32))
    return order(kernel, outs, (core, odd, *refs), "finish_up", 12, smem=2)


def finish_attn(order, core, odd, refs):
    half = refs[0].shape[0] - 16

    def kernel(core, odd, *refs):
        w_qkv, b_qv, w_out = refs[4:]
        for i, pair in enumerate(final_halves(core, odd, refs[:4])):
            place = slice(i * 128, (i + 1) * 128)
            for j, value in enumerate(pair):
                rows = slice(j * half, (j + 1) * half)
                for k in range(3):
                    w_qkv[k, rows, place] = value[:half, k * 128 : (k + 1) * 128]
                w_out[place, rows] = value[:half, 384:512].T
            b_qv[0:1, place] = pair[1][half : half + 1, 0:128]
            b_qv[1:2, place] = pair[1][half : half + 1, 256:384]

    outs = (((3, 2 * half, 256), F32), ((2, 256), F32), ((256, 2 * half), F32))
    return order(kernel, outs, (core, odd, *refs), "finish_attn", 12, smem=2)


def attn_bwd(order, seqs, qk, vo, low=False):
    width = qk.shape[0] - 16
    half = width // 2
    rows = seqs[0][1].shape[1]
    counts, args, outs, aliases = [], [qk, vo], [], {}
    for index, (g, gt, xt, pt, qkv, ctx, acc) in enumerate(seqs):
        counts += [len(g), 1, 1, 1, 1, 1, acc is not None]
        args += [*g, gt, xt, pt, qkv, ctx]
        down = low and index == 1
        if acc is not None:
            if not down:
                aliases[len(args)] = len(outs)
            args.append(acc)
        outs.append(((rows, width), BF if down else F32))

    def kernel(qk, vo, *refs):
        ins = split_refs(refs[: sum(counts)], counts)
        totals, outs = refs[sum(counts) : sum(counts) + 2], refs[sum(counts) + 2 :]
        row = lax.broadcasted_iota(jnp.int32, (128, rows), 0)
        lane = lax.broadcasted_iota(jnp.int32, (rows, 128), 1)
        first = lax.broadcasted_iota(jnp.int32, (16, 256), 0) == 0
        dqks, dvs_all, ctxs = [], [], []
        for index in (0, 1):
            g, _, _, (pt_ref,), (qkv_ref,), (ctx_ref,), acc = ins[7 * index : 7 * index + 7]
            ctx = ctx_ref[...]
            d_o = dotf(whole(g), vo[0:width, 128:256], 1, 0).astype(BF)
            d_ot = d_o.astype(F32).T
            prod = d_ot * ctx.astype(F32).T * (HEAD_DIM**-0.5)
            d_ot = (d_ot * (HEAD_DIM**-0.5)).astype(BF)
            k_t = qkv_ref[1].astype(F32).T.astype(BF)
            dvs, dks, dqs = [], [], []
            for h in range(2):
                head = slice(h * HEAD_DIM, (h + 1) * HEAD_DIM)
                inner = jnp.sum(prod[head, :], 0, keepdims=True)
                p = pt_ref[h]
                dvs.append(dotf(p, d_o, 1, 0))
                d_h = jnp.where((row // HEAD_DIM) == h, d_ot, jnp.zeros_like(d_ot))
                ds = (p.astype(F32) * (dotf(qkv_ref[2], d_h, 1, 0) - inner)).astype(BF)
                dks.append(dotf(ds, qkv_ref[0], 1, 0))
                dqs.append(dotf(k_t[head, :], ds, 1, 0))
            dv = jnp.where(lane < HEAD_DIM, dvs[0], dvs[1]).astype(BF)
            dk = jnp.where(lane < HEAD_DIM, dks[0], dks[1]).astype(BF)
            dq = jnp.concatenate(dqs, 0).T.astype(BF)
            dqk = jnp.concatenate([dq, dk], 1)
            total = dotf(dqk, qk[0:width, :], 1, 1) + dotf(dv, vo[0:width, 0:128], 1, 1)
            if acc:
                total = total + acc[0][...]
            totals[index][...] = total.astype(totals[index].dtype)
            dqks.append(dqk)
            dvs_all.append(dv)
            ctxs.append(ctx)

        def both(place, rights, piece):
            return sum(dotf(ins[7 * i + place][0][piece, :], rights[i], 1, 0) for i in (0, 1))

        def column_sums(values):
            return sum(jnp.sum(v.astype(F32), 0, keepdims=True) for v in values)

        sums = [column_sums(dqks), jnp.concatenate([column_sums(dvs_all), jnp.zeros((1, 128), F32)], 1)]
        for index in (0, 1):
            out = outs[index : index + 1]
            for part in (0, 1):
                piece = slice(part * half, (part + 1) * half)
                if index == 0:
                    value = both(2, dqks, piece)
                else:
                    value = jnp.concatenate([both(2, dvs_all, piece), both(1, ctxs, piece)], 1)
                put(out, part, half, 16, value)
            put(out, 2, half, 16, jnp.where(first, sums[index], 0.0))
            put(out, 3, half, 16, jnp.zeros((16, 256), F32))

    outs += [*gradient_shapes(width, 256, 16, False) * 2]
    return order(kernel, tuple(outs), tuple(args), "attn_bwd", 8, aliases)


def ffn_fwd(order, seqs, up, dn, low=False):
    width = dn.shape[1]
    counts, args, outs, aliases = [], [up, dn], [], {}
    rows = sum(m.shape[0] for m in seqs[0][0])
    mid = ((rows, dn.shape[0]), BF)
    for n, acc in seqs:
        counts += [len(n), acc is not None]
        args += n
        if acc is not None:
            if not low:
                aliases[len(args)] = len(outs)
            args.append(acc)
        outs += [*((((rows // 2, width), BF),) * 2 if low else (((rows, width), F32),)), mid, mid]

    def kernel(up, dn, *refs):
        ins = split_refs(refs[: sum(counts)], counts)
        results = refs[sum(counts) :]
        for index in range(len(seqs)):
            n_refs, acc = ins[2 * index : 2 * index + 2]
            total_refs, results = results[: 1 + low], results[1 + low :]
            (act_ref, slope_ref), results = results[:2], results[2:]
            for i in (0, 1):
                part = slice(i * (rows // 2), (i + 1) * (rows // 2))
                u = dotf(take(n_refs, part), up[0:width, :], 1, 0) + up[width : width + 16, :][0:1, :].astype(F32)
                cdf = 0.5 + 0.5 * lax.erf(u * root_half)
                act = (u * cdf).astype(BF)
                act_ref[part, :] = act
                slope = cdf + u * (jnp.exp2(u * u * (-0.5 * LOG2E)) * inverse_root_two_pi)
                slope_ref[part, :] = slope.astype(BF)
                total = dotf(act, dn[...], 1, 0)
                if acc:
                    total = total + acc[0][part, :]
                if low:
                    total_refs[i][...] = total.astype(BF)
                else:
                    total_refs[0][part, :] = total

    result = list(order(kernel, tuple(outs), tuple(args), "ffn_fwd", 8, aliases))
    out = []
    for _ in seqs:
        out.append((result[: 1 + low], result[1 + low : 3 + low]))
        result = result[3 + low :]
    return out


def ffn_bwd(order, seqs, up, dn, low=False):
    width = dn.shape[1]
    counts, args, outs, aliases = [], [up, dn], [], {}
    rows = seqs[0][1].shape[0]
    for g, slope, acc in seqs:
        counts += [len(g), 1, acc is not None]
        args += [*g, slope]
        if acc is not None:
            if not low:
                aliases[len(args)] = len(outs)
            args.append(acc)
        outs += [*((((rows // 2, width), BF),) * 2 if low else (((rows, width), F32),)), (slope.shape, BF)]

    def kernel(up, dn, *refs):
        ins = split_refs(refs[: sum(counts)], counts)
        results = refs[sum(counts) :]
        for index in range(len(seqs)):
            g, (slope,), acc = ins[3 * index : 3 * index + 3]
            total_refs, results = results[: 1 + low], results[1 + low :]
            d_ref, *results = results
            d_up = (dotf(whole(g), dn[...], 1, 1) * slope[...].astype(F32)).astype(BF)
            d_ref[...] = d_up
            total = dotf(d_up, up[0:width, :], 1, 1)
            if acc:
                total = total + acc[0][...]
            if low:
                total_refs[0][...] = total[: rows // 2].astype(BF)
                total_refs[1][...] = total[rows // 2 :].astype(BF)
            else:
                total_refs[0][...] = total

    result = list(order(kernel, tuple(outs), tuple(args), "ffn_bwd", 8, aliases))
    out = []
    for _ in seqs:
        out.append((result[: 1 + low], result[1 + low]))
        result = result[2 + low :]
    return out


def standard(v):
    centered = v - jnp.mean(v, -1, keepdims=True)
    inv = lax.rsqrt(jnp.mean(centered * centered, -1, keepdims=True) + norm_epsilon)
    return centered * inv, inv


def back_through(g, scaled, inv, gain):
    e = g * gain
    return inv * (e - jnp.mean(e, -1, keepdims=True) - scaled * jnp.mean(e * scaled, -1, keepdims=True))


def half_of(refs, i):
    per = refs[0].shape[0] // 128
    return refs[i // per][(i % per) * 128 : (i % per + 1) * 128, :]


def first_norm(order, x, acc, got, b_out, gain, bias, b_down):
    rows, width = x.shape

    def kernel(x_ref, acc_ref, got_ref, b_out, gain, bias, b_down, sum_ref, out_ref, low_a, low_b, low_t):
        for i in range(rows // 128):
            part = slice(i * 128, (i + 1) * 128)
            total = x_ref[part, :].astype(F32) + b_out[...].astype(F32)
            total = total + acc_ref[part, :] + got_ref[part, :].astype(F32)
            sum_ref[part, :] = total
            scaled, _ = standard(total)
            normed = scaled * gain[...] + bias[...]
            out_ref[part, :] = normed + b_down[...].astype(F32)
            low = normed.astype(BF)
            place = (i * 128) % (rows // 2)
            (low_a, low_b)[i * 256 // rows][place : place + 128, :] = low
            low_t[:, part] = low.astype(F32).T.astype(BF)

    half = ((rows // 2, width), BF)
    outs = (((rows, width), F32), ((rows, width), F32), half, half, ((width, rows), BF))
    args = (x, acc, got, b_out[None], gain[None], bias[None], b_down[None])
    return order(kernel, outs, args, "first_norm", 14, {1: 0})


def emit_back(i, carry, g, scaled, inv, gain, out_ref, low_halves, low_t):
    part = slice(i * 128, (i + 1) * 128)
    d_rows = back_through(g, scaled, inv, gain)
    out_ref[part, :] = d_rows
    low = d_rows.astype(BF)
    half = low_halves[0].shape[0]
    place = (i * 128) % half
    low_halves[i * 128 // half][place : place + 128, :] = low
    low = low.astype(F32)
    low_t[:, part] = low.T.astype(BF)
    terms = (g * scaled, g, low)
    return tuple(c + jnp.sum(t, 0, keepdims=True) for c, t in zip(carry, terms))


def put_sums(sums_ref, carry):
    row = lax.broadcasted_iota(jnp.int32, sums_ref.shape, 0)
    sums_ref[...] = jnp.where(row == 0, carry[0], jnp.where(row == 1, carry[1], jnp.where(row == 2, carry[2], 0.0)))


def back_outs(rows, width):
    half = ((rows // 2, width), BF)
    return (((rows, width), F32), half, half, ((width, rows), BF), ((8, width), F32))


def second_norm(order, total, got, cotangent, gain, bias):
    rows, width = total.shape

    def kernel(sum_ref, got_a, got_b, cot_ref, gain, bias, d_ref, low_a, low_b, low_t, sums_ref, y_ref):
        carry = (jnp.zeros((1, width), F32),) * 3
        for i in range(rows // 128):
            part = slice(i * 128, (i + 1) * 128)
            scaled, inv = standard(sum_ref[part, :] + half_of((got_a, got_b), i).astype(F32))
            y_ref[part, :] = (scaled * gain[...] + bias[...]).astype(BF)
            g = cot_ref[part, :].astype(F32)
            carry = emit_back(i, carry, g, scaled, inv, gain[...], d_ref, (low_a, low_b), low_t)
        put_sums(sums_ref, carry)

    outs = (*back_outs(rows, width), ((rows, width), BF))
    return order(kernel, outs, (total, *got, cotangent, gain[None], bias[None]), "second_norm", 14, {0: 0})


def first_back(order, first, gain, d_normed, got):
    rows, width = first.shape

    def kernel(sum_ref, gain, d_ref, got_a, got_b, out_ref, low_a, low_b, low_t, sums_ref):
        carry = (jnp.zeros((1, width), F32),) * 3
        for i in range(rows // 128):
            part = slice(i * 128, (i + 1) * 128)
            scaled, inv = standard(sum_ref[part, :])
            g = d_ref[part, :] + half_of((got_a, got_b), i).astype(F32)
            carry = emit_back(i, carry, g, scaled, inv, gain[...], out_ref, (low_a, low_b), low_t)
        put_sums(sums_ref, carry)

    return order(kernel, back_outs(rows, width), (first, gain[None], d_normed, *got), "first_back", 14, {2: 0})

CORE = [(d, d ^ 1) for d in range(8)]
ROW = [(t, t ^ 1) for t in range(4)]
COL = [(t, t ^ 2) for t in range(4)]
NEAR = [(d, d ^ 2) for d in range(8)]
FAR = [(d, d ^ 4) for d in range(8)]


def swap_core(v):
    return lax.ppermute(v, "dp", CORE)


def swap_row(v):
    return lax.ppermute(v, "tensor", ROW)


def swap_col(v):
    return lax.ppermute(v, "tensor", COL)


def swap_near(v):
    return lax.ppermute(v, "dp", NEAR)


def swap_far(v):
    return lax.ppermute(v, "dp", FAR)


class Piece:
    def __init__(self, order, odd):
        self.order, self.odd = order, odd
        self.mine = [None] * 4

    def diagonal(self, top, bottom):
        self.top, self.bottom = swap_row(top), swap_col(bottom)

    def direct(self, row_part, col_part):
        self.row_part, self.col_part = swap_row(row_part), swap_col(col_part)

    def along_z(self, keep, send):
        self.keep, self.got = keep, swap_near(send)

    def second(self):
        self.keep = self.order.add(self.got, self.keep)
        self.got = swap_far(self.keep)

    def third(self):
        self.keep = self.order.add(self.got, self.keep)

    def fourth(self):
        self.got = swap_near(self.order.now(self.keep))

    def kept(self):
        self.keep_o = swap_core(self.order.now(self.keep))

    def last(self):
        self.got_o = swap_core(self.order.now(self.got))

    def all(self):
        return self.keep, self.keep_o, self.got, self.got_o


def fast(
    layer_input,
    segment_ids,
    w_qkv,
    b_qv,
    w_out,
    b_out,
    ln1_gain,
    ln1_bias,
    w_up,
    b_up,
    w_down,
    b_down,
    ln2_gain,
    ln2_bias,
    cotangent,
):
    rows, width = layer_input.shape
    hidden = w_up.shape[1] // 2
    core = lax.axis_index("dp") % 2
    odd_index = (lax.axis_index("dp") // 2) % 2
    odd = odd_index.astype(jnp.int32)[None]
    core = core.astype(jnp.int32)[None]
    order = Order()
    now, wait = order.now, order.wait

    segment = lax.dynamic_index_in_dim(segment_ids, lax.axis_index("tensor"), keepdims=False)
    inputs = ((layer_input,), (swap_core(layer_input),))
    qk, vo, up_w, dn_w = [None] * 4, [None] * 4, [None] * 4, [None] * 4
    qk[0], vo[0] = pack_attn(order, core, w_qkv, w_out, b_qv)
    qk[1], qk[2] = swap_row(qk[0]), swap_col(qk[0])
    vo[1], vo[2] = swap_row(vo[0]), swap_col(vo[0])
    up_w[0], dn_w[0] = pack_ffn(order, core, w_up, b_up[None], w_down)

    masks = [
        jnp.where(ids[:, None] == ids[None, :], 0.0, -1e30).astype(F32) for ids in (segment, swap_core(segment))
    ]
    total = [None, None]
    saved = [[None, None] for _ in range(4)]

    def attend(r, which, low=False):
        found = attn_fwd(order, [(inputs[s], masks[s], total[s], low) for s in which], qk[r], vo[r])
        for s, (total[s], saved[r][s]) in zip(which, found):
            continue

    attend(0, (0, 1))
    qk[3], vo[3] = swap_row(now(qk[2])), swap_col(now(vo[1]))
    attend(1, (0, 1))
    up_w[1], up_w[2] = swap_row(now(up_w[0])), swap_col(now(up_w[0]))
    attend(2, (0, 1))
    attend(3, (1,), True)
    got = swap_core(total[1])
    attend(3, (0,))
    dn_w[1], dn_w[2] = swap_row(now(dn_w[0])), swap_col(now(dn_w[0]))
    wait(up_w[1], up_w[2])
    first, branch, *low, normed_t = first_norm(
        order, layer_input, total[0], got, b_out, ln1_gain, ln1_bias, b_down
    )
    normed = (tuple(low), tuple(swap_core(v) for v in low))
    total = [branch, None]
    acts = [[None, None] for _ in range(4)]
    slopes = [[None, None] for _ in range(4)]

    def expand(r, which, low=False):
        found = ffn_fwd(order, [(normed[s], total[s]) for s in which], up_w[r], dn_w[r], low)
        for s, (total[s], (acts[r][s], slopes[r][s])) in zip(which, found):
            total[s] = total[s] if low else total[s][0]

    expand(0, (0,))
    expand(0, (1,))
    wait(dn_w[1], dn_w[2])
    normed_t = (normed_t, flip(order, normed[1]))
    up_w[3], dn_w[3] = swap_row(now(up_w[2])), swap_col(now(dn_w[1]))
    expand(1, (0, 1))
    expand(2, (0, 1))
    expand(3, (1,), True)
    got = [swap_core(v) for v in total[1]]
    expand(3, (0,))
    d_second, *low, branch_t, sums_two, output = second_norm(order, total[0], got, cotangent, ln2_gain, ln2_bias)
    branch_low = (tuple(low), tuple(swap_core(v) for v in low))

    down, up = Piece(order, odd), Piece(order, odd)
    attn, attn_qk, attn_vo = Piece(order, odd), Piece(order, odd), Piece(order, odd)
    total = [d_second, None]
    d_up = [[None, None] for _ in range(4)]

    def back(r, which, low=False):
        found = ffn_bwd(order, [(branch_low[s], slopes[r][s], total[s]) for s in which], up_w[r], dn_w[r], low)
        for s, (total[s], d_up[r][s]) in zip(which, found):
            total[s] = total[s] if low else total[s][0]

    def grad_down(r, got=(), split=False, z=None):
        return outer(order, branch_t, acts[r], got, split, "grad_down", False, z)

    def grad_up(r, got=(), split=False, z=None):
        return outer(order, normed_t, d_up[r], got, split, "grad_up", True, z)

    back(3, (0,))
    branch_t = (branch_t, flip(order, branch_low[1]))
    down.diagonal(*grad_down(3, split=True))
    back(3, (1,))
    up.diagonal(*grad_up(3, split=True))
    back(1, (0, 1))
    back(2, (0, 1))
    down_row, down_col = grad_down(1)[0], grad_down(2)[0]
    down.direct(*pass_on(order, down_row, down.bottom, down_col, down.top))
    back(0, (1,), True)
    got = [swap_core(v) for v in total[1]]
    back(0, (0,))
    d_first, *low, attention_t, sums_one = first_back(order, first, ln1_gain, total[0], got)
    attention_low = (tuple(low), tuple(swap_core(v) for v in low))
    inputs_t = [flip(order, inputs[s]) for s in (0, 1)]
    attention_t = (attention_t, flip(order, attention_low[1]))
    total = [d_first, None]

    def attend_back(r, low=False):
        seqs = [
            (attention_low[s], attention_t[s], inputs_t[s], *saved[r][s], total[s]) for s in (0, 1)
        ]
        total[0], total[1], attn_qk.mine[r], attn_vo.mine[r] = attn_bwd(order, seqs, qk[r], vo[r], low)

    up_row, up_col = grad_up(1, split=True), grad_up(2, split=True)
    down_own = grad_down(0)[0]
    down.along_z(*sum_halves(order, odd, down_own, down.row_part, down.col_part))
    low_row, high_col = add_pair(order, up_row[1], up.bottom, up_col[0], up.top)
    up_rows, up_cols = [swap_row(v) for v in (up_row[0], low_row)], [swap_col(v) for v in (high_col, up_col[1])]
    down.second()
    attend_back(3)
    qk_diag, vo_diag = swap_row(attn_qk.mine[3]), swap_col(attn_vo.mine[3])
    attend_back(1)
    arrived = [(kind, v) for part in (up_rows, up_cols) for kind, v in zip(("top", "bottom"), part)]
    up.along_z(*grad_up(0, arrived, True, odd))
    attend_back(2)
    down.third()
    up.second()
    row, col = relay(order, attn_qk.mine[1], attn_vo.mine[1], vo_diag, attn_qk.mine[2], attn_vo.mine[2], qk_diag)
    row, col = swap_row(row), swap_col(col)
    down.fourth()
    attend_back(0, True)
    wait(down.got)
    attn.along_z(*own_sum(order, odd, attn_qk.mine[0], attn_vo.mine[0], row, col))
    up.third()
    small = jnp.concatenate([sums_one, sums_two], 0)
    small = order.add(swap_core(now(small)), small)
    small = order.add(swap_row(small), small)
    small = order.add(swap_col(small), small)
    small_near = swap_near(small)
    attn.second()
    up.fourth()
    down.kept()
    down.last()
    got = swap_core(now(total[1]))
    grad_w_down = finish_down(order, core, odd, down.all())
    grad_input = order.add(got, total[0])
    small = order.add(small_near, small)
    wait(up.got)
    attn.third()
    attn.fourth()
    small_far = swap_far(now(small))
    attn.kept()
    up.kept()
    up.last()
    grad_b_up, grad_w_up = finish_up(order, core, odd, up.all())
    small = order.add(small_far, small)
    attn.last()
    grad_w_qkv, grad_b_qv, grad_w_out = finish_attn(order, core, odd, attn.all())
    return (
        output,
        grad_input,
        grad_w_qkv,
        grad_b_qv,
        grad_w_out,
        small[2],
        small[0],
        small[1],
        grad_w_up,
        grad_b_up[0],
        grad_w_down,
        small[10],
        small[8],
        small[9],
    )


def local(*arrays):
    my_rows = arrays[0].shape[0]
    seq_len = arrays[1].shape[1]
    grid = (lax.axis_size("dp"), lax.axis_size("tensor"))
    if grid == (8, 4) and my_rows == seq_len and arrays[4].shape[0] == 4 * HEAD_DIM:
        return fast(*arrays)
    return general(*arrays)


def solution(mesh):
    return jax.shard_map(
        local,
        mesh=mesh,
        in_specs=(
            P(("dp", "tensor"), None),
            P("dp", None),
            P(None, None, "tensor"),
            P(None, "tensor"),
            P("tensor", None),
            P(),
            P(),
            P(),
            P(None, "tensor"),
            P("tensor"),
            P("tensor", None),
            P(),
            P(),
            P(),
            P(("dp", "tensor"), None),
        ),
        out_specs=(
            P(("dp", "tensor"), None),
            P(("dp", "tensor"), None),
            P(None, None, "tensor"),
            P(None, "tensor"),
            P("tensor", None),
            P(),
            P(),
            P(),
            P(None, "tensor"),
            P("tensor"),
            P("tensor", None),
            P(),
            P(),
            P(),
        ),
        check_vma=False,
    )
```

```python
import jax
import jax.numpy as jnp
from jax import lax
from jax.experimental import pallas as pl
from jax.experimental.pallas import tpu as pltpu
from jax.sharding import PartitionSpec as P

HEAD_DIM = 64


norm_epsilon = 1e-05
root_half = 0.7071067811865476
inverse_root_two_pi = 0.3989422804014327


def layer_norm(token_rows, norm_gain, norm_bias):
    row_mean = jnp.mean(token_rows, -1, keepdims=True)
    centered = token_rows - row_mean
    variance = jnp.mean(centered * centered, -1, keepdims=True)
    inv_std = lax.rsqrt(variance + norm_epsilon)
    scaled = centered * inv_std
    return (scaled * norm_gain + norm_bias, scaled, inv_std)


def norm_back(incoming, scaled, inv_std, norm_gain):
    weighted = incoming * norm_gain
    d_rows = inv_std * (
        weighted
        - jnp.mean(weighted, -1, keepdims=True)
        - scaled * jnp.mean(weighted * scaled, -1, keepdims=True)
    )
    return (d_rows, jnp.sum(incoming * scaled, 0), jnp.sum(incoming, 0))


def gelu_value(up_proj):
    return 0.5 * up_proj * (1.0 + lax.erf(up_proj * root_half))


def gelu_slope(up_proj):
    return (
        0.5 * (1.0 + lax.erf(up_proj * root_half))
        + up_proj * jnp.exp(-0.5 * up_proj * up_proj) * inverse_root_two_pi
    )


def split_heads(matrix, head_count):
    return matrix.reshape(matrix.shape[0], head_count, -1)


def project(token_rows, w_qkv, b_qv):
    queries = (
        jnp.dot(token_rows, w_qkv[0], preferred_element_type=jnp.float32)
        + b_qv[0].astype(jnp.float32)
    ).astype(jnp.bfloat16)
    keys_low = jnp.dot(token_rows, w_qkv[1], preferred_element_type=jnp.float32).astype(
        jnp.bfloat16
    )
    values = (
        jnp.dot(token_rows, w_qkv[2], preferred_element_type=jnp.float32)
        + b_qv[1].astype(jnp.float32)
    ).astype(jnp.bfloat16)
    return (queries, keys_low, values)


def scores(queries, keys_low, segment, head_count, score_scale):
    raw = jnp.einsum(
        "qhd,khd->hqk",
        split_heads(queries, head_count),
        split_heads(keys_low, head_count),
        preferred_element_type=jnp.float32,
    )
    same_doc = segment[:, None] == segment[None, :]
    return jnp.where(same_doc[None], raw * score_scale, -1e30)


def mix_values(prob_low, values, head_count):
    context = jnp.einsum(
        "hqk,khd->qhd",
        prob_low,
        split_heads(values, head_count),
        preferred_element_type=jnp.float32,
    )
    return context.reshape(context.shape[0], -1).astype(jnp.bfloat16)


def ffn_forward(normed_low, up_weight, up_bias, down_weight):
    up_proj = jnp.dot(normed_low, up_weight, preferred_element_type=jnp.float32) + up_bias.astype(
        jnp.float32
    )
    activation = gelu_value(up_proj).astype(jnp.bfloat16)
    return jnp.dot(activation, down_weight, preferred_element_type=jnp.float32)


def ffn_backward(normed_low, branch_low, up_weight, up_bias, down_weight):
    up_proj = jnp.dot(normed_low, up_weight, preferred_element_type=jnp.float32) + up_bias.astype(
        jnp.float32
    )
    activation = gelu_value(up_proj).astype(jnp.bfloat16)
    grad_down = jnp.einsum("tf,td->fd", activation, branch_low, preferred_element_type=jnp.float32)
    d_activation = jnp.einsum(
        "td,fd->tf", branch_low, down_weight, preferred_element_type=jnp.float32
    )
    d_up = (d_activation * gelu_slope(up_proj)).astype(jnp.bfloat16)
    grad_up = jnp.einsum("td,tf->df", normed_low, d_up, preferred_element_type=jnp.float32)
    grad_up_bias = jnp.sum(d_up.astype(jnp.float32), 0)
    return (grad_up, grad_up_bias, grad_down, d_up)


def general(
    layer_input,
    segment_ids,
    w_qkv,
    b_qv,
    w_out,
    b_out,
    ln1_gain,
    ln1_bias,
    w_up,
    b_up,
    w_down,
    b_down,
    ln2_gain,
    ln2_bias,
    cotangent,
):
    my_rows, model_width = layer_input.shape
    seq_len = segment_ids.shape[1]
    score_scale = HEAD_DIM ** (-0.5)
    whole_input = lax.all_gather(layer_input, "tensor", axis=0, tiled=True)
    seq_input = whole_input.reshape(segment_ids.shape[0], seq_len, model_width)
    attn_width = w_out.shape[0]
    head_count = attn_width // HEAD_DIM

    def forward_seq(running, seq_item):
        token_rows, segment = seq_item
        queries, keys_low, values = project(token_rows, w_qkv, b_qv)
        logits = scores(queries, keys_low, segment, head_count, score_scale)
        row_max = jnp.max(logits, -1, keepdims=True)
        exponent = jnp.exp(logits - row_max)
        expo_sum = jnp.sum(exponent, -1, keepdims=True)
        prob_low = (exponent / expo_sum).astype(jnp.bfloat16)
        return (running, (mix_values(prob_low, values, head_count), row_max + jnp.log(expo_sum)))

    _, (seq_context, seq_lse) = lax.scan(forward_seq, None, (seq_input, segment_ids))
    all_context = seq_context.reshape(-1, attn_width)
    attention = lax.psum_scatter(
        jnp.dot(all_context, w_out, preferred_element_type=jnp.float32),
        "tensor",
        scatter_dimension=0,
        tiled=True,
    ) + b_out.astype(jnp.float32)
    normed_one, scaled_one, inv_one = layer_norm(
        layer_input.astype(jnp.float32) + attention, ln1_gain, ln1_bias
    )
    normed_low = normed_one.astype(jnp.bfloat16)
    whole_normed = lax.all_gather(normed_low, "tensor", axis=0, tiled=True)
    branch = lax.psum_scatter(
        ffn_forward(whole_normed, w_up, b_up, w_down), "tensor", scatter_dimension=0, tiled=True
    )
    normed_two, scaled_two, inv_two = layer_norm(
        normed_one + branch + b_down.astype(jnp.float32), ln2_gain, ln2_bias
    )
    d_second, grad_ln2_gain, grad_ln2_bias = norm_back(
        cotangent.astype(jnp.float32), scaled_two, inv_two, ln2_gain
    )
    branch_low = d_second.astype(jnp.bfloat16)
    grad_b_down = jnp.sum(branch_low.astype(jnp.float32), 0)
    whole_branch = lax.all_gather(branch_low, "tensor", axis=0, tiled=True)
    grad_w_up, grad_b_up, grad_w_down, d_up = ffn_backward(
        whole_normed, whole_branch, w_up, b_up, w_down
    )
    d_normed = lax.psum_scatter(
        jnp.einsum("tf,df->td", d_up, w_up, preferred_element_type=jnp.float32),
        "tensor",
        scatter_dimension=0,
        tiled=True,
    )
    d_first, grad_ln1_gain, grad_ln1_bias = norm_back(
        d_second + d_normed, scaled_one, inv_one, ln1_gain
    )
    attention_low = d_first.astype(jnp.bfloat16)
    grad_b_out = jnp.sum(attention_low.astype(jnp.float32), 0)
    whole_grad = lax.all_gather(attention_low, "tensor", axis=0, tiled=True)
    seq_grad = whole_grad.reshape(seq_input.shape[0], seq_len, model_width)

    def backward_seq(running, seq_item):
        grad_qkv, grad_bias, grad_out = running
        token_rows, segment, seq_lse_one, grad_rows = seq_item
        queries, keys_low, values = project(token_rows, w_qkv, b_qv)
        logits = scores(queries, keys_low, segment, head_count, score_scale)
        probability = jnp.exp(logits - seq_lse_one)
        prob_low = probability.astype(jnp.bfloat16)
        context = mix_values(prob_low, values, head_count)
        grad_out = grad_out + jnp.einsum(
            "te,td->ed", context, grad_rows, preferred_element_type=jnp.float32
        )
        d_context = jnp.einsum(
            "td,ed->te", grad_rows, w_out, preferred_element_type=jnp.float32
        ).astype(jnp.bfloat16)
        d_heads = split_heads(d_context, head_count)
        d_prob = jnp.einsum(
            "qhd,khd->hqk",
            d_heads,
            split_heads(values, head_count),
            preferred_element_type=jnp.float32,
        )
        d_values = (
            jnp.einsum("hqk,qhd->khd", prob_low, d_heads, preferred_element_type=jnp.float32)
            .reshape(seq_len, -1)
            .astype(jnp.bfloat16)
        )
        inner_sum = jnp.sum(probability * d_prob, -1, keepdims=True)
        d_raw = (probability * (d_prob - inner_sum) * score_scale).astype(jnp.bfloat16)
        d_queries = (
            jnp.einsum(
                "hqk,khd->qhd",
                d_raw,
                split_heads(keys_low, head_count),
                preferred_element_type=jnp.float32,
            )
            .reshape(seq_len, -1)
            .astype(jnp.bfloat16)
        )
        d_keys = (
            jnp.einsum(
                "hqk,qhd->khd",
                d_raw,
                split_heads(queries, head_count),
                preferred_element_type=jnp.float32,
            )
            .reshape(seq_len, -1)
            .astype(jnp.bfloat16)
        )
        grad_qkv = grad_qkv + jnp.stack(
            [
                jnp.einsum("td,te->de", token_rows, gradient, preferred_element_type=jnp.float32)
                for gradient in (d_queries, d_keys, d_values)
            ]
        )
        grad_bias = grad_bias + jnp.stack(
            [jnp.sum(d_queries.astype(jnp.float32), 0), jnp.sum(d_values.astype(jnp.float32), 0)]
        )
        return ((grad_qkv, grad_bias, grad_out), (d_queries, d_keys, d_values))

    start_grads = (
        jnp.zeros((3, model_width, attn_width), jnp.float32),
        jnp.zeros((2, attn_width), jnp.float32),
        jnp.zeros((attn_width, model_width), jnp.float32),
    )
    (grad_w_qkv, grad_b_qv, grad_w_out), seq_d = lax.scan(
        backward_seq, start_grads, (seq_input, segment_ids, seq_lse, seq_grad)
    )
    all_d = [gradient.reshape(-1, attn_width) for gradient in seq_d]
    summed = jnp.zeros((my_rows * lax.axis_size("tensor"), model_width), jnp.float32)
    for which in range(3):
        piece = all_d[which]
        summed = summed + jnp.einsum(
            "te,de->td", piece, w_qkv[which], preferred_element_type=jnp.float32
        )
    grad_input = d_first + lax.psum_scatter(
        summed.astype(jnp.bfloat16), "tensor", scatter_dimension=0, tiled=True
    ).astype(jnp.float32)
    grad_w_qkv, grad_b_qv, grad_w_out, grad_w_up, grad_b_up, grad_w_down = (
        lax.psum(grad_w_qkv.astype(jnp.bfloat16), "dp").astype(jnp.float32),
        lax.psum(grad_b_qv.astype(jnp.bfloat16), "dp").astype(jnp.float32),
        lax.psum(grad_w_out.astype(jnp.bfloat16), "dp").astype(jnp.float32),
        lax.psum(grad_w_up.astype(jnp.bfloat16), "dp").astype(jnp.float32),
        lax.psum(grad_b_up.astype(jnp.bfloat16), "dp").astype(jnp.float32),
        lax.psum(grad_w_down.astype(jnp.bfloat16), "dp").astype(jnp.float32),
    )
    grad_b_out, grad_ln1_gain, grad_ln1_bias, grad_b_down, grad_ln2_gain, grad_ln2_bias = lax.psum(
        (grad_b_out, grad_ln1_gain, grad_ln1_bias, grad_b_down, grad_ln2_gain, grad_ln2_bias),
        ("dp", "tensor"),
    )
    return (
        normed_two.astype(jnp.bfloat16),
        grad_input,
        grad_w_qkv,
        grad_b_qv,
        grad_w_out,
        grad_b_out,
        grad_ln1_gain,
        grad_ln1_bias,
        grad_w_up,
        grad_b_up,
        grad_w_down,
        grad_b_down,
        grad_ln2_gain,
        grad_ln2_bias,
    )


F32 = jnp.float32
BF = jnp.bfloat16
LOG2E = 1.4426950408889634


def dotf(a, b, ca, cb):
    return lax.dot_general(a, b, (((ca,), (cb,)), ((), ())), preferred_element_type=F32)


class Order:
    def __init__(self):
        self.token, self.waited = None, []

    def wait(self, *values):
        self.waited.extend(values)

    def __call__(self, kernel, outs, args, name, limit, aliases=None, smem=0):
        count = len(args)
        specs = [pl.BlockSpec(memory_space=pltpu.SMEM)] * smem + [pl.BlockSpec()] * (count - smem)
        unread = ([] if self.token is None else [self.token]) + self.waited
        specs += [pl.BlockSpec(memory_space=pltpu.HBM)] * len(unread)
        self.waited = []
        args = (*args, *unread)

        def body(*refs):
            kernel(*refs[:count], *refs[len(args) : -1])
            refs[-1][...] = jnp.zeros((8, 128), F32)

        *result, self.token = pl.pallas_call(
            body,
            out_shape=tuple(jax.ShapeDtypeStruct(s, d) for s, d in (*outs, ((8, 128), F32))),
            in_specs=specs,
            input_output_aliases=aliases or {},
            compiler_params=pltpu.CompilerParams(vmem_limit_bytes=limit << 20),
            cost_estimate=pl.CostEstimate(flops=1, bytes_accessed=1, transcendentals=0),
            name=name,
        )(*args)
        return result

    def add(self, a, b):
        def kernel(a_ref, b_ref, out):
            out[...] = (a_ref[...].astype(F32) + b_ref[...].astype(F32)).astype(out.dtype)

        return self(kernel, ((b.shape, b.dtype),), (a, b), "add", 8)[0]

    def now(self, value):
        return lax.optimization_barrier((value, self.token))[0]


def pack_attn(order, core, w_qkv, w_out, b_qv):
    width = w_qkv.shape[1]

    def kernel(core, w_qkv, w_out, b_qv, qk, vo, token, rows, done):
        part = pl.ds(pl.multiple_of(core[0] * 128, 128), 128)
        places = (qk.at[0:width, 0:128], qk.at[0:width, 128:256], vo.at[0:width, 0:128])
        copies = [pltpu.make_async_copy(w_out.at[part, :], rows, done.at[3])]
        copies += [pltpu.make_async_copy(w_qkv.at[i, :, part], place, done.at[i]) for i, place in enumerate(places)]
        for copy in copies:
            copy.start()
        zero = jnp.zeros((16, 128), BF)
        first = lax.broadcasted_iota(jnp.int32, (16, 128), 0) == 0
        for i, out in enumerate((qk, vo)):
            out[width : width + 16, 0:128] = jnp.where(first, b_qv[i : i + 1, part].astype(F32), 0.0).astype(BF)
            out[width : width + 16, 128:256] = zero
        token[...] = jnp.zeros((8, 128), F32)
        copies[0].wait()
        vo[0:width, 128:256] = rows[...].astype(F32).T.astype(BF)
        for copy in copies[1:]:
            copy.wait()

    out = jax.ShapeDtypeStruct((width + 16, 256), BF)
    hbm = pl.BlockSpec(memory_space=pltpu.HBM)
    qk, vo, order.token = pl.pallas_call(
        kernel,
        out_shape=(out, out, jax.ShapeDtypeStruct((8, 128), F32)),
        in_specs=[pl.BlockSpec(memory_space=pltpu.SMEM), hbm, hbm, pl.BlockSpec()],
        scratch_shapes=[pltpu.VMEM((128, w_out.shape[1]), BF), pltpu.SemaphoreType.DMA((4,))],
        compiler_params=pltpu.CompilerParams(vmem_limit_bytes=58 << 20),
        cost_estimate=pl.CostEstimate(flops=1, bytes_accessed=1, transcendentals=0),
        name="pack_attn",
    )(core, w_qkv, w_out, b_qv)
    return qk, vo


def pack_ffn_kernel(core, w_up, b_up, w_down, up, dn):
    width = w_up.shape[0]
    hid = w_up.shape[1] // 2
    first = lax.broadcasted_iota(jnp.int32, (16, hid), 0) == 0
    part = pl.ds(pl.multiple_of(core[0] * hid, hid), hid)
    up[0:width, :] = w_up[:, part]
    up[width : width + 16, :] = jnp.where(first, b_up[0:1, part].astype(F32), 0.0).astype(BF)
    dn[...] = w_down[part, :]


def pack_ffn(order, core, w_up, b_up, w_down):
    width, hid = w_up.shape[0], w_up.shape[1] // 2
    outs = (((width + 16, hid), BF), ((hid, width), BF))
    return order(pack_ffn_kernel, outs, (core, w_up, b_up, w_down), "pack_ffn", 12, smem=1)


def flip(order, matrix):
    width = matrix[0].shape[1]

    def kernel(*refs):
        start = 0
        for ref in refs[:-1]:
            rows = ref.shape[0]
            refs[-1][:, start : start + rows] = ref[...].astype(F32).T.astype(BF)
            start += rows

    rows = sum(m.shape[0] for m in matrix)
    return order(kernel, (((width, rows), BF),), tuple(matrix), "flip", 8)[0]


def take(refs, part):
    if len(refs) == 1:
        return refs[0][part, :]
    half = refs[0].shape[0]
    return refs[part.start // half][part.start % half : (part.stop - 1) % half + 1, :]


def whole(refs):
    return refs[0][...] if len(refs) == 1 else jnp.concatenate([r[...] for r in refs], 0)


def split_refs(refs, counts):
    out = []
    for count in counts:
        out.append(refs[:count])
        refs = refs[count:]
    return out


def attn_fwd(order, seqs, qk, vo):
    rows = sum(m.shape[0] for m in seqs[0][0])
    width = qk.shape[0] - 16
    counts, args, outs, aliases = [], [qk, vo], [], {}
    pt, qkv, ctx = ((2, rows, rows), BF), ((3, rows, 128), BF), ((rows, 128), BF)
    for x, mask, acc, low in seqs:
        counts += [len(x), 1, acc is not None]
        args += [*x, mask]
        if acc is not None:
            if not low:
                aliases[len(args)] = len(outs)
            args.append(acc)
        outs += [((rows, width), BF if low else F32), pt, qkv, ctx]

    def kernel(qk, vo, *refs):
        ins = split_refs(refs[: sum(counts)], counts)
        results = refs[sum(counts) :]
        row = lax.broadcasted_iota(jnp.int32, (128, rows), 0)
        for index, (_, _, _, low) in enumerate(seqs):
            x_refs, (mask,), acc = ins[3 * index : 3 * index + 3]
            (total_ref, pt, qkv, ctx_ref), results = results[:4], results[4:]
            x = whole(x_refs)
            qkf = dotf(x, qk[0:width, :], 1, 0) + qk[width : width + 16, :][0:1, :].astype(F32)
            vf = dotf(x, vo[0:width, 0:128], 1, 0) + vo[width : width + 16, 0:128][0:1, :].astype(F32)
            k = qkf[:, 128:].astype(BF)
            qkv[0] = qkf[:, :128].astype(BF)
            qkv[1] = k
            qkv[2] = vf.astype(BF)
            q_t = qkf[:, :128].T.astype(BF)
            v_t = vf.T.astype(BF)
            parts = []
            for h in range(2):
                q_h = jnp.where((row // HEAD_DIM) == h, q_t, jnp.zeros_like(q_t))
                s = dotf(k, q_h, 1, 0) * (HEAD_DIM**-0.5 * LOG2E) + mask[...]
                e = jnp.exp2(s - jnp.max(s, 0, keepdims=True))
                p = (e * (1.0 / jnp.sum(e, 0, keepdims=True))).astype(BF)
                pt[h] = p
                parts.append(dotf(v_t[h * HEAD_DIM : (h + 1) * HEAD_DIM, :], p, 1, 0))
            ctx = jnp.concatenate(parts, 0).T.astype(BF)
            ctx_ref[...] = ctx
            total = dotf(ctx, vo[0:width, 128:256], 1, 1)
            if acc:
                total = total + acc[0][...]
            total_ref[...] = total.astype(total_ref.dtype)

    result = list(order(kernel, tuple(outs), tuple(args), "attn_fwd", 8, aliases))
    out = []
    for _ in seqs:
        out.append((result[0], result[1:4]))
        result = result[4:]
    return out


def part_rows(part, half, extra):
    whole = ((0, half), (half + extra, 2 * half + extra), (2 * half + extra, 2 * half + 2 * extra), (half, half + extra))
    own = ((0, half), (0, half), (half, half + extra), (half, half + extra))
    return whole[part], own[part]


def add_got(value, got, part, half, extra):
    whole, own = part_rows(part, half, extra)
    for kind, ref in got:
        if kind == "whole":
            value = value + ref[whole[0] : whole[1], :].astype(F32)
        elif (kind == "top") == (part == 0):
            value = value + ref[own[0] : own[1], :].astype(F32)
    return value


def put(outs, part, half, extra, value):
    whole, own = part_rows(part, half, extra)
    if len(outs) == 1:
        outs[0][whole[0] : whole[1], :] = value.astype(BF)
    else:
        outs[part in (1, 2)][own[0] : own[1], :] = value.astype(BF)


def gradient_shapes(width, columns, extra, split):
    if split:
        return (((width // 2 + extra, columns), BF),) * 2
    return (((width + 2 * extra, columns), BF),)


def outer(order, left_t, right, got, split, name, bias, odd=None):
    kinds = [kind for kind, _ in got]
    width = left_t[0].shape[0]
    half, extra = width // 2, 16

    def kernel(*refs):
        if odd is not None:
            flag, *refs = refs
        left_refs, right_refs, refs = refs[:2], refs[2:4], refs[4:]
        received = list(zip(kinds, refs))
        outs = refs[len(kinds) :]
        if odd is not None:
            swapped = flag[0] == 1
        values = []
        for part in (0, 1):
            piece = slice(part * half, (part + 1) * half)
            value = dotf(left_refs[0][piece, :], right_refs[0][...], 1, 0)
            value = value + dotf(left_refs[1][piece, :], right_refs[1][...], 1, 0)
            values.append(add_got(value, received, part, half, extra))
        zero = jnp.zeros((extra, values[0].shape[1]), F32)
        row = zero
        if bias:
            first = lax.broadcasted_iota(jnp.int32, zero.shape, 0) == 0
            row = sum(jnp.sum(r[...].astype(F32), 0, keepdims=True) for r in right_refs)
            row = add_got(jnp.where(first, row, 0.0), received, 2, half, extra)
        if odd is None:
            for part in (0, 1):
                put(outs, part, half, extra, values[part])
            put(outs, 2, half, extra, row)
            put(outs, 3, half, extra, zero)
        else:
            outs[0][0:half, :] = jnp.where(swapped, values[1], values[0]).astype(BF)
            outs[1][0:half, :] = jnp.where(swapped, values[0], values[1]).astype(BF)
            outs[0][half:, :] = jnp.where(swapped, row, zero).astype(BF)
            outs[1][half:, :] = jnp.where(swapped, zero, row).astype(BF)

    outs = gradient_shapes(width, right[0].shape[1], extra, split)
    flags = () if odd is None else (odd,)
    args = (*flags, *left_t, *right, *(v for _, v in got))
    return order(kernel, outs, args, name, 8, smem=len(flags))


def pass_on(order, row_part, bottom, col_part, top):
    half = row_part.shape[0] // 2

    def kernel(row_ref, bottom_ref, col_ref, top_ref, row, col):
        row[0:half, :] = row_ref[0:half, :]
        row[half:, :] = (row_ref[half:, :].astype(F32) + bottom_ref[...].astype(F32)).astype(BF)
        col[half:, :] = col_ref[half:, :]
        col[0:half, :] = (col_ref[0:half, :].astype(F32) + top_ref[...].astype(F32)).astype(BF)

    out = (row_part.shape, BF)
    return order(kernel, (out, out), (row_part, bottom, col_part, top), "pass_on", 10)


def add_pair(order, a, b, c, d):
    def kernel(a, b, c, d, first, second):
        first[...] = (a[...].astype(F32) + b[...].astype(F32)).astype(BF)
        second[...] = (c[...].astype(F32) + d[...].astype(F32)).astype(BF)

    return order(kernel, ((a.shape, BF), (c.shape, BF)), (a, b, c, d), "add_pair", 8)


def sum_halves(order, odd, own, row, col):
    half = own.shape[0] // 2

    def kernel(flag, own, row, col, keep, send):
        swapped = flag[0] == 1
        total = own[...].astype(F32) + row[...].astype(F32) + col[...].astype(F32)
        keep[...] = jnp.where(swapped, total[half:], total[:half]).astype(BF)
        send[...] = jnp.where(swapped, total[:half], total[half:]).astype(BF)

    out = ((half, own.shape[1]), BF)
    return order(kernel, (out, out), (odd, own, row, col), "sum_halves", 10, smem=1)


def relay(order, row_qk, row_vo, vo_diag, col_qk, col_vo, qk_diag):
    def kernel(row_qk, row_vo, vo_diag, col_qk, col_vo, qk_diag, row, col):
        row[:, 0:256] = row_qk[...]
        row[:, 256:512] = (row_vo[...].astype(F32) + vo_diag[...].astype(F32)).astype(BF)
        col[:, 0:256] = (col_qk[...].astype(F32) + qk_diag[...].astype(F32)).astype(BF)
        col[:, 256:512] = col_vo[...]

    out = ((row_qk.shape[0], 512), BF)
    return order(kernel, (out, out), (row_qk, row_vo, vo_diag, col_qk, col_vo, qk_diag), "relay", 10)


def own_sum(order, odd, own_qk, own_vo, row, col):
    half = row.shape[0] // 2

    def kernel(flag, own_qk, own_vo, row, col, keep, send):
        swapped = flag[0] == 1
        for own, place in ((own_qk, slice(0, 256)), (own_vo, slice(256, 512))):
            total = own[...].astype(F32) + row[:, place].astype(F32) + col[:, place].astype(F32)
            keep[:, place] = jnp.where(swapped, total[half:], total[:half]).astype(BF)
            send[:, place] = jnp.where(swapped, total[:half], total[half:]).astype(BF)

    out = ((half, 512), BF)
    return order(kernel, (out, out), (odd, own_qk, own_vo, row, col), "own_sum", 12, smem=1)


def final_halves(core, odd, refs):
    keep, keep_o, got, got_o = refs
    second, swapped = core[0] == 1, odd[0] == 1

    def value(ref):
        return ref[...].astype(F32)

    out = []
    for a, b, c, d in ((keep, keep_o, got, got_o), (keep_o, keep, got_o, got)):
        kept = jnp.where(second, value(b), value(a))
        received = jnp.where(second, value(d), value(c))
        out.append((jnp.where(swapped, received, kept), jnp.where(swapped, kept, received)))
    return out


def finish_down(order, core, odd, refs):
    half, columns = refs[0].shape
    half -= 16

    def kernel(core, odd, *refs):
        for i, pair in enumerate(final_halves(core, odd, refs[:4])):
            for j, value in enumerate(pair):
                refs[4][i * columns : (i + 1) * columns, j * half : (j + 1) * half] = value[:half].T

    return order(kernel, (((2 * columns, 2 * half), F32),), (core, odd, *refs), "finish_down", 12, smem=2)[0]


def finish_up(order, core, odd, refs):
    half, columns = refs[0].shape
    half -= 16

    def kernel(core, odd, *refs):
        for i, pair in enumerate(final_halves(core, odd, refs[:4])):
            place = slice(i * columns, (i + 1) * columns)
            for j, value in enumerate(pair):
                refs[5][j * half : (j + 1) * half, place] = value[:half]
            refs[4][0:1, place] = pair[1][half : half + 1]

    outs = (((1, 2 * columns), F32), ((2 * half, 2 * columns), F32))
    return order(kernel, outs, (core, odd, *refs), "finish_up", 12, smem=2)


def finish_attn(order, core, odd, refs):
    half = refs[0].shape[0] - 16

    def kernel(core, odd, *refs):
        w_qkv, b_qv, w_out = refs[4:]
        for i, pair in enumerate(final_halves(core, odd, refs[:4])):
            place = slice(i * 128, (i + 1) * 128)
            for j, value in enumerate(pair):
                rows = slice(j * half, (j + 1) * half)
                for k in range(3):
                    w_qkv[k, rows, place] = value[:half, k * 128 : (k + 1) * 128]
                w_out[place, rows] = value[:half, 384:512].T
            b_qv[0:1, place] = pair[1][half : half + 1, 0:128]
            b_qv[1:2, place] = pair[1][half : half + 1, 256:384]

    outs = (((3, 2 * half, 256), F32), ((2, 256), F32), ((256, 2 * half), F32))
    return order(kernel, outs, (core, odd, *refs), "finish_attn", 12, smem=2)


def attn_bwd(order, seqs, qk, vo, low=False):
    width = qk.shape[0] - 16
    half = width // 2
    rows = seqs[0][1].shape[1]
    counts, args, outs, aliases = [], [qk, vo], [], {}
    for index, (g, gt, xt, pt, qkv, ctx, acc) in enumerate(seqs):
        counts += [len(g), 1, 1, 1, 1, 1, acc is not None]
        args += [*g, gt, xt, pt, qkv, ctx]
        down = low and index == 1
        if acc is not None:
            if not down:
                aliases[len(args)] = len(outs)
            args.append(acc)
        outs.append(((rows, width), BF if down else F32))

    def kernel(qk, vo, *refs):
        ins = split_refs(refs[: sum(counts)], counts)
        totals, outs = refs[sum(counts) : sum(counts) + 2], refs[sum(counts) + 2 :]
        row = lax.broadcasted_iota(jnp.int32, (128, rows), 0)
        lane = lax.broadcasted_iota(jnp.int32, (rows, 128), 1)
        first = lax.broadcasted_iota(jnp.int32, (16, 256), 0) == 0
        dqks, dvs_all, ctxs = [], [], []
        for index in (0, 1):
            g, _, _, (pt_ref,), (qkv_ref,), (ctx_ref,), acc = ins[7 * index : 7 * index + 7]
            ctx = ctx_ref[...]
            d_o = dotf(whole(g), vo[0:width, 128:256], 1, 0).astype(BF)
            d_ot = d_o.astype(F32).T
            prod = d_ot * ctx.astype(F32).T * (HEAD_DIM**-0.5)
            d_ot = (d_ot * (HEAD_DIM**-0.5)).astype(BF)
            k_t = qkv_ref[1].astype(F32).T.astype(BF)
            dvs, dks, dqs = [], [], []
            for h in range(2):
                head = slice(h * HEAD_DIM, (h + 1) * HEAD_DIM)
                inner = jnp.sum(prod[head, :], 0, keepdims=True)
                p = pt_ref[h]
                dvs.append(dotf(p, d_o, 1, 0))
                d_h = jnp.where((row // HEAD_DIM) == h, d_ot, jnp.zeros_like(d_ot))
                ds = (p.astype(F32) * (dotf(qkv_ref[2], d_h, 1, 0) - inner)).astype(BF)
                dks.append(dotf(ds, qkv_ref[0], 1, 0))
                dqs.append(dotf(k_t[head, :], ds, 1, 0))
            dv = jnp.where(lane < HEAD_DIM, dvs[0], dvs[1]).astype(BF)
            dk = jnp.where(lane < HEAD_DIM, dks[0], dks[1]).astype(BF)
            dq = jnp.concatenate(dqs, 0).T.astype(BF)
            dqk = jnp.concatenate([dq, dk], 1)
            total = dotf(dqk, qk[0:width, :], 1, 1) + dotf(dv, vo[0:width, 0:128], 1, 1)
            if acc:
                total = total + acc[0][...]
            totals[index][...] = total.astype(totals[index].dtype)
            dqks.append(dqk)
            dvs_all.append(dv)
            ctxs.append(ctx)

        def both(place, rights, piece):
            return sum(dotf(ins[7 * i + place][0][piece, :], rights[i], 1, 0) for i in (0, 1))

        def column_sums(values):
            return sum(jnp.sum(v.astype(F32), 0, keepdims=True) for v in values)

        sums = [column_sums(dqks), jnp.concatenate([column_sums(dvs_all), jnp.zeros((1, 128), F32)], 1)]
        for index in (0, 1):
            out = outs[index : index + 1]
            for part in (0, 1):
                piece = slice(part * half, (part + 1) * half)
                if index == 0:
                    value = both(2, dqks, piece)
                else:
                    value = jnp.concatenate([both(2, dvs_all, piece), both(1, ctxs, piece)], 1)
                put(out, part, half, 16, value)
            put(out, 2, half, 16, jnp.where(first, sums[index], 0.0))
            put(out, 3, half, 16, jnp.zeros((16, 256), F32))

    outs += [*gradient_shapes(width, 256, 16, False) * 2]
    return order(kernel, tuple(outs), tuple(args), "attn_bwd", 8, aliases)


def ffn_fwd(order, seqs, up, dn, low=False):
    width = dn.shape[1]
    counts, args, outs, aliases = [], [up, dn], [], {}
    rows = sum(m.shape[0] for m in seqs[0][0])
    mid = ((rows, dn.shape[0]), BF)
    for n, acc in seqs:
        counts += [len(n), acc is not None]
        args += n
        if acc is not None:
            if not low:
                aliases[len(args)] = len(outs)
            args.append(acc)
        outs += [*((((rows // 2, width), BF),) * 2 if low else (((rows, width), F32),)), mid, mid]

    def kernel(up, dn, *refs):
        ins = split_refs(refs[: sum(counts)], counts)
        results = refs[sum(counts) :]
        for index in range(len(seqs)):
            n_refs, acc = ins[2 * index : 2 * index + 2]
            total_refs, results = results[: 1 + low], results[1 + low :]
            (act_ref, slope_ref), results = results[:2], results[2:]
            for i in (0, 1):
                part = slice(i * (rows // 2), (i + 1) * (rows // 2))
                u = dotf(take(n_refs, part), up[0:width, :], 1, 0) + up[width : width + 16, :][0:1, :].astype(F32)
                cdf = 0.5 + 0.5 * lax.erf(u * root_half)
                act = (u * cdf).astype(BF)
                act_ref[part, :] = act
                slope = cdf + u * (jnp.exp2(u * u * (-0.5 * LOG2E)) * inverse_root_two_pi)
                slope_ref[part, :] = slope.astype(BF)
                total = dotf(act, dn[...], 1, 0)
                if acc:
                    total = total + acc[0][part, :]
                if low:
                    total_refs[i][...] = total.astype(BF)
                else:
                    total_refs[0][part, :] = total

    result = list(order(kernel, tuple(outs), tuple(args), "ffn_fwd", 8, aliases))
    out = []
    for _ in seqs:
        out.append((result[: 1 + low], result[1 + low : 3 + low]))
        result = result[3 + low :]
    return out


def ffn_bwd(order, seqs, up, dn, low=False):
    width = dn.shape[1]
    counts, args, outs, aliases = [], [up, dn], [], {}
    rows = seqs[0][1].shape[0]
    for g, slope, acc in seqs:
        counts += [len(g), 1, acc is not None]
        args += [*g, slope]
        if acc is not None:
            if not low:
                aliases[len(args)] = len(outs)
            args.append(acc)
        outs += [*((((rows // 2, width), BF),) * 2 if low else (((rows, width), F32),)), (slope.shape, BF)]

    def kernel(up, dn, *refs):
        ins = split_refs(refs[: sum(counts)], counts)
        results = refs[sum(counts) :]
        for index in range(len(seqs)):
            g, (slope,), acc = ins[3 * index : 3 * index + 3]
            total_refs, results = results[: 1 + low], results[1 + low :]
            d_ref, *results = results
            d_up = (dotf(whole(g), dn[...], 1, 1) * slope[...].astype(F32)).astype(BF)
            d_ref[...] = d_up
            total = dotf(d_up, up[0:width, :], 1, 1)
            if acc:
                total = total + acc[0][...]
            if low:
                total_refs[0][...] = total[: rows // 2].astype(BF)
                total_refs[1][...] = total[rows // 2 :].astype(BF)
            else:
                total_refs[0][...] = total

    result = list(order(kernel, tuple(outs), tuple(args), "ffn_bwd", 8, aliases))
    out = []
    for _ in seqs:
        out.append((result[: 1 + low], result[1 + low]))
        result = result[2 + low :]
    return out


def standard(v):
    centered = v - jnp.mean(v, -1, keepdims=True)
    inv = lax.rsqrt(jnp.mean(centered * centered, -1, keepdims=True) + norm_epsilon)
    return centered * inv, inv


def back_through(g, scaled, inv, gain):
    e = g * gain
    return inv * (e - jnp.mean(e, -1, keepdims=True) - scaled * jnp.mean(e * scaled, -1, keepdims=True))


def half_of(refs, i):
    per = refs[0].shape[0] // 128
    return refs[i // per][(i % per) * 128 : (i % per + 1) * 128, :]


def first_norm(order, x, acc, got, b_out, gain, bias, b_down):
    rows, width = x.shape

    def kernel(x_ref, acc_ref, got_ref, b_out, gain, bias, b_down, sum_ref, out_ref, low_a, low_b, low_t):
        for i in range(rows // 128):
            part = slice(i * 128, (i + 1) * 128)
            total = x_ref[part, :].astype(F32) + b_out[...].astype(F32)
            total = total + acc_ref[part, :] + got_ref[part, :].astype(F32)
            sum_ref[part, :] = total
            scaled, _ = standard(total)
            normed = scaled * gain[...] + bias[...]
            out_ref[part, :] = normed + b_down[...].astype(F32)
            low = normed.astype(BF)
            place = (i * 128) % (rows // 2)
            (low_a, low_b)[i * 256 // rows][place : place + 128, :] = low
            low_t[:, part] = low.astype(F32).T.astype(BF)

    half = ((rows // 2, width), BF)
    outs = (((rows, width), F32), ((rows, width), F32), half, half, ((width, rows), BF))
    args = (x, acc, got, b_out[None], gain[None], bias[None], b_down[None])
    return order(kernel, outs, args, "first_norm", 14, {1: 0})


def emit_back(i, carry, g, scaled, inv, gain, out_ref, low_halves, low_t):
    part = slice(i * 128, (i + 1) * 128)
    d_rows = back_through(g, scaled, inv, gain)
    out_ref[part, :] = d_rows
    low = d_rows.astype(BF)
    half = low_halves[0].shape[0]
    place = (i * 128) % half
    low_halves[i * 128 // half][place : place + 128, :] = low
    low = low.astype(F32)
    low_t[:, part] = low.T.astype(BF)
    terms = (g * scaled, g, low)
    return tuple(c + jnp.sum(t, 0, keepdims=True) for c, t in zip(carry, terms))


def put_sums(sums_ref, carry):
    row = lax.broadcasted_iota(jnp.int32, sums_ref.shape, 0)
    sums_ref[...] = jnp.where(row == 0, carry[0], jnp.where(row == 1, carry[1], jnp.where(row == 2, carry[2], 0.0)))


def back_outs(rows, width):
    half = ((rows // 2, width), BF)
    return (((rows, width), F32), half, half, ((width, rows), BF), ((8, width), F32))


def second_norm(order, total, got, cotangent, gain, bias):
    rows, width = total.shape

    def kernel(sum_ref, got_a, got_b, cot_ref, gain, bias, d_ref, low_a, low_b, low_t, sums_ref, y_ref):
        carry = (jnp.zeros((1, width), F32),) * 3
        for i in range(rows // 128):
            part = slice(i * 128, (i + 1) * 128)
            scaled, inv = standard(sum_ref[part, :] + half_of((got_a, got_b), i).astype(F32))
            y_ref[part, :] = (scaled * gain[...] + bias[...]).astype(BF)
            g = cot_ref[part, :].astype(F32)
            carry = emit_back(i, carry, g, scaled, inv, gain[...], d_ref, (low_a, low_b), low_t)
        put_sums(sums_ref, carry)

    outs = (*back_outs(rows, width), ((rows, width), BF))
    return order(kernel, outs, (total, *got, cotangent, gain[None], bias[None]), "second_norm", 14, {0: 0})


def first_back(order, first, gain, d_normed, got):
    rows, width = first.shape

    def kernel(sum_ref, gain, d_ref, got_a, got_b, out_ref, low_a, low_b, low_t, sums_ref):
        carry = (jnp.zeros((1, width), F32),) * 3
        for i in range(rows // 128):
            part = slice(i * 128, (i + 1) * 128)
            scaled, inv = standard(sum_ref[part, :])
            g = d_ref[part, :] + half_of((got_a, got_b), i).astype(F32)
            carry = emit_back(i, carry, g, scaled, inv, gain[...], out_ref, (low_a, low_b), low_t)
        put_sums(sums_ref, carry)

    return order(kernel, back_outs(rows, width), (first, gain[None], d_normed, *got), "first_back", 14, {2: 0})

CORE = [(d, d ^ 1) for d in range(8)]
ROW = [(t, t ^ 1) for t in range(4)]
COL = [(t, t ^ 2) for t in range(4)]
NEAR = [(d, d ^ 2) for d in range(8)]
FAR = [(d, d ^ 4) for d in range(8)]


def swap_core(v):
    return lax.ppermute(v, "dp", CORE)


def swap_row(v):
    return lax.ppermute(v, "tensor", ROW)


def swap_col(v):
    return lax.ppermute(v, "tensor", COL)


def swap_near(v):
    return lax.ppermute(v, "dp", NEAR)


def swap_far(v):
    return lax.ppermute(v, "dp", FAR)


class Piece:
    def __init__(self, order, odd):
        self.order, self.odd = order, odd
        self.mine = [None] * 4

    def diagonal(self, top, bottom):
        self.top, self.bottom = swap_row(top), swap_col(bottom)

    def direct(self, row_part, col_part):
        self.row_part, self.col_part = swap_row(row_part), swap_col(col_part)

    def along_z(self, keep, send):
        self.keep, self.got = keep, swap_near(send)

    def second(self):
        self.keep = self.order.add(self.got, self.keep)
        self.got = swap_far(self.keep)

    def third(self):
        self.keep = self.order.add(self.got, self.keep)

    def fourth(self):
        self.got = swap_near(self.order.now(self.keep))

    def kept(self):
        self.keep_o = swap_core(self.order.now(self.keep))

    def last(self):
        self.got_o = swap_core(self.order.now(self.got))

    def all(self):
        return self.keep, self.keep_o, self.got, self.got_o


def fast(
    layer_input,
    segment_ids,
    w_qkv,
    b_qv,
    w_out,
    b_out,
    ln1_gain,
    ln1_bias,
    w_up,
    b_up,
    w_down,
    b_down,
    ln2_gain,
    ln2_bias,
    cotangent,
):
    rows, width = layer_input.shape
    hidden = w_up.shape[1] // 2
    core = lax.axis_index("dp") % 2
    odd_index = (lax.axis_index("dp") // 2) % 2
    odd = odd_index.astype(jnp.int32)[None]
    core = core.astype(jnp.int32)[None]
    order = Order()
    now, wait = order.now, order.wait

    segment = lax.dynamic_index_in_dim(segment_ids, lax.axis_index("tensor"), keepdims=False)
    inputs = ((layer_input,), (swap_core(layer_input),))
    qk, vo, up_w, dn_w = [None] * 4, [None] * 4, [None] * 4, [None] * 4
    qk[0], vo[0] = pack_attn(order, core, w_qkv, w_out, b_qv)
    qk[1], qk[2] = swap_row(qk[0]), swap_col(qk[0])
    vo[1], vo[2] = swap_row(vo[0]), swap_col(vo[0])
    up_w[0], dn_w[0] = pack_ffn(order, core, w_up, b_up[None], w_down)

    masks = [
        jnp.where(ids[:, None] == ids[None, :], 0.0, -1e30).astype(F32) for ids in (segment, swap_core(segment))
    ]
    total = [None, None]
    saved = [[None, None] for _ in range(4)]

    def attend(r, which, low=False):
        found = attn_fwd(order, [(inputs[s], masks[s], total[s], low) for s in which], qk[r], vo[r])
        for s, (total[s], saved[r][s]) in zip(which, found):
            continue

    attend(0, (0, 1))
    qk[3], vo[3] = swap_row(now(qk[2])), swap_col(now(vo[1]))
    attend(1, (0, 1))
    up_w[1], up_w[2] = swap_row(now(up_w[0])), swap_col(now(up_w[0]))
    attend(2, (0, 1))
    attend(3, (1,), True)
    got = swap_core(total[1])
    attend(3, (0,))
    dn_w[1], dn_w[2] = swap_row(now(dn_w[0])), swap_col(now(dn_w[0]))
    wait(up_w[1], up_w[2])
    first, branch, *low, normed_t = first_norm(
        order, layer_input, total[0], got, b_out, ln1_gain, ln1_bias, b_down
    )
    normed = (tuple(low), tuple(swap_core(v) for v in low))
    total = [branch, None]
    acts = [[None, None] for _ in range(4)]
    slopes = [[None, None] for _ in range(4)]

    def expand(r, which, low=False):
        found = ffn_fwd(order, [(normed[s], total[s]) for s in which], up_w[r], dn_w[r], low)
        for s, (total[s], (acts[r][s], slopes[r][s])) in zip(which, found):
            total[s] = total[s] if low else total[s][0]

    expand(0, (0,))
    expand(0, (1,))
    wait(dn_w[1], dn_w[2])
    normed_t = (normed_t, flip(order, normed[1]))
    up_w[3], dn_w[3] = swap_row(now(up_w[2])), swap_col(now(dn_w[1]))
    expand(1, (0, 1))
    expand(2, (0, 1))
    expand(3, (1,), True)
    got = [swap_core(v) for v in total[1]]
    expand(3, (0,))
    d_second, *low, branch_t, sums_two, output = second_norm(order, total[0], got, cotangent, ln2_gain, ln2_bias)
    branch_low = (tuple(low), tuple(swap_core(v) for v in low))

    down, up = Piece(order, odd), Piece(order, odd)
    attn, attn_qk, attn_vo = Piece(order, odd), Piece(order, odd), Piece(order, odd)
    total = [d_second, None]
    d_up = [[None, None] for _ in range(4)]

    def back(r, which, low=False):
        found = ffn_bwd(order, [(branch_low[s], slopes[r][s], total[s]) for s in which], up_w[r], dn_w[r], low)
        for s, (total[s], d_up[r][s]) in zip(which, found):
            total[s] = total[s] if low else total[s][0]

    def grad_down(r, got=(), split=False, z=None):
        return outer(order, branch_t, acts[r], got, split, "grad_down", False, z)

    def grad_up(r, got=(), split=False, z=None):
        return outer(order, normed_t, d_up[r], got, split, "grad_up", True, z)

    back(3, (0,))
    branch_t = (branch_t, flip(order, branch_low[1]))
    down.diagonal(*grad_down(3, split=True))
    back(3, (1,))
    up.diagonal(*grad_up(3, split=True))
    back(1, (0, 1))
    back(2, (0, 1))
    down_row, down_col = grad_down(1)[0], grad_down(2)[0]
    down.direct(*pass_on(order, down_row, down.bottom, down_col, down.top))
    back(0, (1,), True)
    got = [swap_core(v) for v in total[1]]
    back(0, (0,))
    d_first, *low, attention_t, sums_one = first_back(order, first, ln1_gain, total[0], got)
    attention_low = (tuple(low), tuple(swap_core(v) for v in low))
    inputs_t = [flip(order, inputs[s]) for s in (0, 1)]
    attention_t = (attention_t, flip(order, attention_low[1]))
    total = [d_first, None]

    def attend_back(r, low=False):
        seqs = [
            (attention_low[s], attention_t[s], inputs_t[s], *saved[r][s], total[s]) for s in (0, 1)
        ]
        total[0], total[1], attn_qk.mine[r], attn_vo.mine[r] = attn_bwd(order, seqs, qk[r], vo[r], low)

    up_row, up_col = grad_up(1, split=True), grad_up(2, split=True)
    down_own = grad_down(0)[0]
    down.along_z(*sum_halves(order, odd, down_own, down.row_part, down.col_part))
    low_row, high_col = add_pair(order, up_row[1], up.bottom, up_col[0], up.top)
    up_rows, up_cols = [swap_row(v) for v in (up_row[0], low_row)], [swap_col(v) for v in (high_col, up_col[1])]
    down.second()
    attend_back(3)
    qk_diag, vo_diag = swap_row(attn_qk.mine[3]), swap_col(attn_vo.mine[3])
    attend_back(1)
    arrived = [(kind, v) for part in (up_rows, up_cols) for kind, v in zip(("top", "bottom"), part)]
    up.along_z(*grad_up(0, arrived, True, odd))
    attend_back(2)
    down.third()
    up.second()
    row, col = relay(order, attn_qk.mine[1], attn_vo.mine[1], vo_diag, attn_qk.mine[2], attn_vo.mine[2], qk_diag)
    row, col = swap_row(row), swap_col(col)
    down.fourth()
    attend_back(0, True)
    wait(down.got)
    attn.along_z(*own_sum(order, odd, attn_qk.mine[0], attn_vo.mine[0], row, col))
    up.third()
    small = jnp.concatenate([sums_one, sums_two], 0)
    small = order.add(swap_core(now(small)), small)
    small = order.add(swap_row(small), small)
    small = order.add(swap_col(small), small)
    small_near = swap_near(small)
    attn.second()
    up.fourth()
    down.kept()
    down.last()
    got = swap_core(now(total[1]))
    grad_w_down = finish_down(order, core, odd, down.all())
    grad_input = order.add(got, total[0])
    small = order.add(small_near, small)
    wait(up.got)
    attn.third()
    attn.fourth()
    small_far = swap_far(now(small))
    attn.kept()
    up.kept()
    up.last()
    grad_b_up, grad_w_up = finish_up(order, core, odd, up.all())
    small = order.add(small_far, small)
    attn.last()
    grad_w_qkv, grad_b_qv, grad_w_out = finish_attn(order, core, odd, attn.all())
    return (
        output,
        grad_input,
        grad_w_qkv,
        grad_b_qv,
        grad_w_out,
        small[2],
        small[0],
        small[1],
        grad_w_up,
        grad_b_up[0],
        grad_w_down,
        small[10],
        small[8],
        small[9],
    )


def local(*arrays):
    my_rows = arrays[0].shape[0]
    seq_len = arrays[1].shape[1]
    grid = (lax.axis_size("dp"), lax.axis_size("tensor"))
    if grid == (8, 4) and my_rows == seq_len and arrays[4].shape[0] == 4 * HEAD_DIM:
        return fast(*arrays)
    return general(*arrays)


def solution(mesh):
    return jax.shard_map(
        local,
        mesh=mesh,
        in_specs=(
            P(("dp", "tensor"), None),
            P("dp", None),
            P(None, None, "tensor"),
            P(None, "tensor"),
            P("tensor", None),
            P(),
            P(),
            P(),
            P(None, "tensor"),
            P("tensor"),
            P("tensor", None),
            P(),
            P(),
            P(),
            P(("dp", "tensor"), None),
        ),
        out_specs=(
            P(("dp", "tensor"), None),
            P(("dp", "tensor"), None),
            P(None, None, "tensor"),
            P(None, "tensor"),
            P("tensor", None),
            P(),
            P(),
            P(),
            P(None, "tensor"),
            P("tensor"),
            P("tensor", None),
            P(),
            P(),
            P(),
        ),
        check_vma=False,
    )
```

```python
import jax
import jax.numpy as jnp
from jax import lax
from jax.experimental import pallas as pl
from jax.experimental.pallas import tpu as pltpu
from jax.sharding import PartitionSpec as P

HEAD_DIM = 64


norm_epsilon = 1e-05
root_half = 0.7071067811865476
inverse_root_two_pi = 0.3989422804014327


def layer_norm(token_rows, norm_gain, norm_bias):
    row_mean = jnp.mean(token_rows, -1, keepdims=True)
    centered = token_rows - row_mean
    variance = jnp.mean(centered * centered, -1, keepdims=True)
    inv_std = lax.rsqrt(variance + norm_epsilon)
    scaled = centered * inv_std
    return (scaled * norm_gain + norm_bias, scaled, inv_std)


def norm_back(incoming, scaled, inv_std, norm_gain):
    weighted = incoming * norm_gain
    d_rows = inv_std * (
        weighted
        - jnp.mean(weighted, -1, keepdims=True)
        - scaled * jnp.mean(weighted * scaled, -1, keepdims=True)
    )
    return (d_rows, jnp.sum(incoming * scaled, 0), jnp.sum(incoming, 0))


def gelu_value(up_proj):
    return 0.5 * up_proj * (1.0 + lax.erf(up_proj * root_half))


def gelu_slope(up_proj):
    return (
        0.5 * (1.0 + lax.erf(up_proj * root_half))
        + up_proj * jnp.exp(-0.5 * up_proj * up_proj) * inverse_root_two_pi
    )


def split_heads(matrix, head_count):
    return matrix.reshape(matrix.shape[0], head_count, -1)


def project(token_rows, w_qkv, b_qv):
    queries = (
        jnp.dot(token_rows, w_qkv[0], preferred_element_type=jnp.float32)
        + b_qv[0].astype(jnp.float32)
    ).astype(jnp.bfloat16)
    keys_low = jnp.dot(token_rows, w_qkv[1], preferred_element_type=jnp.float32).astype(
        jnp.bfloat16
    )
    values = (
        jnp.dot(token_rows, w_qkv[2], preferred_element_type=jnp.float32)
        + b_qv[1].astype(jnp.float32)
    ).astype(jnp.bfloat16)
    return (queries, keys_low, values)


def scores(queries, keys_low, segment, head_count, score_scale):
    raw = jnp.einsum(
        "qhd,khd->hqk",
        split_heads(queries, head_count),
        split_heads(keys_low, head_count),
        preferred_element_type=jnp.float32,
    )
    same_doc = segment[:, None] == segment[None, :]
    return jnp.where(same_doc[None], raw * score_scale, -1e30)


def mix_values(prob_low, values, head_count):
    context = jnp.einsum(
        "hqk,khd->qhd",
        prob_low,
        split_heads(values, head_count),
        preferred_element_type=jnp.float32,
    )
    return context.reshape(context.shape[0], -1).astype(jnp.bfloat16)


def ffn_forward(normed_low, up_weight, up_bias, down_weight):
    up_proj = jnp.dot(normed_low, up_weight, preferred_element_type=jnp.float32) + up_bias.astype(
        jnp.float32
    )
    activation = gelu_value(up_proj).astype(jnp.bfloat16)
    return jnp.dot(activation, down_weight, preferred_element_type=jnp.float32)


def ffn_backward(normed_low, branch_low, up_weight, up_bias, down_weight):
    up_proj = jnp.dot(normed_low, up_weight, preferred_element_type=jnp.float32) + up_bias.astype(
        jnp.float32
    )
    activation = gelu_value(up_proj).astype(jnp.bfloat16)
    grad_down = jnp.einsum("tf,td->fd", activation, branch_low, preferred_element_type=jnp.float32)
    d_activation = jnp.einsum(
        "td,fd->tf", branch_low, down_weight, preferred_element_type=jnp.float32
    )
    d_up = (d_activation * gelu_slope(up_proj)).astype(jnp.bfloat16)
    grad_up = jnp.einsum("td,tf->df", normed_low, d_up, preferred_element_type=jnp.float32)
    grad_up_bias = jnp.sum(d_up.astype(jnp.float32), 0)
    return (grad_up, grad_up_bias, grad_down, d_up)


def general(
    layer_input,
    segment_ids,
    w_qkv,
    b_qv,
    w_out,
    b_out,
    ln1_gain,
    ln1_bias,
    w_up,
    b_up,
    w_down,
    b_down,
    ln2_gain,
    ln2_bias,
    cotangent,
):
    my_rows, model_width = layer_input.shape
    seq_len = segment_ids.shape[1]
    score_scale = HEAD_DIM ** (-0.5)
    whole_input = lax.all_gather(layer_input, "tensor", axis=0, tiled=True)
    seq_input = whole_input.reshape(segment_ids.shape[0], seq_len, model_width)
    attn_width = w_out.shape[0]
    head_count = attn_width // HEAD_DIM

    def forward_seq(running, seq_item):
        token_rows, segment = seq_item
        queries, keys_low, values = project(token_rows, w_qkv, b_qv)
        logits = scores(queries, keys_low, segment, head_count, score_scale)
        row_max = jnp.max(logits, -1, keepdims=True)
        exponent = jnp.exp(logits - row_max)
        expo_sum = jnp.sum(exponent, -1, keepdims=True)
        prob_low = (exponent / expo_sum).astype(jnp.bfloat16)
        return (running, (mix_values(prob_low, values, head_count), row_max + jnp.log(expo_sum)))

    _, (seq_context, seq_lse) = lax.scan(forward_seq, None, (seq_input, segment_ids))
    all_context = seq_context.reshape(-1, attn_width)
    attention = lax.psum_scatter(
        jnp.dot(all_context, w_out, preferred_element_type=jnp.float32),
        "tensor",
        scatter_dimension=0,
        tiled=True,
    ) + b_out.astype(jnp.float32)
    normed_one, scaled_one, inv_one = layer_norm(
        layer_input.astype(jnp.float32) + attention, ln1_gain, ln1_bias
    )
    normed_low = normed_one.astype(jnp.bfloat16)
    whole_normed = lax.all_gather(normed_low, "tensor", axis=0, tiled=True)
    branch = lax.psum_scatter(
        ffn_forward(whole_normed, w_up, b_up, w_down), "tensor", scatter_dimension=0, tiled=True
    )
    normed_two, scaled_two, inv_two = layer_norm(
        normed_one + branch + b_down.astype(jnp.float32), ln2_gain, ln2_bias
    )
    d_second, grad_ln2_gain, grad_ln2_bias = norm_back(
        cotangent.astype(jnp.float32), scaled_two, inv_two, ln2_gain
    )
    branch_low = d_second.astype(jnp.bfloat16)
    grad_b_down = jnp.sum(branch_low.astype(jnp.float32), 0)
    whole_branch = lax.all_gather(branch_low, "tensor", axis=0, tiled=True)
    grad_w_up, grad_b_up, grad_w_down, d_up = ffn_backward(
        whole_normed, whole_branch, w_up, b_up, w_down
    )
    d_normed = lax.psum_scatter(
        jnp.einsum("tf,df->td", d_up, w_up, preferred_element_type=jnp.float32),
        "tensor",
        scatter_dimension=0,
        tiled=True,
    )
    d_first, grad_ln1_gain, grad_ln1_bias = norm_back(
        d_second + d_normed, scaled_one, inv_one, ln1_gain
    )
    attention_low = d_first.astype(jnp.bfloat16)
    grad_b_out = jnp.sum(attention_low.astype(jnp.float32), 0)
    whole_grad = lax.all_gather(attention_low, "tensor", axis=0, tiled=True)
    seq_grad = whole_grad.reshape(seq_input.shape[0], seq_len, model_width)

    def backward_seq(running, seq_item):
        grad_qkv, grad_bias, grad_out = running
        token_rows, segment, seq_lse_one, grad_rows = seq_item
        queries, keys_low, values = project(token_rows, w_qkv, b_qv)
        logits = scores(queries, keys_low, segment, head_count, score_scale)
        probability = jnp.exp(logits - seq_lse_one)
        prob_low = probability.astype(jnp.bfloat16)
        context = mix_values(prob_low, values, head_count)
        grad_out = grad_out + jnp.einsum(
            "te,td->ed", context, grad_rows, preferred_element_type=jnp.float32
        )
        d_context = jnp.einsum(
            "td,ed->te", grad_rows, w_out, preferred_element_type=jnp.float32
        ).astype(jnp.bfloat16)
        d_heads = split_heads(d_context, head_count)
        d_prob = jnp.einsum(
            "qhd,khd->hqk",
            d_heads,
            split_heads(values, head_count),
            preferred_element_type=jnp.float32,
        )
        d_values = (
            jnp.einsum("hqk,qhd->khd", prob_low, d_heads, preferred_element_type=jnp.float32)
            .reshape(seq_len, -1)
            .astype(jnp.bfloat16)
        )
        inner_sum = jnp.sum(probability * d_prob, -1, keepdims=True)
        d_raw = (probability * (d_prob - inner_sum) * score_scale).astype(jnp.bfloat16)
        d_queries = (
            jnp.einsum(
                "hqk,khd->qhd",
                d_raw,
                split_heads(keys_low, head_count),
                preferred_element_type=jnp.float32,
            )
            .reshape(seq_len, -1)
            .astype(jnp.bfloat16)
        )
        d_keys = (
            jnp.einsum(
                "hqk,qhd->khd",
                d_raw,
                split_heads(queries, head_count),
                preferred_element_type=jnp.float32,
            )
            .reshape(seq_len, -1)
            .astype(jnp.bfloat16)
        )
        grad_qkv = grad_qkv + jnp.stack(
            [
                jnp.einsum("td,te->de", token_rows, gradient, preferred_element_type=jnp.float32)
                for gradient in (d_queries, d_keys, d_values)
            ]
        )
        grad_bias = grad_bias + jnp.stack(
            [jnp.sum(d_queries.astype(jnp.float32), 0), jnp.sum(d_values.astype(jnp.float32), 0)]
        )
        return ((grad_qkv, grad_bias, grad_out), (d_queries, d_keys, d_values))

    start_grads = (
        jnp.zeros((3, model_width, attn_width), jnp.float32),
        jnp.zeros((2, attn_width), jnp.float32),
        jnp.zeros((attn_width, model_width), jnp.float32),
    )
    (grad_w_qkv, grad_b_qv, grad_w_out), seq_d = lax.scan(
        backward_seq, start_grads, (seq_input, segment_ids, seq_lse, seq_grad)
    )
    all_d = [gradient.reshape(-1, attn_width) for gradient in seq_d]
    summed = jnp.zeros((my_rows * lax.axis_size("tensor"), model_width), jnp.float32)
    for which in range(3):
        piece = all_d[which]
        summed = summed + jnp.einsum(
            "te,de->td", piece, w_qkv[which], preferred_element_type=jnp.float32
        )
    grad_input = d_first + lax.psum_scatter(
        summed.astype(jnp.bfloat16), "tensor", scatter_dimension=0, tiled=True
    ).astype(jnp.float32)
    grad_w_qkv, grad_b_qv, grad_w_out, grad_w_up, grad_b_up, grad_w_down = (
        lax.psum(grad_w_qkv.astype(jnp.bfloat16), "dp").astype(jnp.float32),
        lax.psum(grad_b_qv.astype(jnp.bfloat16), "dp").astype(jnp.float32),
        lax.psum(grad_w_out.astype(jnp.bfloat16), "dp").astype(jnp.float32),
        lax.psum(grad_w_up.astype(jnp.bfloat16), "dp").astype(jnp.float32),
        lax.psum(grad_b_up.astype(jnp.bfloat16), "dp").astype(jnp.float32),
        lax.psum(grad_w_down.astype(jnp.bfloat16), "dp").astype(jnp.float32),
    )
    grad_b_out, grad_ln1_gain, grad_ln1_bias, grad_b_down, grad_ln2_gain, grad_ln2_bias = lax.psum(
        (grad_b_out, grad_ln1_gain, grad_ln1_bias, grad_b_down, grad_ln2_gain, grad_ln2_bias),
        ("dp", "tensor"),
    )
    return (
        normed_two.astype(jnp.bfloat16),
        grad_input,
        grad_w_qkv,
        grad_b_qv,
        grad_w_out,
        grad_b_out,
        grad_ln1_gain,
        grad_ln1_bias,
        grad_w_up,
        grad_b_up,
        grad_w_down,
        grad_b_down,
        grad_ln2_gain,
        grad_ln2_bias,
    )


F32 = jnp.float32
BF = jnp.bfloat16
LOG2E = 1.4426950408889634


def dotf(a, b, ca, cb):
    return lax.dot_general(a, b, (((ca,), (cb,)), ((), ())), preferred_element_type=F32)


class Order:
    def __init__(self):
        self.token, self.waited = None, []

    def wait(self, *values):
        self.waited.extend(values)

    def __call__(self, kernel, outs, args, name, limit, aliases=None, smem=0):
        count = len(args)
        specs = [pl.BlockSpec(memory_space=pltpu.SMEM)] * smem + [pl.BlockSpec()] * (count - smem)
        unread = ([] if self.token is None else [self.token]) + self.waited
        specs += [pl.BlockSpec(memory_space=pltpu.HBM)] * len(unread)
        self.waited = []
        args = (*args, *unread)

        def body(*refs):
            kernel(*refs[:count], *refs[len(args) : -1])
            refs[-1][...] = jnp.zeros((8, 128), F32)

        *result, self.token = pl.pallas_call(
            body,
            out_shape=tuple(jax.ShapeDtypeStruct(s, d) for s, d in (*outs, ((8, 128), F32))),
            in_specs=specs,
            input_output_aliases=aliases or {},
            compiler_params=pltpu.CompilerParams(vmem_limit_bytes=limit << 20),
            cost_estimate=pl.CostEstimate(flops=1, bytes_accessed=1, transcendentals=0),
            name=name,
        )(*args)
        return result

    def add(self, a, b):
        def kernel(a_ref, b_ref, out):
            out[...] = (a_ref[...].astype(F32) + b_ref[...].astype(F32)).astype(out.dtype)

        return self(kernel, ((b.shape, b.dtype),), (a, b), "add", 8)[0]

    def now(self, value):
        return lax.optimization_barrier((value, self.token))[0]


def pack_attn(order, core, w_qkv, w_out, b_qv):
    width = w_qkv.shape[1]

    def kernel(core, w_qkv, w_out, b_qv, qk, vo, token, rows, done):
        part = pl.ds(pl.multiple_of(core[0] * 128, 128), 128)
        places = (qk.at[0:width, 0:128], qk.at[0:width, 128:256], vo.at[0:width, 0:128])
        copies = [pltpu.make_async_copy(w_out.at[part, :], rows, done.at[3])]
        copies += [pltpu.make_async_copy(w_qkv.at[i, :, part], place, done.at[i]) for i, place in enumerate(places)]
        for copy in copies:
            copy.start()
        zero = jnp.zeros((16, 128), BF)
        first = lax.broadcasted_iota(jnp.int32, (16, 128), 0) == 0
        for i, out in enumerate((qk, vo)):
            out[width : width + 16, 0:128] = jnp.where(first, b_qv[i : i + 1, part].astype(F32), 0.0).astype(BF)
            out[width : width + 16, 128:256] = zero
        token[...] = jnp.zeros((8, 128), F32)
        copies[0].wait()
        vo[0:width, 128:256] = rows[...].astype(F32).T.astype(BF)
        for copy in copies[1:]:
            copy.wait()

    out = jax.ShapeDtypeStruct((width + 16, 256), BF)
    hbm = pl.BlockSpec(memory_space=pltpu.HBM)
    qk, vo, order.token = pl.pallas_call(
        kernel,
        out_shape=(out, out, jax.ShapeDtypeStruct((8, 128), F32)),
        in_specs=[pl.BlockSpec(memory_space=pltpu.SMEM), hbm, hbm, pl.BlockSpec()],
        scratch_shapes=[pltpu.VMEM((128, w_out.shape[1]), BF), pltpu.SemaphoreType.DMA((4,))],
        compiler_params=pltpu.CompilerParams(vmem_limit_bytes=58 << 20),
        cost_estimate=pl.CostEstimate(flops=1, bytes_accessed=1, transcendentals=0),
        name="pack_attn",
    )(core, w_qkv, w_out, b_qv)
    return qk, vo


def pack_ffn_kernel(core, w_up, b_up, w_down, up, dn):
    width = w_up.shape[0]
    hid = w_up.shape[1] // 2
    first = lax.broadcasted_iota(jnp.int32, (16, hid), 0) == 0
    part = pl.ds(pl.multiple_of(core[0] * hid, hid), hid)
    up[0:width, :] = w_up[:, part]
    up[width : width + 16, :] = jnp.where(first, b_up[0:1, part].astype(F32), 0.0).astype(BF)
    dn[...] = w_down[part, :]


def pack_ffn(order, core, w_up, b_up, w_down):
    width, hid = w_up.shape[0], w_up.shape[1] // 2
    outs = (((width + 16, hid), BF), ((hid, width), BF))
    return order(pack_ffn_kernel, outs, (core, w_up, b_up, w_down), "pack_ffn", 12, smem=1)


def flip(order, matrix):
    width = matrix[0].shape[1]

    def kernel(*refs):
        start = 0
        for ref in refs[:-1]:
            rows = ref.shape[0]
            refs[-1][:, start : start + rows] = ref[...].astype(F32).T.astype(BF)
            start += rows

    rows = sum(m.shape[0] for m in matrix)
    return order(kernel, (((width, rows), BF),), tuple(matrix), "flip", 8)[0]


def take(refs, part):
    if len(refs) == 1:
        return refs[0][part, :]
    half = refs[0].shape[0]
    return refs[part.start // half][part.start % half : (part.stop - 1) % half + 1, :]


def whole(refs):
    return refs[0][...] if len(refs) == 1 else jnp.concatenate([r[...] for r in refs], 0)


def split_refs(refs, counts):
    out = []
    for count in counts:
        out.append(refs[:count])
        refs = refs[count:]
    return out


def attn_fwd(order, seqs, qk, vo):
    rows = sum(m.shape[0] for m in seqs[0][0])
    width = qk.shape[0] - 16
    counts, args, outs, aliases = [], [qk, vo], [], {}
    pt, qkv, ctx = ((2, rows, rows), BF), ((3, rows, 128), BF), ((rows, 128), BF)
    for x, mask, acc, low in seqs:
        counts += [len(x), 1, acc is not None]
        args += [*x, mask]
        if acc is not None:
            if not low:
                aliases[len(args)] = len(outs)
            args.append(acc)
        outs += [((rows, width), BF if low else F32), pt, qkv, ctx]

    def kernel(qk, vo, *refs):
        ins = split_refs(refs[: sum(counts)], counts)
        results = refs[sum(counts) :]
        row = lax.broadcasted_iota(jnp.int32, (128, rows), 0)
        for index, (_, _, _, low) in enumerate(seqs):
            x_refs, (mask,), acc = ins[3 * index : 3 * index + 3]
            (total_ref, pt, qkv, ctx_ref), results = results[:4], results[4:]
            x = whole(x_refs)
            qkf = dotf(x, qk[0:width, :], 1, 0) + qk[width : width + 16, :][0:1, :].astype(F32)
            vf = dotf(x, vo[0:width, 0:128], 1, 0) + vo[width : width + 16, 0:128][0:1, :].astype(F32)
            k = qkf[:, 128:].astype(BF)
            qkv[0] = qkf[:, :128].astype(BF)
            qkv[1] = k
            qkv[2] = vf.astype(BF)
            q_t = qkf[:, :128].T.astype(BF)
            v_t = vf.T.astype(BF)
            parts = []
            for h in range(2):
                q_h = jnp.where((row // HEAD_DIM) == h, q_t, jnp.zeros_like(q_t))
                s = dotf(k, q_h, 1, 0) * (HEAD_DIM**-0.5 * LOG2E) + mask[...]
                e = jnp.exp2(s - jnp.max(s, 0, keepdims=True))
                p = (e * (1.0 / jnp.sum(e, 0, keepdims=True))).astype(BF)
                pt[h] = p
                parts.append(dotf(v_t[h * HEAD_DIM : (h + 1) * HEAD_DIM, :], p, 1, 0))
            ctx = jnp.concatenate(parts, 0).T.astype(BF)
            ctx_ref[...] = ctx
            total = dotf(ctx, vo[0:width, 128:256], 1, 1)
            if acc:
                total = total + acc[0][...]
            total_ref[...] = total.astype(total_ref.dtype)

    result = list(order(kernel, tuple(outs), tuple(args), "attn_fwd", 8, aliases))
    out = []
    for _ in seqs:
        out.append((result[0], result[1:4]))
        result = result[4:]
    return out


def part_rows(part, half, extra):
    whole = ((0, half), (half + extra, 2 * half + extra), (2 * half + extra, 2 * half + 2 * extra), (half, half + extra))
    own = ((0, half), (0, half), (half, half + extra), (half, half + extra))
    return whole[part], own[part]


def add_got(value, got, part, half, extra):
    whole, own = part_rows(part, half, extra)
    for kind, ref in got:
        if kind == "whole":
            value = value + ref[whole[0] : whole[1], :].astype(F32)
        elif (kind == "top") == (part == 0):
            value = value + ref[own[0] : own[1], :].astype(F32)
    return value


def put(outs, part, half, extra, value):
    whole, own = part_rows(part, half, extra)
    if len(outs) == 1:
        outs[0][whole[0] : whole[1], :] = value.astype(BF)
    else:
        outs[part in (1, 2)][own[0] : own[1], :] = value.astype(BF)


def gradient_shapes(width, columns, extra, split):
    if split:
        return (((width // 2 + extra, columns), BF),) * 2
    return (((width + 2 * extra, columns), BF),)


def outer(order, left_t, right, got, split, name, bias, odd=None):
    kinds = [kind for kind, _ in got]
    width = left_t[0].shape[0]
    half, extra = width // 2, 16

    def kernel(*refs):
        if odd is not None:
            flag, *refs = refs
        left_refs, right_refs, refs = refs[:2], refs[2:4], refs[4:]
        received = list(zip(kinds, refs))
        outs = refs[len(kinds) :]
        if odd is not None:
            swapped = flag[0] == 1
        values = []
        for part in (0, 1):
            piece = slice(part * half, (part + 1) * half)
            value = dotf(left_refs[0][piece, :], right_refs[0][...], 1, 0)
            value = value + dotf(left_refs[1][piece, :], right_refs[1][...], 1, 0)
            values.append(add_got(value, received, part, half, extra))
        zero = jnp.zeros((extra, values[0].shape[1]), F32)
        row = zero
        if bias:
            first = lax.broadcasted_iota(jnp.int32, zero.shape, 0) == 0
            row = sum(jnp.sum(r[...].astype(F32), 0, keepdims=True) for r in right_refs)
            row = add_got(jnp.where(first, row, 0.0), received, 2, half, extra)
        if odd is None:
            for part in (0, 1):
                put(outs, part, half, extra, values[part])
            put(outs, 2, half, extra, row)
            put(outs, 3, half, extra, zero)
        else:
            outs[0][0:half, :] = jnp.where(swapped, values[1], values[0]).astype(BF)
            outs[1][0:half, :] = jnp.where(swapped, values[0], values[1]).astype(BF)
            outs[0][half:, :] = jnp.where(swapped, row, zero).astype(BF)
            outs[1][half:, :] = jnp.where(swapped, zero, row).astype(BF)

    outs = gradient_shapes(width, right[0].shape[1], extra, split)
    flags = () if odd is None else (odd,)
    args = (*flags, *left_t, *right, *(v for _, v in got))
    return order(kernel, outs, args, name, 8, smem=len(flags))


def pass_on(order, row_part, bottom, col_part, top):
    half = row_part.shape[0] // 2

    def kernel(row_ref, bottom_ref, col_ref, top_ref, row, col):
        row[0:half, :] = row_ref[0:half, :]
        row[half:, :] = (row_ref[half:, :].astype(F32) + bottom_ref[...].astype(F32)).astype(BF)
        col[half:, :] = col_ref[half:, :]
        col[0:half, :] = (col_ref[0:half, :].astype(F32) + top_ref[...].astype(F32)).astype(BF)

    out = (row_part.shape, BF)
    return order(kernel, (out, out), (row_part, bottom, col_part, top), "pass_on", 10)


def add_pair(order, a, b, c, d):
    def kernel(a, b, c, d, first, second):
        first[...] = (a[...].astype(F32) + b[...].astype(F32)).astype(BF)
        second[...] = (c[...].astype(F32) + d[...].astype(F32)).astype(BF)

    return order(kernel, ((a.shape, BF), (c.shape, BF)), (a, b, c, d), "add_pair", 8)


def sum_halves(order, odd, own, row, col):
    half = own.shape[0] // 2

    def kernel(flag, own, row, col, keep, send):
        swapped = flag[0] == 1
        total = own[...].astype(F32) + row[...].astype(F32) + col[...].astype(F32)
        keep[...] = jnp.where(swapped, total[half:], total[:half]).astype(BF)
        send[...] = jnp.where(swapped, total[:half], total[half:]).astype(BF)

    out = ((half, own.shape[1]), BF)
    return order(kernel, (out, out), (odd, own, row, col), "sum_halves", 10, smem=1)


def relay(order, row_qk, row_vo, vo_diag, col_qk, col_vo, qk_diag):
    def kernel(row_qk, row_vo, vo_diag, col_qk, col_vo, qk_diag, row, col):
        row[:, 0:256] = row_qk[...]
        row[:, 256:512] = (row_vo[...].astype(F32) + vo_diag[...].astype(F32)).astype(BF)
        col[:, 0:256] = (col_qk[...].astype(F32) + qk_diag[...].astype(F32)).astype(BF)
        col[:, 256:512] = col_vo[...]

    out = ((row_qk.shape[0], 512), BF)
    return order(kernel, (out, out), (row_qk, row_vo, vo_diag, col_qk, col_vo, qk_diag), "relay", 10)


def own_sum(order, odd, own_qk, own_vo, row, col):
    half = row.shape[0] // 2

    def kernel(flag, own_qk, own_vo, row, col, keep, send):
        swapped = flag[0] == 1
        for own, place in ((own_qk, slice(0, 256)), (own_vo, slice(256, 512))):
            total = own[...].astype(F32) + row[:, place].astype(F32) + col[:, place].astype(F32)
            keep[:, place] = jnp.where(swapped, total[half:], total[:half]).astype(BF)
            send[:, place] = jnp.where(swapped, total[:half], total[half:]).astype(BF)

    out = ((half, 512), BF)
    return order(kernel, (out, out), (odd, own_qk, own_vo, row, col), "own_sum", 12, smem=1)


def final_halves(core, odd, refs):
    keep, keep_o, got, got_o = refs
    second, swapped = core[0] == 1, odd[0] == 1

    def value(ref):
        return ref[...].astype(F32)

    out = []
    for a, b, c, d in ((keep, keep_o, got, got_o), (keep_o, keep, got_o, got)):
        kept = jnp.where(second, value(b), value(a))
        received = jnp.where(second, value(d), value(c))
        out.append((jnp.where(swapped, received, kept), jnp.where(swapped, kept, received)))
    return out


def finish_down(order, core, odd, refs):
    half, columns = refs[0].shape
    half -= 16

    def kernel(core, odd, *refs):
        for i, pair in enumerate(final_halves(core, odd, refs[:4])):
            for j, value in enumerate(pair):
                refs[4][i * columns : (i + 1) * columns, j * half : (j + 1) * half] = value[:half].T

    return order(kernel, (((2 * columns, 2 * half), F32),), (core, odd, *refs), "finish_down", 12, smem=2)[0]


def finish_up(order, core, odd, refs):
    half, columns = refs[0].shape
    half -= 16

    def kernel(core, odd, *refs):
        for i, pair in enumerate(final_halves(core, odd, refs[:4])):
            place = slice(i * columns, (i + 1) * columns)
            for j, value in enumerate(pair):
                refs[5][j * half : (j + 1) * half, place] = value[:half]
            refs[4][0:1, place] = pair[1][half : half + 1]

    outs = (((1, 2 * columns), F32), ((2 * half, 2 * columns), F32))
    return order(kernel, outs, (core, odd, *refs), "finish_up", 12, smem=2)


def finish_attn(order, core, odd, refs):
    half = refs[0].shape[0] - 16

    def kernel(core, odd, *refs):
        w_qkv, b_qv, w_out = refs[4:]
        for i, pair in enumerate(final_halves(core, odd, refs[:4])):
            place = slice(i * 128, (i + 1) * 128)
            for j, value in enumerate(pair):
                rows = slice(j * half, (j + 1) * half)
                for k in range(3):
                    w_qkv[k, rows, place] = value[:half, k * 128 : (k + 1) * 128]
                w_out[place, rows] = value[:half, 384:512].T
            b_qv[0:1, place] = pair[1][half : half + 1, 0:128]
            b_qv[1:2, place] = pair[1][half : half + 1, 256:384]

    outs = (((3, 2 * half, 256), F32), ((2, 256), F32), ((256, 2 * half), F32))
    return order(kernel, outs, (core, odd, *refs), "finish_attn", 12, smem=2)


def attn_bwd(order, seqs, qk, vo, low=False):
    width = qk.shape[0] - 16
    half = width // 2
    rows = seqs[0][1].shape[1]
    counts, args, outs, aliases = [], [qk, vo], [], {}
    for index, (g, gt, xt, pt, qkv, ctx, acc) in enumerate(seqs):
        counts += [len(g), 1, 1, 1, 1, 1, acc is not None]
        args += [*g, gt, xt, pt, qkv, ctx]
        down = low and index == 1
        if acc is not None:
            if not down:
                aliases[len(args)] = len(outs)
            args.append(acc)
        outs.append(((rows, width), BF if down else F32))

    def kernel(qk, vo, *refs):
        ins = split_refs(refs[: sum(counts)], counts)
        totals, outs = refs[sum(counts) : sum(counts) + 2], refs[sum(counts) + 2 :]
        row = lax.broadcasted_iota(jnp.int32, (128, rows), 0)
        lane = lax.broadcasted_iota(jnp.int32, (rows, 128), 1)
        first = lax.broadcasted_iota(jnp.int32, (16, 256), 0) == 0
        dqks, dvs_all, ctxs = [], [], []
        for index in (0, 1):
            g, _, _, (pt_ref,), (qkv_ref,), (ctx_ref,), acc = ins[7 * index : 7 * index + 7]
            ctx = ctx_ref[...]
            d_o = dotf(whole(g), vo[0:width, 128:256], 1, 0).astype(BF)
            d_ot = d_o.astype(F32).T
            prod = d_ot * ctx.astype(F32).T * (HEAD_DIM**-0.5)
            d_ot = (d_ot * (HEAD_DIM**-0.5)).astype(BF)
            k_t = qkv_ref[1].astype(F32).T.astype(BF)
            dvs, dks, dqs = [], [], []
            for h in range(2):
                head = slice(h * HEAD_DIM, (h + 1) * HEAD_DIM)
                inner = jnp.sum(prod[head, :], 0, keepdims=True)
                p = pt_ref[h]
                dvs.append(dotf(p, d_o, 1, 0))
                d_h = jnp.where((row // HEAD_DIM) == h, d_ot, jnp.zeros_like(d_ot))
                ds = (p.astype(F32) * (dotf(qkv_ref[2], d_h, 1, 0) - inner)).astype(BF)
                dks.append(dotf(ds, qkv_ref[0], 1, 0))
                dqs.append(dotf(k_t[head, :], ds, 1, 0))
            dv = jnp.where(lane < HEAD_DIM, dvs[0], dvs[1]).astype(BF)
            dk = jnp.where(lane < HEAD_DIM, dks[0], dks[1]).astype(BF)
            dq = jnp.concatenate(dqs, 0).T.astype(BF)
            dqk = jnp.concatenate([dq, dk], 1)
            total = dotf(dqk, qk[0:width, :], 1, 1) + dotf(dv, vo[0:width, 0:128], 1, 1)
            if acc:
                total = total + acc[0][...]
            totals[index][...] = total.astype(totals[index].dtype)
            dqks.append(dqk)
            dvs_all.append(dv)
            ctxs.append(ctx)

        def both(place, rights, piece):
            return sum(dotf(ins[7 * i + place][0][piece, :], rights[i], 1, 0) for i in (0, 1))

        def column_sums(values):
            return sum(jnp.sum(v.astype(F32), 0, keepdims=True) for v in values)

        sums = [column_sums(dqks), jnp.concatenate([column_sums(dvs_all), jnp.zeros((1, 128), F32)], 1)]
        for index in (0, 1):
            out = outs[index : index + 1]
            for part in (0, 1):
                piece = slice(part * half, (part + 1) * half)
                if index == 0:
                    value = both(2, dqks, piece)
                else:
                    value = jnp.concatenate([both(2, dvs_all, piece), both(1, ctxs, piece)], 1)
                put(out, part, half, 16, value)
            put(out, 2, half, 16, jnp.where(first, sums[index], 0.0))
            put(out, 3, half, 16, jnp.zeros((16, 256), F32))

    outs += [*gradient_shapes(width, 256, 16, False) * 2]
    return order(kernel, tuple(outs), tuple(args), "attn_bwd", 8, aliases)


def ffn_fwd(order, seqs, up, dn, low=False):
    width = dn.shape[1]
    counts, args, outs, aliases = [], [up, dn], [], {}
    rows = sum(m.shape[0] for m in seqs[0][0])
    mid = ((rows, dn.shape[0]), BF)
    for n, acc in seqs:
        counts += [len(n), acc is not None]
        args += n
        if acc is not None:
            if not low:
                aliases[len(args)] = len(outs)
            args.append(acc)
        outs += [*((((rows // 2, width), BF),) * 2 if low else (((rows, width), F32),)), mid, mid]

    def kernel(up, dn, *refs):
        ins = split_refs(refs[: sum(counts)], counts)
        results = refs[sum(counts) :]
        for index in range(len(seqs)):
            n_refs, acc = ins[2 * index : 2 * index + 2]
            total_refs, results = results[: 1 + low], results[1 + low :]
            (act_ref, slope_ref), results = results[:2], results[2:]
            for i in (0, 1):
                part = slice(i * (rows // 2), (i + 1) * (rows // 2))
                u = dotf(take(n_refs, part), up[0:width, :], 1, 0) + up[width : width + 16, :][0:1, :].astype(F32)
                cdf = 0.5 + 0.5 * lax.erf(u * root_half)
                act = (u * cdf).astype(BF)
                act_ref[part, :] = act
                slope = cdf + u * (jnp.exp2(u * u * (-0.5 * LOG2E)) * inverse_root_two_pi)
                slope_ref[part, :] = slope.astype(BF)
                total = dotf(act, dn[...], 1, 0)
                if acc:
                    total = total + acc[0][part, :]
                if low:
                    total_refs[i][...] = total.astype(BF)
                else:
                    total_refs[0][part, :] = total

    result = list(order(kernel, tuple(outs), tuple(args), "ffn_fwd", 8, aliases))
    out = []
    for _ in seqs:
        out.append((result[: 1 + low], result[1 + low : 3 + low]))
        result = result[3 + low :]
    return out


def ffn_bwd(order, seqs, up, dn, low=False):
    width = dn.shape[1]
    counts, args, outs, aliases = [], [up, dn], [], {}
    rows = seqs[0][1].shape[0]
    for g, slope, acc in seqs:
        counts += [len(g), 1, acc is not None]
        args += [*g, slope]
        if acc is not None:
            if not low:
                aliases[len(args)] = len(outs)
            args.append(acc)
        outs += [*((((rows // 2, width), BF),) * 2 if low else (((rows, width), F32),)), (slope.shape, BF)]

    def kernel(up, dn, *refs):
        ins = split_refs(refs[: sum(counts)], counts)
        results = refs[sum(counts) :]
        for index in range(len(seqs)):
            g, (slope,), acc = ins[3 * index : 3 * index + 3]
            total_refs, results = results[: 1 + low], results[1 + low :]
            d_ref, *results = results
            d_up = (dotf(whole(g), dn[...], 1, 1) * slope[...].astype(F32)).astype(BF)
            d_ref[...] = d_up
            total = dotf(d_up, up[0:width, :], 1, 1)
            if acc:
                total = total + acc[0][...]
            if low:
                total_refs[0][...] = total[: rows // 2].astype(BF)
                total_refs[1][...] = total[rows // 2 :].astype(BF)
            else:
                total_refs[0][...] = total

    result = list(order(kernel, tuple(outs), tuple(args), "ffn_bwd", 8, aliases))
    out = []
    for _ in seqs:
        out.append((result[: 1 + low], result[1 + low]))
        result = result[2 + low :]
    return out


def standard(v):
    centered = v - jnp.mean(v, -1, keepdims=True)
    inv = lax.rsqrt(jnp.mean(centered * centered, -1, keepdims=True) + norm_epsilon)
    return centered * inv, inv


def back_through(g, scaled, inv, gain):
    e = g * gain
    return inv * (e - jnp.mean(e, -1, keepdims=True) - scaled * jnp.mean(e * scaled, -1, keepdims=True))


def half_of(refs, i):
    per = refs[0].shape[0] // 128
    return refs[i // per][(i % per) * 128 : (i % per + 1) * 128, :]


def first_norm(order, x, acc, got, b_out, gain, bias, b_down):
    rows, width = x.shape

    def kernel(x_ref, acc_ref, got_ref, b_out, gain, bias, b_down, sum_ref, out_ref, low_a, low_b, low_t):
        for i in range(rows // 128):
            part = slice(i * 128, (i + 1) * 128)
            total = x_ref[part, :].astype(F32) + b_out[...].astype(F32)
            total = total + acc_ref[part, :] + got_ref[part, :].astype(F32)
            sum_ref[part, :] = total
            scaled, _ = standard(total)
            normed = scaled * gain[...] + bias[...]
            out_ref[part, :] = normed + b_down[...].astype(F32)
            low = normed.astype(BF)
            place = (i * 128) % (rows // 2)
            (low_a, low_b)[i * 256 // rows][place : place + 128, :] = low
            low_t[:, part] = low.astype(F32).T.astype(BF)

    half = ((rows // 2, width), BF)
    outs = (((rows, width), F32), ((rows, width), F32), half, half, ((width, rows), BF))
    args = (x, acc, got, b_out[None], gain[None], bias[None], b_down[None])
    return order(kernel, outs, args, "first_norm", 14, {1: 0})


def emit_back(i, carry, g, scaled, inv, gain, out_ref, low_halves, low_t):
    part = slice(i * 128, (i + 1) * 128)
    d_rows = back_through(g, scaled, inv, gain)
    out_ref[part, :] = d_rows
    low = d_rows.astype(BF)
    half = low_halves[0].shape[0]
    place = (i * 128) % half
    low_halves[i * 128 // half][place : place + 128, :] = low
    low = low.astype(F32)
    low_t[:, part] = low.T.astype(BF)
    terms = (g * scaled, g, low)
    return tuple(c + jnp.sum(t, 0, keepdims=True) for c, t in zip(carry, terms))


def put_sums(sums_ref, carry):
    row = lax.broadcasted_iota(jnp.int32, sums_ref.shape, 0)
    sums_ref[...] = jnp.where(row == 0, carry[0], jnp.where(row == 1, carry[1], jnp.where(row == 2, carry[2], 0.0)))


def back_outs(rows, width):
    half = ((rows // 2, width), BF)
    return (((rows, width), F32), half, half, ((width, rows), BF), ((8, width), F32))


def second_norm(order, total, got, cotangent, gain, bias):
    rows, width = total.shape

    def kernel(sum_ref, got_a, got_b, cot_ref, gain, bias, d_ref, low_a, low_b, low_t, sums_ref, y_ref):
        carry = (jnp.zeros((1, width), F32),) * 3
        for i in range(rows // 128):
            part = slice(i * 128, (i + 1) * 128)
            scaled, inv = standard(sum_ref[part, :] + half_of((got_a, got_b), i).astype(F32))
            y_ref[part, :] = (scaled * gain[...] + bias[...]).astype(BF)
            g = cot_ref[part, :].astype(F32)
            carry = emit_back(i, carry, g, scaled, inv, gain[...], d_ref, (low_a, low_b), low_t)
        put_sums(sums_ref, carry)

    outs = (*back_outs(rows, width), ((rows, width), BF))
    return order(kernel, outs, (total, *got, cotangent, gain[None], bias[None]), "second_norm", 14, {0: 0})


def first_back(order, first, gain, d_normed, got):
    rows, width = first.shape

    def kernel(sum_ref, gain, d_ref, got_a, got_b, out_ref, low_a, low_b, low_t, sums_ref):
        carry = (jnp.zeros((1, width), F32),) * 3
        for i in range(rows // 128):
            part = slice(i * 128, (i + 1) * 128)
            scaled, inv = standard(sum_ref[part, :])
            g = d_ref[part, :] + half_of((got_a, got_b), i).astype(F32)
            carry = emit_back(i, carry, g, scaled, inv, gain[...], out_ref, (low_a, low_b), low_t)
        put_sums(sums_ref, carry)

    return order(kernel, back_outs(rows, width), (first, gain[None], d_normed, *got), "first_back", 14, {2: 0})

CORE = [(d, d ^ 1) for d in range(8)]
ROW = [(t, t ^ 1) for t in range(4)]
COL = [(t, t ^ 2) for t in range(4)]
NEAR = [(d, d ^ 2) for d in range(8)]
FAR = [(d, d ^ 4) for d in range(8)]


def swap_core(v):
    return lax.ppermute(v, "dp", CORE)


def swap_row(v):
    return lax.ppermute(v, "tensor", ROW)


def swap_col(v):
    return lax.ppermute(v, "tensor", COL)


def swap_near(v):
    return lax.ppermute(v, "dp", NEAR)


def swap_far(v):
    return lax.ppermute(v, "dp", FAR)


class Piece:
    def __init__(self, order, odd):
        self.order, self.odd = order, odd
        self.mine = [None] * 4

    def diagonal(self, top, bottom):
        self.top, self.bottom = swap_row(top), swap_col(bottom)

    def direct(self, row_part, col_part):
        self.row_part, self.col_part = swap_row(row_part), swap_col(col_part)

    def along_z(self, keep, send):
        self.keep, self.got = keep, swap_near(send)

    def second(self):
        self.keep = self.order.add(self.got, self.keep)
        self.got = swap_far(self.keep)

    def third(self):
        self.keep = self.order.add(self.got, self.keep)

    def fourth(self):
        self.got = swap_near(self.order.now(self.keep))

    def kept(self):
        self.keep_o = swap_core(self.order.now(self.keep))

    def last(self):
        self.got_o = swap_core(self.order.now(self.got))

    def all(self):
        return self.keep, self.keep_o, self.got, self.got_o


def fast(
    layer_input,
    segment_ids,
    w_qkv,
    b_qv,
    w_out,
    b_out,
    ln1_gain,
    ln1_bias,
    w_up,
    b_up,
    w_down,
    b_down,
    ln2_gain,
    ln2_bias,
    cotangent,
):
    rows, width = layer_input.shape
    hidden = w_up.shape[1] // 2
    core = lax.axis_index("dp") % 2
    odd_index = (lax.axis_index("dp") // 2) % 2
    odd = odd_index.astype(jnp.int32)[None]
    core = core.astype(jnp.int32)[None]
    order = Order()
    now, wait = order.now, order.wait

    segment = lax.dynamic_index_in_dim(segment_ids, lax.axis_index("tensor"), keepdims=False)
    inputs = ((layer_input,), (swap_core(layer_input),))
    qk, vo, up_w, dn_w = [None] * 4, [None] * 4, [None] * 4, [None] * 4
    qk[0], vo[0] = pack_attn(order, core, w_qkv, w_out, b_qv)
    qk[1], qk[2] = swap_row(qk[0]), swap_col(qk[0])
    vo[1], vo[2] = swap_row(vo[0]), swap_col(vo[0])
    up_w[0], dn_w[0] = pack_ffn(order, core, w_up, b_up[None], w_down)

    masks = [
        jnp.where(ids[:, None] == ids[None, :], 0.0, -1e30).astype(F32) for ids in (segment, swap_core(segment))
    ]
    total = [None, None]
    saved = [[None, None] for _ in range(4)]

    def attend(r, which, low=False):
        found = attn_fwd(order, [(inputs[s], masks[s], total[s], low) for s in which], qk[r], vo[r])
        for s, (total[s], saved[r][s]) in zip(which, found):
            continue

    attend(0, (0, 1))
    qk[3], vo[3] = swap_row(now(qk[2])), swap_col(now(vo[1]))
    attend(1, (0, 1))
    up_w[1], up_w[2] = swap_row(now(up_w[0])), swap_col(now(up_w[0]))
    attend(2, (0, 1))
    attend(3, (1,), True)
    got = swap_core(total[1])
    attend(3, (0,))
    dn_w[1], dn_w[2] = swap_row(now(dn_w[0])), swap_col(now(dn_w[0]))
    wait(up_w[1], up_w[2])
    first, branch, *low, normed_t = first_norm(
        order, layer_input, total[0], got, b_out, ln1_gain, ln1_bias, b_down
    )
    normed = (tuple(low), tuple(swap_core(v) for v in low))
    total = [branch, None]
    acts = [[None, None] for _ in range(4)]
    slopes = [[None, None] for _ in range(4)]

    def expand(r, which, low=False):
        found = ffn_fwd(order, [(normed[s], total[s]) for s in which], up_w[r], dn_w[r], low)
        for s, (total[s], (acts[r][s], slopes[r][s])) in zip(which, found):
            total[s] = total[s] if low else total[s][0]

    expand(0, (0,))
    expand(0, (1,))
    wait(dn_w[1], dn_w[2])
    normed_t = (normed_t, flip(order, normed[1]))
    up_w[3], dn_w[3] = swap_row(now(up_w[2])), swap_col(now(dn_w[1]))
    expand(1, (0, 1))
    expand(2, (0, 1))
    expand(3, (1,), True)
    got = [swap_core(v) for v in total[1]]
    expand(3, (0,))
    d_second, *low, branch_t, sums_two, output = second_norm(order, total[0], got, cotangent, ln2_gain, ln2_bias)
    branch_low = (tuple(low), tuple(swap_core(v) for v in low))

    down, up = Piece(order, odd), Piece(order, odd)
    attn, attn_qk, attn_vo = Piece(order, odd), Piece(order, odd), Piece(order, odd)
    total = [d_second, None]
    d_up = [[None, None] for _ in range(4)]

    def back(r, which, low=False):
        found = ffn_bwd(order, [(branch_low[s], slopes[r][s], total[s]) for s in which], up_w[r], dn_w[r], low)
        for s, (total[s], d_up[r][s]) in zip(which, found):
            total[s] = total[s] if low else total[s][0]

    def grad_down(r, got=(), split=False, z=None):
        return outer(order, branch_t, acts[r], got, split, "grad_down", False, z)

    def grad_up(r, got=(), split=False, z=None):
        return outer(order, normed_t, d_up[r], got, split, "grad_up", True, z)

    back(3, (0,))
    branch_t = (branch_t, flip(order, branch_low[1]))
    down.diagonal(*grad_down(3, split=True))
    back(3, (1,))
    up.diagonal(*grad_up(3, split=True))
    back(1, (0, 1))
    back(2, (0, 1))
    down_row, down_col = grad_down(1)[0], grad_down(2)[0]
    down.direct(*pass_on(order, down_row, down.bottom, down_col, down.top))
    back(0, (1,), True)
    got = [swap_core(v) for v in total[1]]
    back(0, (0,))
    d_first, *low, attention_t, sums_one = first_back(order, first, ln1_gain, total[0], got)
    attention_low = (tuple(low), tuple(swap_core(v) for v in low))
    inputs_t = [flip(order, inputs[s]) for s in (0, 1)]
    attention_t = (attention_t, flip(order, attention_low[1]))
    total = [d_first, None]

    def attend_back(r, low=False):
        seqs = [
            (attention_low[s], attention_t[s], inputs_t[s], *saved[r][s], total[s]) for s in (0, 1)
        ]
        total[0], total[1], attn_qk.mine[r], attn_vo.mine[r] = attn_bwd(order, seqs, qk[r], vo[r], low)

    up_row, up_col = grad_up(1, split=True), grad_up(2, split=True)
    down_own = grad_down(0)[0]
    down.along_z(*sum_halves(order, odd, down_own, down.row_part, down.col_part))
    low_row, high_col = add_pair(order, up_row[1], up.bottom, up_col[0], up.top)
    up_rows, up_cols = [swap_row(v) for v in (up_row[0], low_row)], [swap_col(v) for v in (high_col, up_col[1])]
    down.second()
    attend_back(3)
    qk_diag, vo_diag = swap_row(attn_qk.mine[3]), swap_col(attn_vo.mine[3])
    attend_back(1)
    arrived = [(kind, v) for part in (up_rows, up_cols) for kind, v in zip(("top", "bottom"), part)]
    up.along_z(*grad_up(0, arrived, True, odd))
    attend_back(2)
    down.third()
    up.second()
    row, col = relay(order, attn_qk.mine[1], attn_vo.mine[1], vo_diag, attn_qk.mine[2], attn_vo.mine[2], qk_diag)
    row, col = swap_row(row), swap_col(col)
    down.fourth()
    attend_back(0, True)
    wait(down.got)
    attn.along_z(*own_sum(order, odd, attn_qk.mine[0], attn_vo.mine[0], row, col))
    up.third()
    small = jnp.concatenate([sums_one, sums_two], 0)
    small = order.add(swap_core(now(small)), small)
    small = order.add(swap_row(small), small)
    small_col = swap_col(small)
    attn.second()
    small = order.add(small_col, small)
    small_near = swap_near(small)
    up.fourth()
    down.kept()
    down.last()
    got = swap_core(now(total[1]))
    grad_w_down = finish_down(order, core, odd, down.all())
    grad_input = order.add(got, total[0])
    small = order.add(small_near, small)
    wait(up.got)
    attn.third()
    attn.fourth()
    small_far = swap_far(now(small))
    attn.kept()
    up.kept()
    up.last()
    grad_b_up, grad_w_up = finish_up(order, core, odd, up.all())
    small = order.add(small_far, small)
    attn.last()
    grad_w_qkv, grad_b_qv, grad_w_out = finish_attn(order, core, odd, attn.all())
    return (
        output,
        grad_input,
        grad_w_qkv,
        grad_b_qv,
        grad_w_out,
        small[2],
        small[0],
        small[1],
        grad_w_up,
        grad_b_up[0],
        grad_w_down,
        small[10],
        small[8],
        small[9],
    )


def local(*arrays):
    my_rows = arrays[0].shape[0]
    seq_len = arrays[1].shape[1]
    grid = (lax.axis_size("dp"), lax.axis_size("tensor"))
    if grid == (8, 4) and my_rows == seq_len and arrays[4].shape[0] == 4 * HEAD_DIM:
        return fast(*arrays)
    return general(*arrays)


def solution(mesh):
    return jax.shard_map(
        local,
        mesh=mesh,
        in_specs=(
            P(("dp", "tensor"), None),
            P("dp", None),
            P(None, None, "tensor"),
            P(None, "tensor"),
            P("tensor", None),
            P(),
            P(),
            P(),
            P(None, "tensor"),
            P("tensor"),
            P("tensor", None),
            P(),
            P(),
            P(),
            P(("dp", "tensor"), None),
        ),
        out_specs=(
            P(("dp", "tensor"), None),
            P(("dp", "tensor"), None),
            P(None, None, "tensor"),
            P(None, "tensor"),
            P("tensor", None),
            P(),
            P(),
            P(),
            P(None, "tensor"),
            P("tensor"),
            P("tensor", None),
            P(),
            P(),
            P(),
        ),
        check_vma=False,
    )
```
